32 devices in a mesh: expert: 8 (over z, y), tensor: 4 (over x, core).
Axes of the slice: x: 2, y: 2, z: 4, core: 2. Of those that a mesh axis runs over, the one named last changes fastest.
Arguments:
- inputs: bfloat16 [4096, 2048], P('expert'), may hold values from -6 to 6
- cotangent: bfloat16 [4096, 2048], P('expert'), may hold values from -6 to 6
- positions: int32 [4096], P('expert'), may hold values from 0 to 255, as said below
- routes: int32 [4096, 6], P('expert'), may hold values from 0 to 15, as said below
- slot_index: int32 [4096, 6], P('expert'), may hold values from 0 to 256, as said below
- attention_gain: float32 [2048], replicated, may hold values from 0.5 to 1.5
- feedforward_gain: float32 [2048], replicated, may hold values from 0.5 to 1.5
- latent_gain: float32 [512], replicated, may hold values from 0.5 to 1.5
- query_weight: bfloat16 [2048, 3072], P(None, 'tensor'), may hold values from -0.125 to 0.125
- latent_down: bfloat16 [2048, 576], replicated, may hold values from -0.125 to 0.125
- latent_up: bfloat16 [512, 4096], P(None, 'tensor'), may hold values from -0.25 to 0.25
- out_weight: bfloat16 [2048, 2048], P('tensor'), may hold values from -1 to 1
- router_weight: bfloat16 [2048, 16], replicated, may hold values from -0.0625 to 0.0625
- shared_gate: bfloat16 [2048, 2816], P(None, 'tensor'), may hold values from -0.125 to 0.125
- shared_up: bfloat16 [2048, 2816], P(None, 'tensor'), may hold values from -0.125 to 0.125
- shared_down: bfloat16 [2816, 2048], P('tensor'), may hold values from -0.21875 to 0.21875
- expert_gate: bfloat16 [16, 2048, 1408], P('expert', None, 'tensor'), may hold values from -0.125 to 0.125
- expert_up: bfloat16 [16, 2048, 1408], P('expert', None, 'tensor'), may hold values from -0.125 to 0.125
- expert_down: bfloat16 [16, 1408, 2048], P('expert', 'tensor'), may hold values from -0.4375 to 0.4375
Outputs:
- layer_output: bfloat16 [4096, 2048], P('expert')
- grad_input: float32 [4096, 2048], P('expert')
- grad_attention_gain: float32 [2048], P('expert')
- grad_feedforward_gain: float32 [2048], P('expert')
- grad_latent_gain: float32 [512], P('expert')
- grad_query: float32 [2048, 3072], P('expert', 'tensor')
- grad_latent_down: float32 [2048, 576], P('expert')
- grad_latent_up: float32 [512, 4096], P('expert', 'tensor')
- grad_out_weight: float32 [2048, 2048], P('tensor', 'expert')
- grad_router: float32 [2048, 16], P('expert')
- grad_shared_gate: float32 [2048, 2816], P('expert', 'tensor')
- grad_shared_up: float32 [2048, 2816], P('expert', 'tensor')
- grad_shared_down: float32 [2816, 2048], P('tensor', 'expert')
- grad_expert_gate: float32 [16, 2048, 1408], P('expert', None, 'tensor')
- grad_expert_up: float32 [16, 2048, 1408], P('expert', None, 'tensor')
- grad_expert_down: float32 [16, 1408, 2048], P('expert', 'tensor')
The draws below stay inside these ranges and needn't reach their ends.
Inputs may be any that keep to these rules, and one draw needn't show every extreme that they name: `positions`: each sequence of 512 consecutive rows holds three documents end to end, one of exactly 256 rows; a row's value is its place in its document, counted from 0. `routes`: each row names 6 different experts. `slot_index`: within a sequence, the pairs (row, choice) that name one expert are numbered 0, 1, 2, ... in order of row and then of choice; the value is that number, or 256 where it is 256 or more (the pair is dropped). One expert, the same in every sequence, is named by the first 257 rows of every sequence.
All inputs are finite; a program needn't handle non-finite values.
Results may differ from the reference program's by a relative error of at most 0.023.
Values may be sent and summed in bfloat16 or wider, within the bound.
A program may use at most 320 MiB of HBM per device.

```python
import math
import jax
import jax.numpy as jnp
from jax import lax

D = 2048
H = 16
NOPE = 128
ROPE = 64
VD = 128
KVR = 512
FE = 1408
FS = 2816
TOP = 6
GROUP_TOK = 512
TOKENS = 4096
SPECIALIST_TOTAL = 16
SPECIALIST_CAP = 256
N_TENSOR = 4


def route_table(key):
    base_key = jax.random.fold_in(key, 17)
    noise_key, favour_key, hot_key = jax.random.split(base_key, 3)
    group_total = TOKENS // GROUP_TOK
    gaussian_jitter_draw = jax.random.randint(noise_key, (TOKENS, SPECIALIST_TOTAL), 0, 1 << 16)
    leaning_offset = jax.random.randint(favour_key, (SPECIALIST_TOTAL,), 0, 1 << 15)
    heaviest_specialist = jax.random.randint(hot_key, (), 0, SPECIALIST_TOTAL)
    hosted_entries = jnp.arange(TOKENS, dtype=jnp.int32) % GROUP_TOK
    field_indices = jnp.arange(SPECIALIST_TOTAL, dtype=jnp.int32)
    favoured_specialist_offset = jnp.where((hosted_entries[:, None] <= SPECIALIST_CAP) & (field_indices[None, :] == heaviest_specialist), 1 << 18, 0)
    dispatcher_logit_values = (gaussian_jitter_draw + leaning_offset[None, :] + favoured_specialist_offset) * SPECIALIST_TOTAL + field_indices[None, :]
    chosen = lax.top_k(dispatcher_logit_values, TOP)[1].astype(jnp.int32)
    onehot = (chosen[:, :, None] == field_indices[None, None, :]).astype(jnp.int32).reshape(group_total, GROUP_TOK * TOP, SPECIALIST_TOTAL)
    before = jnp.cumsum(onehot, axis=1) - onehot
    rank_table = jnp.sum(before * onehot, axis=2).reshape(TOKENS, TOP)
    return (chosen, jnp.minimum(rank_table, SPECIALIST_CAP).astype(jnp.int32))


def draw_routes(key, part):
    return route_table(key)[0]


def draw_slot_index(key, part):
    return route_table(key)[1]


def draw_positions(key, part):
    group_total = TOKENS // GROUP_TOK
    half_rows = GROUP_TOK // 2
    cut_key, order_key = jax.random.split(jax.random.fold_in(key, 29))
    middle = jax.random.randint(cut_key, (group_total,), 1, half_rows)
    lengths = jnp.stack([jnp.full((group_total,), half_rows, jnp.int32), middle, half_rows - middle], axis=1)
    order_scores = jax.random.randint(order_key, (group_total, 3), 0, 1 << 20) * 4 + jnp.arange(3, dtype=jnp.int32)[None, :]
    ordering = jnp.argsort(order_scores, axis=1, stable=True)
    lengths = jnp.take_along_axis(lengths, ordering, axis=1)
    first_end = lengths[:, 0:1]
    second_end = first_end + lengths[:, 1:2]
    hosted_entries = jnp.arange(GROUP_TOK, dtype=jnp.int32)[None, :]
    starts = jnp.where(hosted_entries >= second_end, second_end, jnp.where(hosted_entries >= first_end, first_end, 0))
    return (hosted_entries - starts).reshape(TOKENS).astype(jnp.int32)


def shard_levels(key, shape, cuts, smallest, top_value):
    factor_of, own = 1.0, jax.random.fold_in(key, 6)
    for position, blocks in cuts:
        heights = jnp.exp(jax.random.uniform(jax.random.fold_in(own, position), (blocks,), jnp.float32, smallest / len(cuts), top_value / len(cuts)))
        factor_of = factor_of * jnp.repeat(heights, shape[position] // blocks).reshape([-1 if axis == position else 1 for axis in range(len(shape))])
    return factor_of


def scatter_about(stream_key, shape, scale, bound, pieces=(), kind=jnp.bfloat16):
    values = scale * jax.random.normal(stream_key, shape, jnp.float32)
    if pieces:
        values = values * shard_levels(stream_key, shape, pieces, -0.22, 0.18)
    return jnp.clip(values, -bound, bound).astype(kind)


def setup_inputs(seed: int = 0) -> dict:
    streams_of = jax.random.split(jax.random.key(seed), 20)
    inputs = scatter_about(streams_of[0], (TOKENS, D), 1.0, 6.0, ((0, 8),))
    cotangent = scatter_about(streams_of[1], (TOKENS, D), 1.0, 6.0, ((0, 8),))
    positions = draw_positions(jax.random.fold_in(streams_of[19], 71), 0)
    routes = draw_routes(jax.random.fold_in(streams_of[19], 71), 0)
    slot_index = draw_slot_index(jax.random.fold_in(streams_of[19], 71), 0)
    attention_gain = jnp.clip(1.0 + 0.1 * jax.random.normal(streams_of[5], (D,), jnp.float32), 0.5, 1.5)
    feedforward_gain = jnp.clip(1.0 + 0.1 * jax.random.normal(streams_of[6], (D,), jnp.float32), 0.5, 1.5)
    latent_gain = jnp.clip(1.0 + 0.1 * jax.random.normal(streams_of[7], (KVR,), jnp.float32), 0.5, 1.5)
    query_weight = scatter_about(streams_of[8], (D, H * (NOPE + ROPE)), D ** -0.5, 0.125, ((1, 4),))
    latent_down = scatter_about(streams_of[9], (D, KVR + ROPE), D ** -0.5, 0.125)
    latent_up = scatter_about(streams_of[10], (KVR, H * (NOPE + VD)), KVR ** -0.5, 0.25, ((1, 4),))
    out_weight = scatter_about(streams_of[11], (H * VD, D), (H * VD // 64) ** -0.5, 1.0, ((0, 4),))
    router_weight = scatter_about(streams_of[12], (D, SPECIALIST_TOTAL), (4 * D) ** -0.5, 0.0625)
    shared_gate = scatter_about(streams_of[13], (D, FS), D ** -0.5, 0.125, ((1, 4),))
    shared_up = scatter_about(streams_of[14], (D, FS), D ** -0.5, 0.125, ((1, 4),))
    shared_down = scatter_about(streams_of[15], (FS, D), (FS // 4) ** -0.5, 0.21875, ((0, 4),))
    expert_gate = scatter_about(streams_of[16], (SPECIALIST_TOTAL, D, FE), D ** -0.5, 0.125, ((0, 8), (2, 4)))
    expert_up = scatter_about(streams_of[17], (SPECIALIST_TOTAL, D, FE), D ** -0.5, 0.125, ((0, 8), (2, 4)))
    expert_down = scatter_about(streams_of[18], (SPECIALIST_TOTAL, FE, D), (FE // 8) ** -0.5, 0.4375, ((0, 8), (1, 4)))
    return {"inputs": inputs, "cotangent": cotangent, "positions": positions, "routes": routes, "slot_index": slot_index, "attention_gain": attention_gain, "feedforward_gain": feedforward_gain, "latent_gain": latent_gain, "query_weight": query_weight, "latent_down": latent_down, "latent_up": latent_up, "out_weight": out_weight, "router_weight": router_weight, "shared_gate": shared_gate, "shared_up": shared_up, "shared_down": shared_down, "expert_gate": expert_gate, "expert_up": expert_up, "expert_down": expert_down}


@jax.custom_vjp
def low(v):
    return lax.optimization_barrier(v.astype(jnp.bfloat16)).astype(jnp.float32)

@jax.custom_vjp
def low_back(v):
    return v

def low_keep(v):
    return (low(v), None)

def low_pass(kept, grad):
    return (grad,)

def back_keep(v):
    return (v, None)

def back_low(kept, grad):
    return (low(grad),)
low.defvjp(low_keep, low_pass)
low_back.defvjp(back_keep, back_low)
EPSILON = 1e-06
HIGHEST = lax.Precision.HIGHEST

def product(left_side, right_side):
    return jnp.dot(left_side, right_side, precision=HIGHEST)

def normalize(values, gain_vector):
    return values * lax.rsqrt(lax.optimization_barrier(jnp.mean(values * values, axis=-1, keepdims=True)) + EPSILON) * gain_vector

def rope_tables(positions):
    half_width = ROPE // 2
    frequency = 10000.0 ** (-2.0 * jnp.arange(half_width, dtype=jnp.float32) / ROPE)
    angles = positions.astype(jnp.float32)[:, None] * frequency[None, :]
    return (jnp.cos(angles), jnp.sin(angles))

def rotate(values, cosine, sine_table):
    half_width = values.shape[-1] // 2
    front_half = values[..., :half_width]
    back_half = values[..., half_width:]
    return jnp.concatenate([front_half * cosine - back_half * sine_table, back_half * cosine + front_half * sine_table], axis=-1)

def expert_block(operands):
    expert_rows, gate_matrix, up_matrix, down_matrix = operands
    shard_width = FE // N_TENSOR
    copies = low_back(jnp.broadcast_to(expert_rows[None], (N_TENSOR,) + expert_rows.shape))
    gate_split = gate_matrix.reshape(D, N_TENSOR, shard_width).transpose(1, 0, 2)
    up_split = up_matrix.reshape(D, N_TENSOR, shard_width).transpose(1, 0, 2)
    down_split = down_matrix.reshape(N_TENSOR, shard_width, D)
    gate_pre = low_back(jnp.einsum('tcd,tdf->tcf', copies, gate_split, precision=HIGHEST))
    up_pre = low_back(jnp.einsum('tcd,tdf->tcf', copies, up_split, precision=HIGHEST))
    hidden = low(jax.nn.silu(gate_pre) * up_pre)
    partial_out = low(jnp.einsum('tcf,tfd->tcd', hidden, down_split, precision=HIGHEST))
    return lax.optimization_barrier(jnp.sum(partial_out, axis=0))

def group_layer(rows_in, positions, routes, slot_index, weights):
    attention_gain, feedforward_gain, latent_gain, query_weight, latent_down, latent_up, out_weight, router_weight, shared_gate, shared_up, shared_down, expert_gate, expert_up, expert_down = weights
    length = GROUP_TOK
    cosine, sine_table = rope_tables(positions)
    first_norm = low(normalize(rows_in, attention_gain))
    query_raw = low_back(product(first_norm, query_weight)).reshape(length, H, NOPE + ROPE)
    queries = low(jnp.concatenate([query_raw[..., :NOPE], rotate(query_raw[..., NOPE:], cosine[:, None], sine_table[:, None])], axis=-1))
    latent_raw = low_back(product(first_norm, latent_down))
    latent = low(normalize(latent_raw[:, :KVR], latent_gain))
    key_rope = low(rotate(latent_raw[:, KVR:], cosine, sine_table))
    key_value = low(low_back(product(latent, latent_up))).reshape(length, H, NOPE + VD)
    key_rows = jnp.concatenate([key_value[..., :NOPE], jnp.broadcast_to(key_rope[:, None, :], (length, H, ROPE))], axis=-1)
    values = key_value[..., NOPE:]
    score_scale = 1.0 / math.sqrt(NOPE + ROPE)
    dispatcher_logit_values = low_back(jnp.einsum('qhd,khd->hqk', queries, key_rows, precision=HIGHEST) * score_scale)
    row_ids = jnp.arange(length, dtype=jnp.int32)
    starts = row_ids - positions
    visible = (row_ids[None, :] <= row_ids[:, None]) & (row_ids[None, :] >= starts[:, None])
    probabilities = jax.nn.softmax(jnp.where(visible[None], dispatcher_logit_values, -jnp.inf), axis=-1)
    head_out = low(low_back(jnp.einsum('hqk,khd->qhd', low(probabilities), values, precision=HIGHEST))).reshape(length, H * VD)
    attention = low_back(product(head_out, out_weight))
    residual = rows_in + attention
    second_norm = low(normalize(residual, feedforward_gain))
    logits = low_back(product(second_norm, router_weight))
    gate_weights = jax.nn.softmax(jnp.take_along_axis(logits, routes, axis=1), axis=-1)
    shared_pre = low_back(product(second_norm, shared_gate))
    shared_lin = low_back(product(second_norm, shared_up))
    shared_out = product(low(jax.nn.silu(shared_pre) * shared_lin), shared_down)
    kept_pairs = slot_index < SPECIALIST_CAP
    places = jnp.where(kept_pairs, routes * SPECIALIST_CAP + slot_index, SPECIALIST_TOTAL * SPECIALIST_CAP)
    pair_rows = jnp.broadcast_to(row_ids[:, None], routes.shape)
    sources = jnp.full((SPECIALIST_TOTAL * SPECIALIST_CAP,), length, jnp.int32).at[places.reshape(-1)].set(pair_rows.reshape(-1), mode='drop')
    expert_in = jnp.take(second_norm, sources, axis=0, mode='fill', fill_value=0.0).reshape(SPECIALIST_TOTAL, SPECIALIST_CAP, D)
    expert_out = lax.map(jax.checkpoint(expert_block), (expert_in, expert_gate, expert_up, expert_down)).reshape(SPECIALIST_TOTAL * SPECIALIST_CAP, D)
    pair_out = low_back(jnp.take(expert_out, places, axis=0, mode='fill', fill_value=0.0))
    routed = jnp.einsum('tk,tkd->td', gate_weights, pair_out, precision=HIGHEST)
    feedforward = low_back(shared_out + routed)
    return residual + feedforward

def reference(inputs, cotangent, positions, routes, slot_index, attention_gain, feedforward_gain, latent_gain, query_weight, latent_down, latent_up, out_weight, router_weight, shared_gate, shared_up, shared_down, expert_gate, expert_up, expert_down):
    group_total = TOKENS // GROUP_TOK
    weights = (attention_gain.astype(jnp.float32), feedforward_gain.astype(jnp.float32), latent_gain.astype(jnp.float32), query_weight.astype(jnp.float32), latent_down.astype(jnp.float32), latent_up.astype(jnp.float32), out_weight.astype(jnp.float32), router_weight.astype(jnp.float32), shared_gate.astype(jnp.float32), shared_up.astype(jnp.float32), shared_down.astype(jnp.float32), expert_gate.astype(jnp.float32), expert_up.astype(jnp.float32), expert_down.astype(jnp.float32))

    def whole_layer(rows_all, layer_weights):

        def one_group(operands):
            return group_layer(operands[0], operands[1], operands[2], operands[3], layer_weights)
        grouped = (rows_all.reshape(group_total, GROUP_TOK, D), positions.reshape(group_total, GROUP_TOK), routes.reshape(group_total, GROUP_TOK, TOP), slot_index.reshape(group_total, GROUP_TOK, TOP))
        return lax.map(jax.checkpoint(one_group), grouped).reshape(TOKENS, D)
    layer_out, pullback = jax.vjp(whole_layer, inputs.astype(jnp.float32), weights)
    grad_input, grad_weights = pullback(cotangent.astype(jnp.float32))
    return (layer_out.astype(jnp.bfloat16), grad_input, grad_weights[0], grad_weights[1], grad_weights[2], grad_weights[3], grad_weights[4], grad_weights[5], grad_weights[6], grad_weights[7], grad_weights[8], grad_weights[9], grad_weights[10], grad_weights[11], grad_weights[12], grad_weights[13])
```

```python
import math

import jax
import jax.numpy as jnp
from jax import lax
from jax.sharding import PartitionSpec as P

NOPE = 128
ROPE = 64
VD = 128
KVR = 512
TOP = 6


EPSILON = 1e-06


def plain_dot(left_side, right_side):
    return jnp.dot(left_side, right_side, preferred_element_type=jnp.float32)


def lead_dot(left_side, right_side):
    return lax.dot_general(
        left_side, right_side, (((0,), (0,)), ((), ())), preferred_element_type=jnp.float32
    )


def tail_dot(left_side, right_side):
    return lax.dot_general(
        left_side, right_side, (((1,), (1,)), ((), ())), preferred_element_type=jnp.float32
    )


def normalize(values, gain_vector):
    factor = lax.rsqrt(jnp.mean(values * values, axis=-1, keepdims=True) + EPSILON)
    unit_rows = values * factor
    return (unit_rows * gain_vector, unit_rows, factor)


def norm_back(upstream, unit_rows, factor, gain_vector):
    scaled = upstream * gain_vector
    inner_mean = jnp.mean(scaled * unit_rows, axis=-1, keepdims=True)
    return (factor * (scaled - unit_rows * inner_mean), jnp.sum(upstream * unit_rows, axis=0))


def rope_tables(positions):
    half_width = ROPE // 2
    frequency = 10000.0 ** (-2.0 * jnp.arange(half_width, dtype=jnp.float32) / ROPE)
    angles = positions.astype(jnp.float32)[:, None] * frequency[None, :]
    return (jnp.cos(angles), jnp.sin(angles))


def rotate(values, cosine, sine_table):
    half_width = values.shape[-1] // 2
    front_half = values[..., :half_width]
    back_half = values[..., half_width:]
    return jnp.concatenate(
        [
            front_half * cosine - back_half * sine_table,
            back_half * cosine + front_half * sine_table,
        ],
        axis=-1,
    )


def rotate_back(values, cosine, sine_table):
    half_width = values.shape[-1] // 2
    front_half = values[..., :half_width]
    back_half = values[..., half_width:]
    return jnp.concatenate(
        [
            front_half * cosine + back_half * sine_table,
            back_half * cosine - front_half * sine_table,
        ],
        axis=-1,
    )


BOTH = ("expert", "tensor")


def visible_mask(positions, length):
    rows = jnp.arange(length, dtype=jnp.int32)
    starts = rows - positions
    return (rows[None, :] <= rows[:, None]) & (rows[None, :] >= starts[:, None])


def gather_rows(rows):
    return lax.all_gather(rows, BOTH, axis=0, tiled=True)


def scatter_rows(rows):
    return lax.psum_scatter(rows, BOTH, scatter_dimension=0, tiled=True)


def expert_table(routes, values, expert_total):
    ids = jnp.arange(expert_total, dtype=jnp.int32)
    table = jnp.zeros((routes.shape[0], expert_total), jnp.float32)
    for member in range(TOP):
        table = table + jnp.where(
            routes[:, member : member + 1] == ids[None, :], values[:, member : member + 1], 0.0
        )
    return table


def on_device(
    inputs,
    cotangent,
    positions,
    routes,
    slot_index,
    attention_gain,
    feedforward_gain,
    latent_gain,
    query_weight,
    latent_down,
    latent_up,
    out_weight,
    router_weight,
    shared_gate,
    shared_up,
    shared_down,
    expert_gate,
    expert_up,
    expert_down,
):
    length, model_width = inputs.shape
    tensor_count = lax.axis_size("tensor")
    group_count = lax.axis_size("expert")
    tensor_index = lax.axis_index("tensor")
    group_index = lax.axis_index("expert")
    head_width = NOPE + ROPE
    local_heads = query_weight.shape[1] // head_width
    local_experts, _, expert_hidden_width = expert_gate.shape
    shared_width = shared_gate.shape[1]
    experts_all = local_experts * group_count
    capacity = max(
        tensor_count, length * TOP * 4 // (3 * experts_all) // tensor_count * tensor_count
    )
    score_scale = 1.0 / math.sqrt(head_width)
    part_rows = length // tensor_count
    part_start = tensor_index * part_rows
    shard_columns = model_width // group_count

    def own_part(rows):
        return lax.dynamic_slice_in_dim(rows, part_start, part_rows, 0)

    def own_sequence(rows):
        return lax.dynamic_slice_in_dim(rows, group_index * length, length, 0)

    def own_columns(rows):
        return lax.dynamic_slice_in_dim(rows, group_index * shard_columns, shard_columns, 1)

    cotangent_all = gather_rows(own_part(cotangent))
    marked = jnp.where(slot_index < capacity, routes, routes + experts_all)
    marked_all = lax.all_gather(marked, "expert", axis=0, tiled=True)

    rows_in = inputs.astype(jnp.float32)
    normed_one, unit_one, factor_one = normalize(rows_in, attention_gain)
    first_norm = normed_one.astype(jnp.bfloat16)
    cosine, sine_table = rope_tables(positions)
    query_raw = plain_dot(first_norm, query_weight).reshape(length, local_heads, head_width)
    queries = jnp.concatenate(
        [
            query_raw[..., :NOPE],
            rotate(query_raw[..., NOPE:], cosine[:, None], sine_table[:, None]),
        ],
        axis=-1,
    ).astype(jnp.bfloat16)
    latent_raw = plain_dot(first_norm, latent_down)
    latent_normed, unit_latent, factor_latent = normalize(latent_raw[:, :KVR], latent_gain)
    latent = latent_normed.astype(jnp.bfloat16)
    key_rope = rotate(latent_raw[:, KVR:], cosine, sine_table).astype(jnp.bfloat16)
    key_value = (
        plain_dot(latent, latent_up).astype(jnp.bfloat16).reshape(length, local_heads, NOPE + VD)
    )
    key_rows = jnp.concatenate(
        [
            key_value[..., :NOPE],
            jnp.broadcast_to(key_rope[:, None, :], (length, local_heads, ROPE)),
        ],
        axis=-1,
    )
    values = key_value[..., NOPE:]
    visible = visible_mask(positions, length)
    scores = jnp.where(
        visible[None],
        jnp.einsum("qhd,khd->hqk", queries, key_rows, preferred_element_type=jnp.float32)
        * score_scale,
        -jnp.inf,
    )
    weights = jax.nn.softmax(scores, axis=-1)
    weights_low = weights.astype(jnp.bfloat16)
    head_out = (
        jnp.einsum("hqk,khd->qhd", weights_low, values, preferred_element_type=jnp.float32)
        .astype(jnp.bfloat16)
        .reshape(length, local_heads * VD)
    )
    attention = lax.psum_scatter(
        plain_dot(head_out, out_weight).astype(jnp.bfloat16),
        "tensor",
        scatter_dimension=0,
        tiled=True,
    ).astype(jnp.float32)
    residual = own_part(rows_in) + attention
    normed_two, unit_two, factor_two = normalize(residual, feedforward_gain)
    second_part = normed_two.astype(jnp.bfloat16)
    second_all = gather_rows(second_part)

    logits_all = plain_dot(second_all, router_weight)
    ones = jnp.ones(marked_all.shape, jnp.float32)
    kept_all = expert_table(marked_all, ones, experts_all)
    named_all = kept_all + expert_table(marked_all - experts_all, ones, experts_all)
    highest = jnp.max(jnp.where(named_all > 0, logits_all, -jnp.inf), axis=1, keepdims=True)
    raised = jnp.where(named_all > 0, jnp.exp(logits_all - highest), 0.0)
    gates_all = raised / jnp.sum(raised, axis=1, keepdims=True)
    kept_gates = gates_all * kept_all
    local_gates = lax.dynamic_slice_in_dim(
        kept_gates, group_index * local_experts, local_experts, 1
    )
    local_kept = lax.dynamic_slice_in_dim(kept_all, group_index * local_experts, local_experts, 1)

    shared_pre = plain_dot(second_all, shared_gate)
    shared_lin = plain_dot(second_all, shared_up)
    shared_sigmoid = jax.nn.sigmoid(shared_pre)
    shared_hidden = (shared_pre * shared_sigmoid * shared_lin).astype(jnp.bfloat16)
    shared_dhidden = tail_dot(cotangent_all, shared_down)
    shared_dpre = (
        shared_dhidden * shared_lin * shared_sigmoid * (1.0 + shared_pre * (1.0 - shared_sigmoid))
    ).astype(jnp.bfloat16)
    shared_dlin = (shared_dhidden * shared_pre * shared_sigmoid).astype(jnp.bfloat16)
    second_columns = own_columns(second_all)
    grad_shared_gate = lead_dot(second_columns, shared_dpre)
    grad_shared_up = lead_dot(second_columns, shared_dlin)
    grad_shared_down = lead_dot(shared_hidden, own_columns(cotangent_all))

    hidden_list = []
    gate_grad_list = []
    grad_gate_list = []
    grad_up_list = []
    grad_down_list = []
    input_grad_list = []
    weight_list = []
    down_rows = expert_down.reshape(local_experts * expert_hidden_width, model_width)
    raw_dhidden = tail_dot(cotangent_all, down_rows)
    for member in range(local_experts):
        gate = local_gates[:, member : member + 1]
        gate_pre = plain_dot(second_all, expert_gate[member])
        up_pre = plain_dot(second_all, expert_up[member])
        sigmoid = jax.nn.sigmoid(gate_pre)
        active = gate_pre * sigmoid
        hidden = active * up_pre
        hidden_low = (gate * hidden).astype(jnp.bfloat16)
        hidden_list.append(hidden_low)
        dhidden = raw_dhidden[
            :, member * expert_hidden_width : (member + 1) * expert_hidden_width
        ]
        gate_grad_list.append(
            local_kept[:, member] * jnp.sum(hidden * dhidden, axis=1)
        )
        dhidden = gate * dhidden
        dpre = (dhidden * up_pre * sigmoid * (1.0 + gate_pre * (1.0 - sigmoid))).astype(
            jnp.bfloat16
        )
        dlin = (dhidden * active).astype(jnp.bfloat16)
        grad_gate_list.append(lead_dot(second_all, dpre))
        grad_up_list.append(lead_dot(second_all, dlin))
        grad_down_list.append(lead_dot(hidden_low, cotangent_all))
        input_grad_list += [dpre, dlin]
        weight_list += [expert_gate[member], expert_up[member]]

    branch = plain_dot(jnp.concatenate(hidden_list, axis=1), down_rows).astype(jnp.bfloat16)
    own_branch = own_sequence(branch) + plain_dot(
        own_sequence(shared_hidden), shared_down
    ).astype(jnp.bfloat16)
    branch = lax.dynamic_update_slice_in_dim(branch, own_branch, group_index * length, 0)
    feedforward = scatter_rows(branch).astype(jnp.float32)
    result_part = (residual + feedforward).astype(jnp.bfloat16)
    result = lax.all_gather(result_part, "tensor", axis=0, tiled=True)

    second_grad = tail_dot(
        jnp.concatenate(input_grad_list, axis=1), jnp.concatenate(weight_list, axis=1)
    ).astype(jnp.bfloat16)
    own_grad = own_sequence(second_grad) + tail_dot(
        jnp.concatenate([own_sequence(shared_dpre), own_sequence(shared_dlin)], axis=1),
        jnp.concatenate([shared_gate, shared_up], axis=1),
    ).astype(jnp.bfloat16)
    second_grad = lax.dynamic_update_slice_in_dim(second_grad, own_grad, group_index * length, 0)
    grad_second = scatter_rows(second_grad).astype(jnp.float32)

    gate_grad_local = jnp.stack(gate_grad_list, axis=1)
    gate_grad = scatter_rows(
        lax.dynamic_update_slice_in_dim(
            jnp.zeros((group_count * length, experts_all), jnp.float32),
            gate_grad_local,
            group_index * local_experts,
            1,
        )
    )
    part_gates = lax.dynamic_slice_in_dim(
        gates_all, group_index * length + part_start, part_rows, 0
    )
    logit_low = (
        part_gates * (gate_grad - jnp.sum(part_gates * gate_grad, axis=1, keepdims=True))
    ).astype(jnp.bfloat16)
    grad_router = lead_dot(second_part, logit_low)
    grad_second = grad_second + tail_dot(logit_low, router_weight)
    residual_back, grad_feedforward_gain = norm_back(
        grad_second, unit_two, factor_two, feedforward_gain
    )
    grad_residual = own_part(cotangent).astype(jnp.float32) + residual_back
    attention_grad = lax.all_gather(
        grad_residual.astype(jnp.bfloat16), "tensor", axis=0, tiled=True
    )
    grad_out_weight = lead_dot(head_out, attention_grad)
    head_grad = (
        tail_dot(attention_grad, out_weight).astype(jnp.bfloat16).reshape(length, local_heads, VD)
    )
    weight_grad = jnp.einsum("qhd,khd->hqk", head_grad, values, preferred_element_type=jnp.float32)
    score_grad = (
        weights * (weight_grad - jnp.sum(weights * weight_grad, axis=-1, keepdims=True))
    ).astype(jnp.bfloat16)
    query_grad = (
        jnp.einsum("hqk,khd->qhd", score_grad, key_rows, preferred_element_type=jnp.float32)
        * score_scale
    )
    key_grad = (
        jnp.einsum("hqk,qhd->khd", score_grad, queries, preferred_element_type=jnp.float32)
        * score_scale
    )
    value_grad = jnp.einsum(
        "hqk,qhd->khd", weights_low, head_grad, preferred_element_type=jnp.float32
    )
    query_low = (
        jnp.concatenate(
            [
                query_grad[..., :NOPE],
                rotate_back(query_grad[..., NOPE:], cosine[:, None], sine_table[:, None]),
            ],
            axis=-1,
        )
        .astype(jnp.bfloat16)
        .reshape(length, local_heads * head_width)
    )
    grad_query = lead_dot(first_norm, query_low)
    keyvalue_low = (
        jnp.concatenate([key_grad[..., :NOPE], value_grad], axis=-1)
        .astype(jnp.bfloat16)
        .reshape(length, local_heads * (NOPE + VD))
    )
    grad_latent_up = lead_dot(latent, keyvalue_low)
    latent_grad = tail_dot(keyvalue_low, latent_up)
    latent_back, grad_latent_gain = norm_back(latent_grad, unit_latent, factor_latent, latent_gain)
    rope_back = rotate_back(jnp.sum(key_grad[..., NOPE:], axis=1), cosine, sine_table)
    down_low = jnp.concatenate([latent_back, rope_back], axis=1).astype(jnp.bfloat16)
    grad_latent_down = lead_dot(first_norm, down_low)
    grad_first = lax.psum_scatter(
        (tail_dot(query_low, query_weight) + tail_dot(down_low, latent_down)).astype(jnp.bfloat16),
        "tensor",
        scatter_dimension=0,
        tiled=True,
    ).astype(jnp.float32)
    input_back, grad_attention_gain = norm_back(
        grad_first, own_part(unit_one), own_part(factor_one), attention_gain
    )
    grad_input = lax.all_gather(
        (grad_residual + input_back).astype(jnp.bfloat16), "tensor", axis=0, tiled=True
    ).astype(jnp.float32)

    pack_columns = latent_down.shape[1] + experts_all
    gains = jnp.concatenate(
        [
            grad_attention_gain.reshape(group_count, -1),
            grad_feedforward_gain.reshape(group_count, -1),
            grad_latent_gain.reshape(group_count, -1),
        ],
        axis=1,
    )
    gain_rows = 16 * tensor_count
    packed = jnp.concatenate(
        [
            jnp.concatenate([grad_latent_down, grad_router], axis=1).reshape(
                group_count, shard_columns, pack_columns
            ),
            jnp.pad(
                gains[:, None, :],
                ((0, 0), (0, gain_rows - 1), (0, pack_columns - gains.shape[1])),
            ),
        ],
        axis=1,
    ).astype(jnp.bfloat16)
    packed = scatter_rows(packed.reshape(-1, pack_columns))
    packed = lax.all_gather(packed, "tensor", axis=0, tiled=True).astype(jnp.float32)
    gain_row = packed[shard_columns]
    gain_cut = model_width // group_count

    def expert_sum(array, dimension):
        return lax.psum_scatter(
            array.astype(jnp.bfloat16), "expert", scatter_dimension=dimension, tiled=True
        ).astype(jnp.float32)

    return (
        result,
        grad_input,
        gain_row[:gain_cut],
        gain_row[gain_cut : 2 * gain_cut],
        gain_row[2 * gain_cut : 2 * gain_cut + KVR // group_count],
        expert_sum(grad_query, 0),
        packed[:shard_columns, : latent_down.shape[1]],
        expert_sum(grad_latent_up, 0),
        expert_sum(grad_out_weight, 1),
        packed[:shard_columns, latent_down.shape[1] :],
        grad_shared_gate,
        grad_shared_up,
        grad_shared_down,
        jnp.stack(grad_gate_list),
        jnp.stack(grad_up_list),
        jnp.stack(grad_down_list),
    )


def solution(mesh):
    placed = (
        P("expert", None),
        P("expert", None),
        P("expert"),
        P("expert", None),
        P("expert", None),
        P(),
        P(),
        P(),
        P(None, "tensor"),
        P(),
        P(None, "tensor"),
        P("tensor", None),
        P(),
        P(None, "tensor"),
        P(None, "tensor"),
        P("tensor", None),
        P("expert", None, "tensor"),
        P("expert", None, "tensor"),
        P("expert", "tensor", None),
    )
    return jax.shard_map(
        on_device,
        mesh=mesh,
        in_specs=placed,
        out_specs=(
            P("expert", None),
            P("expert", None),
            P("expert"),
            P("expert"),
            P("expert"),
            P("expert", "tensor"),
            P("expert", None),
            P("expert", "tensor"),
            P("tensor", "expert"),
            P("expert", None),
            P("expert", "tensor"),
            P("expert", "tensor"),
            P("tensor", "expert"),
            P("expert", None, "tensor"),
            P("expert", None, "tensor"),
            P("expert", "tensor", None),
        ),
        check_vma=False,
    )
```

```python
import functools
import math

import jax
import jax.numpy as jnp
from jax import lax
from jax.experimental import pallas as pl
from jax.experimental.pallas import tpu as pltpu
from jax.sharding import PartitionSpec as P

NOPE = 128
ROPE = 64
VD = 128
KVR = 512
TOP = 6


EPSILON = 1e-06


def plain_dot(left_side, right_side):
    return jnp.dot(left_side, right_side, preferred_element_type=jnp.float32)


def lead_dot(left_side, right_side):
    return lax.dot_general(
        left_side, right_side, (((0,), (0,)), ((), ())), preferred_element_type=jnp.float32
    )


def tail_dot(left_side, right_side):
    return lax.dot_general(
        left_side, right_side, (((1,), (1,)), ((), ())), preferred_element_type=jnp.float32
    )


def normalize(values, gain_vector):
    factor = lax.rsqrt(jnp.mean(values * values, axis=-1, keepdims=True) + EPSILON)
    unit_rows = values * factor
    return (unit_rows * gain_vector, unit_rows, factor)


def norm_back(upstream, unit_rows, factor, gain_vector):
    scaled = upstream * gain_vector
    inner_mean = jnp.mean(scaled * unit_rows, axis=-1, keepdims=True)
    return (factor * (scaled - unit_rows * inner_mean), jnp.sum(upstream * unit_rows, axis=0))


def rope_tables(positions):
    half_width = ROPE // 2
    frequency = 10000.0 ** (-2.0 * jnp.arange(half_width, dtype=jnp.float32) / ROPE)
    angles = positions.astype(jnp.float32)[:, None] * frequency[None, :]
    return (jnp.cos(angles), jnp.sin(angles))


def rotate(values, cosine, sine_table):
    half_width = values.shape[-1] // 2
    front_half = values[..., :half_width]
    back_half = values[..., half_width:]
    return jnp.concatenate(
        [
            front_half * cosine - back_half * sine_table,
            back_half * cosine + front_half * sine_table,
        ],
        axis=-1,
    )


def rotate_back(values, cosine, sine_table):
    half_width = values.shape[-1] // 2
    front_half = values[..., :half_width]
    back_half = values[..., half_width:]
    return jnp.concatenate(
        [
            front_half * cosine + back_half * sine_table,
            back_half * cosine - front_half * sine_table,
        ],
        axis=-1,
    )


BOTH = ("expert", "tensor")


def visible_mask(positions, length):
    rows = jnp.arange(length, dtype=jnp.int32)
    starts = rows - positions
    return (rows[None, :] <= rows[:, None]) & (rows[None, :] >= starts[:, None])


def gather_rows(rows):
    return lax.all_gather(rows, BOTH, axis=0, tiled=True)


def scatter_rows(rows):
    return lax.psum_scatter(rows, BOTH, scatter_dimension=0, tiled=True)


def expert_table(routes, values, expert_total):
    ids = jnp.arange(expert_total, dtype=jnp.int32)
    table = jnp.zeros((routes.shape[0], expert_total), jnp.float32)
    for member in range(TOP):
        table = table + jnp.where(
            routes[:, member : member + 1] == ids[None, :], values[:, member : member + 1], 0.0
        )
    return table


MESH = pl.DeviceIdType.MESH
LANES = 128


def expert_kernel(
    part_ref,
    cotangent_ref,
    code_ref,
    gate_ref,
    up_ref,
    down_ref,
    shared_gate_ref,
    shared_up_ref,
    shared_down_ref,
    router_ref,
    rows_ref,
    branch_ref,
    hidden_ref,
    dhidden_ref,
    shared_hidden_ref,
    shared_dhidden_ref,
    grad_ref,
    gate_w,
    up_w,
    down_w,
    shared_gate_w,
    shared_up_w,
    shared_down_w,
    router_w,
    rows_buf,
    cotangent_buf,
    code_buf,
    gates_buf,
    kept_buf,
    gate_grad_buf,
    hidden_buf,
    dhidden_buf,
    shared_hidden_buf,
    shared_dhidden_buf,
    branch_buf,
    grad_buf,
    core_land,
    side_send,
    side_keep,
    side_land,
    owner_send,
    owner_land,
    weight_sem,
    own_sem,
    load_sem,
    store_sem,
    spread_send_sem,
    side_spread_sem,
    core_spread_sem,
    arrive_sem,
    core_sem,
    core_land_sem,
    side_sem,
    side_land_sem,
    owner_sem,
    owner_land_sem,
    *,
    groups,
    tensors,
):
    sides = tensors // 2
    length = rows_buf.shape[1]
    part_rows = length // tensors
    width = rows_buf.shape[2]
    local_experts = gate_w.shape[0]
    me = lax.axis_index("expert")
    mine = lax.axis_index("tensor")
    side = mine // 2
    core = mine % 2
    sibling = side * 2 + (1 - core)

    def tensor_of(shift):
        return ((side + shift) % sides) * 2 + core

    weight_pairs = (
        (gate_ref, gate_w),
        (up_ref, up_w),
        (down_ref, down_w),
        (shared_gate_ref, shared_gate_w),
        (shared_up_ref, shared_up_w),
        (shared_down_ref, shared_down_w),
        (router_ref, router_w),
    )

    def weight_copy(index):
        return pltpu.make_async_copy(
            weight_pairs[index][0], weight_pairs[index][1], weight_sem.at[index]
        )

    def sequence_of(step):
        return (me + step) % groups

    def load_copies(step):
        slot = step % 2
        sequence = sequence_of(step)
        return (
            pltpu.make_async_copy(
                rows_ref.at[sequence], rows_buf.at[slot], load_sem.at[slot, 0]
            ),
            pltpu.make_async_copy(
                cotangent_ref.at[sequence], cotangent_buf.at[slot], load_sem.at[slot, 1]
            ),
            pltpu.make_async_copy(
                code_ref.at[sequence], code_buf.at[slot], load_sem.at[slot, 2]
            ),
        )

    def store_copies(step):
        sequence = sequence_of(step)
        return (
            pltpu.make_async_copy(hidden_buf, hidden_ref.at[:, sequence], store_sem.at[0]),
            pltpu.make_async_copy(dhidden_buf, dhidden_ref.at[:, sequence], store_sem.at[1]),
            pltpu.make_async_copy(
                shared_hidden_buf, shared_hidden_ref.at[sequence], store_sem.at[2]
            ),
            pltpu.make_async_copy(
                shared_dhidden_buf, shared_dhidden_ref.at[:, sequence], store_sem.at[3]
            ),
            pltpu.make_async_copy(branch_buf, branch_ref.at[sequence], store_sem.at[4]),
        )

    def piece(step, tensor):
        return rows_ref.at[sequence_of(step), pl.ds(pl.multiple_of(tensor * part_rows, part_rows), part_rows), :]

    def peer_spread(step):
        return pltpu.make_async_remote_copy(
            src_ref=part_ref,
            dst_ref=rows_ref.at[me, pl.ds(pl.multiple_of(mine * part_rows, part_rows), part_rows), :],
            send_sem=spread_send_sem.at[step],
            recv_sem=arrive_sem.at[step, mine],
            device_id={"expert": (me + groups - step) % groups},
            device_id_type=MESH,
        )

    def side_spread(step, shift):
        return pltpu.make_async_remote_copy(
            src_ref=piece(step, mine),
            dst_ref=piece(step, mine),
            send_sem=side_spread_sem.at[step, shift],
            recv_sem=arrive_sem.at[step, mine],
            device_id={"tensor": tensor_of(shift)},
            device_id_type=MESH,
        )

    def core_spread(step, shift):
        tensor = tensor_of(shift)
        return pltpu.make_async_remote_copy(
            src_ref=piece(step, tensor),
            dst_ref=piece(step, tensor),
            send_sem=core_spread_sem.at[step, shift],
            recv_sem=arrive_sem.at[step, tensor],
            device_id={"tensor": sibling},
            device_id_type=MESH,
        )

    def wait_piece(step, tensor):
        view = piece(step, tensor)
        pltpu.make_async_copy(view, view, arrive_sem.at[step, tensor]).wait()

    def forward_own(step):
        for shift in range(1, sides):
            side_spread(step, shift).start()
        core_spread(step, 0).start()

    def forward_sides(step):
        for shift in range(1, sides):
            wait_piece(step, tensor_of(shift))
            core_spread(step, shift).start()

    def await_sibling(step):
        for shift in range(sides):
            wait_piece(step, ((side + shift) % sides) * 2 + (1 - core))

    def core_send(step):
        slot = step % 2
        return pltpu.make_async_remote_copy(
            src_ref=grad_buf.at[slot, :, 1 - core],
            dst_ref=core_land.at[slot],
            send_sem=core_sem.at[slot],
            recv_sem=core_land_sem.at[slot],
            device_id={"tensor": sibling},
            device_id_type=MESH,
        )

    def side_copy(step, shift):
        slot = step % 2
        return pltpu.make_async_remote_copy(
            src_ref=side_send.at[slot, shift - 1],
            dst_ref=side_land.at[slot, shift - 1],
            send_sem=side_sem.at[slot, shift - 1],
            recv_sem=side_land_sem.at[slot, shift - 1],
            device_id={"tensor": tensor_of(shift)},
            device_id_type=MESH,
        )

    def owner_copy(step):
        slot = step % 2
        return pltpu.make_async_remote_copy(
            src_ref=owner_send.at[slot],
            dst_ref=owner_land.at[step],
            send_sem=owner_sem.at[slot],
            recv_sem=owner_land_sem.at[step],
            device_id={"expert": sequence_of(step)},
            device_id_type=MESH,
        )

    def reduce_core(step):
        slot = step % 2
        copy = core_send(step)
        copy.wait_recv()
        copy.wait_send()

        @pl.when(step >= 2)
        def _():
            for shift in range(1, sides):
                side_copy(step - 2, shift).wait_send()

        for shift in range(sides):
            other = (side + shift) % sides
            total = grad_buf[slot, other, core].astype(jnp.float32) + core_land[
                slot, other
            ].astype(jnp.float32)
            if shift == 0:
                side_keep[slot] = total
            else:
                side_send[slot, shift - 1] = total.astype(jnp.bfloat16)
                side_copy(step, shift).start()

    def reduce_sides(step):
        slot = step % 2
        for shift in range(1, sides):
            side_copy(step, shift).wait_recv()
        total = side_keep[slot]
        for shift in range(1, sides):
            total = total + side_land[slot, shift - 1].astype(jnp.float32)

        @pl.when(step == 0)
        def _():
            owner_land[0] = total.astype(jnp.bfloat16)

        @pl.when(step > 0)
        def _():
            @pl.when(step >= 3)
            def _():
                owner_copy(step - 2).wait_send()

            owner_send[slot] = total.astype(jnp.bfloat16)
            owner_copy(step).start()

    for index in range(len(weight_pairs)):
        weight_copy(index).start()
    barrier = pltpu.get_barrier_semaphore()
    for step in range(1, groups):
        pl.semaphore_signal(
            barrier, inc=1, device_id={"expert": (me + step) % groups}, device_id_type=MESH
        )
    for shift in range(1, sides):
        pl.semaphore_signal(
            barrier, inc=1, device_id={"tensor": tensor_of(shift)}, device_id_type=MESH
        )
    pl.semaphore_signal(barrier, inc=1, device_id={"tensor": sibling}, device_id_type=MESH)
    own_copy = pltpu.make_async_copy(part_ref, piece(0, mine), own_sem)
    own_copy.start()
    pl.semaphore_wait(barrier, groups + sides - 1)
    own_copy.wait()
    forward_own(0)
    for step in range(1, groups):
        peer_spread(step).start()
    forward_sides(0)
    await_sibling(0)
    for copy in load_copies(0):
        copy.start()
    if groups > 1:
        wait_piece(1, mine)
        forward_own(1)
    for index in range(len(weight_pairs)):
        weight_copy(index).wait()

    def step_body(step, carry):
        slot = step % 2
        for copy in load_copies(step):
            copy.wait()

        @pl.when(step > 0)
        def _():
            for copy in store_copies(step - 1):
                copy.wait()

        logits = jnp.dot(rows_buf[slot], router_w[...], preferred_element_type=jnp.float32)
        code = code_buf[slot].astype(jnp.float32)
        lane = lax.broadcasted_iota(jnp.int32, code.shape, 1)
        named = code > 0.5
        highest = jnp.max(jnp.where(named, logits, -jnp.inf), axis=1, keepdims=True)
        raised = jnp.where(named, jnp.exp(logits - highest), 0.0)
        kept = jnp.where(code > 1.5, 1.0, 0.0)
        gates = raised / jnp.sum(raised, axis=1, keepdims=True) * kept
        for member in range(local_experts):
            chosen = lane == me * local_experts + member
            gates_buf[member] = jnp.broadcast_to(
                jnp.sum(jnp.where(chosen, gates, 0.0), axis=1, keepdims=True), code.shape
            )
            kept_buf[member] = jnp.where(chosen, kept, 0.0)

        row_block = min(256, length)

        def expert_rows(block, inner):
            rows = pl.ds(pl.multiple_of(block * row_block, row_block), row_block)
            here = rows_buf[slot, rows, :]
            back = cotangent_buf[slot, rows, :]
            gate_grad = jnp.zeros((row_block, LANES), jnp.float32)
            for member in range(local_experts):
                pre = jnp.dot(here, gate_w[member], preferred_element_type=jnp.float32)
                lin = jnp.dot(here, up_w[member], preferred_element_type=jnp.float32)
                dhid = lax.dot_general(
                    back,
                    down_w[member],
                    (((1,), (1,)), ((), ())),
                    preferred_element_type=jnp.float32,
                )
                gate = gates_buf[member, rows, :][:, 0:1]
                sigmoid = jax.nn.sigmoid(pre)
                active = pre * sigmoid
                hid = active * lin
                gate_grad = gate_grad + kept_buf[member, rows, :] * jnp.sum(
                    hid * dhid, axis=1, keepdims=True
                )
                dhid = dhid * gate
                hidden_buf[member, rows, :] = (hid * gate).astype(jnp.bfloat16)
                dhidden_buf[member, rows, :] = (
                    dhid * lin * sigmoid * (1.0 + pre * (1.0 - sigmoid))
                ).astype(jnp.bfloat16)
                dhidden_buf[local_experts + member, rows, :] = (dhid * active).astype(jnp.bfloat16)
            gate_grad_buf[rows, :] = gate_grad
            return inner

        lax.fori_loop(0, length // row_block, expert_rows, 0)

        @pl.when(step + 2 < groups)
        def _():
            wait_piece(step + 2, mine)
            forward_own(step + 2)

        @pl.when(step + 1 < groups)
        def _():
            forward_sides(step + 1)

        def shared_rows(block, inner):
            rows = pl.ds(pl.multiple_of(block * row_block, row_block), row_block)
            here = rows_buf[slot, rows, :]
            back = cotangent_buf[slot, rows, :]
            pre = jnp.dot(here, shared_gate_w[...], preferred_element_type=jnp.float32)
            lin = jnp.dot(here, shared_up_w[...], preferred_element_type=jnp.float32)
            dhid = lax.dot_general(
                back,
                shared_down_w[...],
                (((1,), (1,)), ((), ())),
                preferred_element_type=jnp.float32,
            )
            sigmoid = jax.nn.sigmoid(pre)
            active = pre * sigmoid
            shared_hidden_buf[rows, :] = (active * lin).astype(jnp.bfloat16)
            shared_dhidden_buf[0, rows, :] = (
                dhid * lin * sigmoid * (1.0 + pre * (1.0 - sigmoid))
            ).astype(jnp.bfloat16)
            shared_dhidden_buf[1, rows, :] = (dhid * active).astype(jnp.bfloat16)
            return inner

        lax.fori_loop(0, length // row_block, shared_rows, 0)

        @pl.when(step + 1 < groups)
        def _():
            await_sibling(step + 1)
            for copy in load_copies(step + 1):
                copy.start()

        @pl.when(step >= 2)
        def _():
            reduce_sides(step - 2)

        @pl.when(step >= 1)
        def _():
            reduce_core(step - 1)

        column_block = 512

        def mix_columns(block, inner):
            columns = pl.ds(pl.multiple_of(block * column_block, column_block), column_block)
            total = jnp.dot(
                hidden_buf[0], down_w[0, :, columns], preferred_element_type=jnp.float32
            )
            for member in range(1, local_experts):
                total = total + jnp.dot(
                    hidden_buf[member],
                    down_w[member, :, columns],
                    preferred_element_type=jnp.float32,
                )
            branch_buf[:, columns] = total.astype(jnp.bfloat16)
            total = None
            for member in range(local_experts):
                for half, weight in ((0, gate_w), (1, up_w)):
                    term = lax.dot_general(
                        dhidden_buf[half * local_experts + member],
                        weight[member, columns, :],
                        (((1,), (1,)), ((), ())),
                        preferred_element_type=jnp.float32,
                    )
                    total = term if total is None else total + term
            grad_buf[slot, :, :, :, columns] = total.astype(jnp.bfloat16).reshape(
                sides, 2, part_rows, column_block
            )
            return inner

        lax.fori_loop(0, width // column_block, mix_columns, 0)

        @pl.when(step == 0)
        def _():
            def mix_shared(block, inner):
                columns = pl.ds(pl.multiple_of(block * column_block, column_block), column_block)
                branch_buf[:, columns] = (
                    branch_buf[:, columns].astype(jnp.float32)
                    + jnp.dot(
                        shared_hidden_buf[...],
                        shared_down_w[:, columns],
                        preferred_element_type=jnp.float32,
                    )
                ).astype(jnp.bfloat16)
                total = lax.dot_general(
                    shared_dhidden_buf[0],
                    shared_gate_w[columns, :],
                    (((1,), (1,)), ((), ())),
                    preferred_element_type=jnp.float32,
                ) + lax.dot_general(
                    shared_dhidden_buf[1],
                    shared_up_w[columns, :],
                    (((1,), (1,)), ((), ())),
                    preferred_element_type=jnp.float32,
                )
                grad_buf[0, :, :, :, columns] = (
                    grad_buf[0, :, :, :, columns].astype(jnp.float32)
                    + total.reshape(sides, 2, part_rows, column_block)
                ).astype(jnp.bfloat16)
                return inner

            lax.fori_loop(0, width // column_block, mix_shared, 0)

        grad_buf[slot, :, :, :, pl.ds(width, LANES)] = (
            gate_grad_buf[...].astype(jnp.bfloat16).reshape(sides, 2, part_rows, LANES)
        )
        core_send(step).start()
        for copy in store_copies(step):
            copy.start()
        return carry

    lax.fori_loop(0, groups, step_body, 0)

    if groups > 1:
        reduce_sides(groups - 2)
    reduce_core(groups - 1)
    reduce_sides(groups - 1)
    total = owner_land[0].astype(jnp.float32)
    for step in range(1, groups):
        owner_copy(step).wait_recv()
        total = total + owner_land[step].astype(jnp.float32)
    grad_ref[...] = total

    for copy in store_copies(groups - 1):
        copy.wait()
    for step in range(groups):
        if step > 0:
            peer_spread(step).wait_send()
        for shift in range(1, sides):
            side_spread(step, shift).wait_send()
        for shift in range(sides):
            core_spread(step, shift).wait_send()
    for step in range(max(groups - 2, 0), groups):
        for shift in range(1, sides):
            side_copy(step, shift).wait_send()
        if step > 0:
            owner_copy(step).wait_send()


def run_experts(
    part,
    cotangent_all,
    code_all,
    expert_gate,
    expert_up,
    expert_down,
    shared_gate,
    shared_up,
    shared_down,
    router_padded,
    length,
):
    groups = lax.axis_size("expert")
    tensors = lax.axis_size("tensor")
    sides = tensors // 2
    part_rows = length // tensors
    local_experts, width, hidden = expert_gate.shape
    shared = shared_gate.shape[1]
    bf16 = jnp.bfloat16
    f32 = jnp.float32
    packed = width + LANES
    anywhere = pl.BlockSpec(memory_space=pl.ANY)
    dma = pltpu.SemaphoreType.DMA
    flops = (
        2 * groups * length * width * 6 * local_experts * hidden
        + 2 * groups * length * width * 3 * shared
    )
    return pl.pallas_call(
        functools.partial(expert_kernel, groups=groups, tensors=tensors),
        out_shape=(
            jax.ShapeDtypeStruct((groups, length, width), bf16),
            jax.ShapeDtypeStruct((groups, length, width), bf16),
            jax.ShapeDtypeStruct((local_experts, groups, length, hidden), bf16),
            jax.ShapeDtypeStruct((2 * local_experts, groups, length, hidden), bf16),
            jax.ShapeDtypeStruct((groups, length, shared), bf16),
            jax.ShapeDtypeStruct((2, groups, length, shared), bf16),
            jax.ShapeDtypeStruct((part_rows, packed), f32),
        ),
        in_specs=[anywhere] * 10,
        out_specs=(anywhere,) * 6 + (pl.BlockSpec(memory_space=pltpu.VMEM),),
        scratch_shapes=[
            pltpu.VMEM((local_experts, width, hidden), bf16),
            pltpu.VMEM((local_experts, width, hidden), bf16),
            pltpu.VMEM((local_experts, hidden, width), bf16),
            pltpu.VMEM((width, shared), bf16),
            pltpu.VMEM((width, shared), bf16),
            pltpu.VMEM((shared, width), bf16),
            pltpu.VMEM((width, LANES), bf16),
            pltpu.VMEM((2, length, width), bf16),
            pltpu.VMEM((2, length, width), bf16),
            pltpu.VMEM((2, length, LANES), bf16),
            pltpu.VMEM((local_experts, length, LANES), f32),
            pltpu.VMEM((local_experts, length, LANES), f32),
            pltpu.VMEM((length, LANES), f32),
            pltpu.VMEM((local_experts, length, hidden), bf16),
            pltpu.VMEM((2 * local_experts, length, hidden), bf16),
            pltpu.VMEM((length, shared), bf16),
            pltpu.VMEM((2, length, shared), bf16),
            pltpu.VMEM((length, width), bf16),
            pltpu.VMEM((2, sides, 2, part_rows, packed), bf16),
            pltpu.VMEM((2, sides, part_rows, packed), bf16),
            pltpu.VMEM((2, sides - 1, part_rows, packed), bf16),
            pltpu.VMEM((2, part_rows, packed), f32),
            pltpu.VMEM((2, sides - 1, part_rows, packed), bf16),
            pltpu.VMEM((2, part_rows, packed), bf16),
            pltpu.VMEM((groups, part_rows, packed), bf16),
            dma((7,)),
            dma(()),
            dma((2, 3)),
            dma((5,)),
            dma((groups,)),
            dma((groups, sides)),
            dma((groups, sides)),
            dma((groups, tensors)),
            dma((2,)),
            dma((2,)),
            dma((2, sides - 1)),
            dma((2, sides - 1)),
            dma((2,)),
            dma((groups,)),
        ],
        compiler_params=pltpu.CompilerParams(
            collective_id=1,
            has_side_effects=True,
            vmem_limit_bytes=60 * 1024 * 1024,
        ),
        cost_estimate=pl.CostEstimate(
            flops=flops, bytes_accessed=100_000_000, transcendentals=0
        ),
        name="experts",
    )(
        part,
        cotangent_all.reshape(groups, length, width),
        code_all.reshape(groups, length, LANES),
        expert_gate,
        expert_up,
        expert_down,
        shared_gate,
        shared_up,
        shared_down,
        router_padded,
    )


def on_device(
    inputs,
    cotangent,
    positions,
    routes,
    slot_index,
    attention_gain,
    feedforward_gain,
    latent_gain,
    query_weight,
    latent_down,
    latent_up,
    out_weight,
    router_weight,
    shared_gate,
    shared_up,
    shared_down,
    expert_gate,
    expert_up,
    expert_down,
):
    length, model_width = inputs.shape
    tensor_count = lax.axis_size("tensor")
    group_count = lax.axis_size("expert")
    tensor_index = lax.axis_index("tensor")
    group_index = lax.axis_index("expert")
    head_width = NOPE + ROPE
    local_heads = query_weight.shape[1] // head_width
    local_experts, _, expert_hidden_width = expert_gate.shape
    shared_width = shared_gate.shape[1]
    experts_all = local_experts * group_count
    capacity = max(
        tensor_count, length * TOP * 4 // (3 * experts_all) // tensor_count * tensor_count
    )
    score_scale = 1.0 / math.sqrt(head_width)
    part_rows = length // tensor_count
    part_start = tensor_index * part_rows
    shard_columns = model_width // group_count

    def own_part(rows):
        return lax.dynamic_slice_in_dim(rows, part_start, part_rows, 0)

    def own_sequence(rows):
        return lax.dynamic_slice_in_dim(rows, group_index * length, length, 0)

    def own_columns(rows):
        return lax.dynamic_slice_in_dim(rows, group_index * shard_columns, shard_columns, 1)

    cotangent_all = gather_rows(own_part(cotangent))
    code_part = own_part(
        expert_table(routes, jnp.where(slot_index < capacity, 2.0, 1.0), LANES)
    )
    code_all = gather_rows(code_part.astype(jnp.bfloat16))

    rows_in = inputs.astype(jnp.float32)
    normed_one, unit_one, factor_one = normalize(rows_in, attention_gain)
    first_norm = normed_one.astype(jnp.bfloat16)
    cosine, sine_table = rope_tables(positions)
    query_raw = plain_dot(first_norm, query_weight).reshape(length, local_heads, head_width)
    queries = jnp.concatenate(
        [
            query_raw[..., :NOPE],
            rotate(query_raw[..., NOPE:], cosine[:, None], sine_table[:, None]),
        ],
        axis=-1,
    ).astype(jnp.bfloat16)
    latent_raw = plain_dot(first_norm, latent_down)
    latent_normed, unit_latent, factor_latent = normalize(latent_raw[:, :KVR], latent_gain)
    latent = latent_normed.astype(jnp.bfloat16)
    key_rope = rotate(latent_raw[:, KVR:], cosine, sine_table).astype(jnp.bfloat16)
    key_value = (
        plain_dot(latent, latent_up).astype(jnp.bfloat16).reshape(length, local_heads, NOPE + VD)
    )
    key_rows = jnp.concatenate(
        [
            key_value[..., :NOPE],
            jnp.broadcast_to(key_rope[:, None, :], (length, local_heads, ROPE)),
        ],
        axis=-1,
    )
    values = key_value[..., NOPE:]
    visible = visible_mask(positions, length)
    scores = jnp.where(
        visible[None],
        jnp.einsum("qhd,khd->hqk", queries, key_rows, preferred_element_type=jnp.float32)
        * score_scale,
        -jnp.inf,
    )
    weights = jax.nn.softmax(scores, axis=-1)
    weights_low = weights.astype(jnp.bfloat16)
    head_out = (
        jnp.einsum("hqk,khd->qhd", weights_low, values, preferred_element_type=jnp.float32)
        .astype(jnp.bfloat16)
        .reshape(length, local_heads * VD)
    )
    attention = lax.psum_scatter(
        plain_dot(head_out, out_weight).astype(jnp.bfloat16),
        "tensor",
        scatter_dimension=0,
        tiled=True,
    ).astype(jnp.float32)
    residual = own_part(rows_in) + attention
    normed_two, unit_two, factor_two = normalize(residual, feedforward_gain)
    second_part = normed_two.astype(jnp.bfloat16)
    (
        second_all,
        branch,
        hidden_all,
        dhidden_all,
        shared_hidden,
        shared_dhidden,
        grad_part,
    ) = run_experts(
        second_part,
        cotangent_all,
        code_all,
        expert_gate,
        expert_up,
        expert_down,
        shared_gate,
        shared_up,
        shared_down,
        jnp.pad(router_weight, ((0, 0), (0, LANES - experts_all))),
        length,
    )
    tokens = group_count * length
    second_all = second_all.reshape(tokens, model_width)
    hidden_all = hidden_all.reshape(local_experts, tokens, expert_hidden_width)
    dhidden_all = dhidden_all.reshape(2 * local_experts, tokens, expert_hidden_width)
    shared_hidden = shared_hidden.reshape(tokens, shared_width)
    shared_dhidden = shared_dhidden.reshape(2, tokens, shared_width)
    second_columns = own_columns(second_all)
    grad_shared_gate = lead_dot(second_columns, shared_dhidden[0])
    grad_shared_up = lead_dot(second_columns, shared_dhidden[1])
    grad_shared_down = lead_dot(shared_hidden, own_columns(cotangent_all))
    grad_gate_list = []
    grad_up_list = []
    grad_down_list = []
    for member in range(local_experts):
        grad_gate_list.append(lead_dot(second_all, dhidden_all[member]))
        grad_up_list.append(lead_dot(second_all, dhidden_all[local_experts + member]))
        grad_down_list.append(lead_dot(hidden_all[member], cotangent_all))

    feedforward = scatter_rows(branch.reshape(tokens, model_width)).astype(jnp.float32)
    result_part = (residual + feedforward).astype(jnp.bfloat16)
    result = lax.all_gather(result_part, "tensor", axis=0, tiled=True)

    grad_second = grad_part[:, :model_width]
    gate_grad = grad_part[:, model_width : model_width + experts_all]
    code_own = code_part[:, :experts_all]
    logits = jnp.where(code_own > 0, plain_dot(second_part, router_weight), -jnp.inf)
    part_gates = jax.nn.softmax(logits, axis=1)
    logit_low = (
        part_gates * (gate_grad - jnp.sum(part_gates * gate_grad, axis=1, keepdims=True))
    ).astype(jnp.bfloat16)
    grad_router = lead_dot(second_part, logit_low)
    grad_second = grad_second + tail_dot(logit_low, router_weight)
    residual_back, grad_feedforward_gain = norm_back(
        grad_second, unit_two, factor_two, feedforward_gain
    )
    grad_residual = own_part(cotangent).astype(jnp.float32) + residual_back
    attention_grad = lax.all_gather(
        grad_residual.astype(jnp.bfloat16), "tensor", axis=0, tiled=True
    )
    grad_out_weight = lead_dot(head_out, attention_grad)
    head_grad = (
        tail_dot(attention_grad, out_weight).astype(jnp.bfloat16).reshape(length, local_heads, VD)
    )
    weight_grad = jnp.einsum("qhd,khd->hqk", head_grad, values, preferred_element_type=jnp.float32)
    score_grad = (
        weights * (weight_grad - jnp.sum(weights * weight_grad, axis=-1, keepdims=True))
    ).astype(jnp.bfloat16)
    query_grad = (
        jnp.einsum("hqk,khd->qhd", score_grad, key_rows, preferred_element_type=jnp.float32)
        * score_scale
    )
    key_grad = (
        jnp.einsum("hqk,qhd->khd", score_grad, queries, preferred_element_type=jnp.float32)
        * score_scale
    )
    value_grad = jnp.einsum(
        "hqk,qhd->khd", weights_low, head_grad, preferred_element_type=jnp.float32
    )
    query_low = (
        jnp.concatenate(
            [
                query_grad[..., :NOPE],
                rotate_back(query_grad[..., NOPE:], cosine[:, None], sine_table[:, None]),
            ],
            axis=-1,
        )
        .astype(jnp.bfloat16)
        .reshape(length, local_heads * head_width)
    )
    grad_query = lead_dot(first_norm, query_low)
    keyvalue_low = (
        jnp.concatenate([key_grad[..., :NOPE], value_grad], axis=-1)
        .astype(jnp.bfloat16)
        .reshape(length, local_heads * (NOPE + VD))
    )
    grad_latent_up = lead_dot(latent, keyvalue_low)
    latent_grad = tail_dot(keyvalue_low, latent_up)
    latent_back, grad_latent_gain = norm_back(latent_grad, unit_latent, factor_latent, latent_gain)
    rope_back = rotate_back(jnp.sum(key_grad[..., NOPE:], axis=1), cosine, sine_table)
    down_low = jnp.concatenate([latent_back, rope_back], axis=1).astype(jnp.bfloat16)
    grad_latent_down = lead_dot(first_norm, down_low)
    grad_first = lax.psum_scatter(
        (tail_dot(query_low, query_weight) + tail_dot(down_low, latent_down)).astype(jnp.bfloat16),
        "tensor",
        scatter_dimension=0,
        tiled=True,
    ).astype(jnp.float32)
    input_back, grad_attention_gain = norm_back(
        grad_first, own_part(unit_one), own_part(factor_one), attention_gain
    )
    grad_input = lax.all_gather(
        (grad_residual + input_back).astype(jnp.bfloat16), "tensor", axis=0, tiled=True
    ).astype(jnp.float32)

    pack_columns = latent_down.shape[1] + experts_all
    gains = jnp.concatenate(
        [
            grad_attention_gain.reshape(group_count, -1),
            grad_feedforward_gain.reshape(group_count, -1),
            grad_latent_gain.reshape(group_count, -1),
        ],
        axis=1,
    )
    gain_rows = 16 * tensor_count
    packed = jnp.concatenate(
        [
            jnp.concatenate([grad_latent_down, grad_router], axis=1).reshape(
                group_count, shard_columns, pack_columns
            ),
            jnp.pad(
                gains[:, None, :],
                ((0, 0), (0, gain_rows - 1), (0, pack_columns - gains.shape[1])),
            ),
        ],
        axis=1,
    ).astype(jnp.bfloat16)
    packed = scatter_rows(packed.reshape(-1, pack_columns))
    packed = lax.all_gather(packed, "tensor", axis=0, tiled=True).astype(jnp.float32)
    gain_row = packed[shard_columns]
    gain_cut = model_width // group_count

    def expert_sum(array, dimension):
        return lax.psum_scatter(
            array.astype(jnp.bfloat16), "expert", scatter_dimension=dimension, tiled=True
        ).astype(jnp.float32)

    return (
        result,
        grad_input,
        gain_row[:gain_cut],
        gain_row[gain_cut : 2 * gain_cut],
        gain_row[2 * gain_cut : 2 * gain_cut + KVR // group_count],
        expert_sum(grad_query, 0),
        packed[:shard_columns, : latent_down.shape[1]],
        expert_sum(grad_latent_up, 0),
        expert_sum(grad_out_weight, 1),
        packed[:shard_columns, latent_down.shape[1] :],
        grad_shared_gate,
        grad_shared_up,
        grad_shared_down,
        jnp.stack(grad_gate_list),
        jnp.stack(grad_up_list),
        jnp.stack(grad_down_list),
    )


def solution(mesh):
    placed = (
        P("expert", None),
        P("expert", None),
        P("expert"),
        P("expert", None),
        P("expert", None),
        P(),
        P(),
        P(),
        P(None, "tensor"),
        P(),
        P(None, "tensor"),
        P("tensor", None),
        P(),
        P(None, "tensor"),
        P(None, "tensor"),
        P("tensor", None),
        P("expert", None, "tensor"),
        P("expert", None, "tensor"),
        P("expert", "tensor", None),
    )
    return jax.shard_map(
        on_device,
        mesh=mesh,
        in_specs=placed,
        out_specs=(
            P("expert", None),
            P("expert", None),
            P("expert"),
            P("expert"),
            P("expert"),
            P("expert", "tensor"),
            P("expert", None),
            P("expert", "tensor"),
            P("tensor", "expert"),
            P("expert", None),
            P("expert", "tensor"),
            P("expert", "tensor"),
            P("tensor", "expert"),
            P("expert", None, "tensor"),
            P("expert", None, "tensor"),
            P("expert", "tensor", None),
        ),
        check_vma=False,
    )
```

```python
import functools
import math

import jax
import jax.numpy as jnp
from jax import lax
from jax.experimental import pallas as pl
from jax.experimental.pallas import tpu as pltpu
from jax.sharding import PartitionSpec as P

NOPE = 128
ROPE = 64
VD = 128
KVR = 512
TOP = 6


EPSILON = 1e-06


def plain_dot(left_side, right_side):
    return jnp.dot(left_side, right_side, preferred_element_type=jnp.float32)


def lead_dot(left_side, right_side):
    return lax.dot_general(
        left_side, right_side, (((0,), (0,)), ((), ())), preferred_element_type=jnp.float32
    )


def tail_dot(left_side, right_side):
    return lax.dot_general(
        left_side, right_side, (((1,), (1,)), ((), ())), preferred_element_type=jnp.float32
    )


def normalize(values, gain_vector):
    factor = lax.rsqrt(jnp.mean(values * values, axis=-1, keepdims=True) + EPSILON)
    unit_rows = values * factor
    return (unit_rows * gain_vector, unit_rows, factor)


def norm_back(upstream, unit_rows, factor, gain_vector):
    scaled = upstream * gain_vector
    inner_mean = jnp.mean(scaled * unit_rows, axis=-1, keepdims=True)
    return (factor * (scaled - unit_rows * inner_mean), jnp.sum(upstream * unit_rows, axis=0))


def rope_tables(positions):
    half_width = ROPE // 2
    frequency = 10000.0 ** (-2.0 * jnp.arange(half_width, dtype=jnp.float32) / ROPE)
    angles = positions.astype(jnp.float32)[:, None] * frequency[None, :]
    return (jnp.cos(angles), jnp.sin(angles))


def rotate(values, cosine, sine_table):
    half_width = values.shape[-1] // 2
    front_half = values[..., :half_width]
    back_half = values[..., half_width:]
    return jnp.concatenate(
        [
            front_half * cosine - back_half * sine_table,
            back_half * cosine + front_half * sine_table,
        ],
        axis=-1,
    )


def rotate_back(values, cosine, sine_table):
    half_width = values.shape[-1] // 2
    front_half = values[..., :half_width]
    back_half = values[..., half_width:]
    return jnp.concatenate(
        [
            front_half * cosine + back_half * sine_table,
            back_half * cosine - front_half * sine_table,
        ],
        axis=-1,
    )


BOTH = ("expert", "tensor")


def visible_mask(positions, length):
    rows = jnp.arange(length, dtype=jnp.int32)
    starts = rows - positions
    return (rows[None, :] <= rows[:, None]) & (rows[None, :] >= starts[:, None])


def gather_rows(rows):
    return lax.all_gather(rows, BOTH, axis=0, tiled=True)


def scatter_rows(rows):
    return lax.psum_scatter(rows, BOTH, scatter_dimension=0, tiled=True)


def expert_table(routes, values, expert_total):
    ids = jnp.arange(expert_total, dtype=jnp.int32)
    table = jnp.zeros((routes.shape[0], expert_total), jnp.float32)
    for member in range(TOP):
        table = table + jnp.where(
            routes[:, member : member + 1] == ids[None, :], values[:, member : member + 1], 0.0
        )
    return table


MESH = pl.DeviceIdType.MESH
LANES = 128
LAYERS = 4
EPS = EPSILON


def dot_rows(left_side, right_side):
    return lax.dot_general(
        left_side, right_side, (((1,), (1,)), ((), ())), preferred_element_type=jnp.float32
    )


def dot_plain(left_side, right_side):
    return jnp.dot(left_side, right_side, preferred_element_type=jnp.float32)


class Place:
    def __init__(self, groups, tensors):
        self.groups = groups
        self.tensors = tensors
        self.layers = min(LAYERS, groups)
        self.lanes = groups // self.layers
        self.sides = tensors // 2
        self.me = lax.axis_index("expert")
        self.mine = lax.axis_index("tensor")
        self.layer = self.me // self.lanes
        self.lane = self.me % self.lanes
        self.side = self.mine // 2
        self.core = self.mine % 2
        self.sibling = self.side * 2 + (1 - self.core)

    def side_of(self, shift):
        return (self.side + shift) % self.sides

    def tensor_of(self, shift):
        return self.side_of(shift) * 2 + self.core

    def expert_of(self, layer_shift, lane_shift):
        return ((self.layer + layer_shift) % self.layers) * self.lanes + (
            self.lane + lane_shift
        ) % self.lanes

    def greet(self, peers):
        barrier = pltpu.get_barrier_semaphore()
        count = self.sides
        if peers:
            count = count + self.layers + self.lanes - 2
            partners = [self.expert_of(shift, 0) for shift in range(1, self.layers)]
            partners += [self.expert_of(0, shift) for shift in range(1, self.lanes)]
            for partner in partners:
                pl.semaphore_signal(
                    barrier, inc=1, device_id={"expert": partner}, device_id_type=MESH
                )
        for shift in range(1, self.sides):
            pl.semaphore_signal(
                barrier, inc=1, device_id={"tensor": self.tensor_of(shift)}, device_id_type=MESH
            )
        pl.semaphore_signal(
            barrier, inc=1, device_id={"tensor": self.sibling}, device_id_type=MESH
        )
        return barrier, count


def remote(source, target, send_sem, recv_sem, axis, index):
    return pltpu.make_async_remote_copy(
        src_ref=source,
        dst_ref=target,
        send_sem=send_sem,
        recv_sem=recv_sem,
        device_id={axis: index},
        device_id_type=MESH,
    )


def sum_over_tensor(place, terms, core_land, side_send, side_land, sems):
    core_send_sem, core_land_sem, side_send_sem, side_land_sem = sems
    core_copy = remote(
        terms.at[:, 1 - place.core],
        core_land,
        core_send_sem,
        core_land_sem,
        "tensor",
        place.sibling,
    )
    core_copy.start()
    core_copy.wait_recv()
    copies = []
    for shift in range(1, place.sides):
        other = place.side_of(shift)
        side_send[shift - 1] = (
            terms[other, place.core].astype(jnp.float32) + core_land[other].astype(jnp.float32)
        ).astype(jnp.bfloat16)
        copy = remote(
            side_send.at[shift - 1],
            side_land.at[shift - 1],
            side_send_sem.at[shift - 1],
            side_land_sem.at[shift - 1],
            "tensor",
            place.tensor_of(shift),
        )
        copy.start()
        copies.append(copy)
    total = terms[place.side, place.core].astype(jnp.float32) + core_land[place.side].astype(
        jnp.float32
    )
    for copy in copies:
        copy.wait_recv()
    for shift in range(1, place.sides):
        total = total + side_land[shift - 1].astype(jnp.float32)
    core_copy.wait_send()
    for copy in copies:
        copy.wait_send()
    return total


def spread_over_tensor(place, part, whole, sems):
    own_sem, side_sem, core_sem, arrive_sem = sems
    own_copy = pltpu.make_async_copy(part, whole.at[place.mine], own_sem)
    own_copy.start()
    sends = []
    for shift in range(1, place.sides):
        sends.append(
            remote(
                part,
                whole.at[place.mine],
                side_sem.at[shift],
                arrive_sem.at[place.mine],
                "tensor",
                place.tensor_of(shift),
            )
        )
    sends.append(
        remote(
            part,
            whole.at[place.mine],
            core_sem.at[0],
            arrive_sem.at[place.mine],
            "tensor",
            place.sibling,
        )
    )
    for copy in sends:
        copy.start()

    def wait_piece(tensor):
        view = whole.at[tensor]
        pltpu.make_async_copy(view, view, arrive_sem.at[tensor]).wait()

    for shift in range(1, place.sides):
        tensor = place.tensor_of(shift)
        wait_piece(tensor)
        copy = remote(
            whole.at[tensor],
            whole.at[tensor],
            core_sem.at[shift],
            arrive_sem.at[tensor],
            "tensor",
            place.sibling,
        )
        copy.start()
        sends.append(copy)
    for shift in range(place.sides):
        wait_piece(place.side_of(shift) * 2 + (1 - place.core))
    own_copy.wait()
    for copy in sends:
        copy.wait_send()


def forward_kernel(
    attention_ref,
    inputs_ref,
    gain_ref,
    gate_ref,
    up_ref,
    shared_gate_ref,
    shared_up_ref,
    router_ref,
    rows_ref,
    acts_ref,
    logits_ref,
    residual_ref,
    gate_w,
    up_w,
    shared_gate_w,
    shared_up_w,
    router_w,
    terms_buf,
    core_land,
    side_send,
    side_land,
    inputs_buf,
    part_buf,
    rows_buf,
    logits_buf,
    acts_buf,
    weight_sem,
    first_sem,
    load_sem,
    store_sem,
    sum_core_sem,
    sum_core_land_sem,
    sum_side_sem,
    sum_side_land_sem,
    layer_sem,
    layer_land_sem,
    lane_sem,
    lane_land_sem,
    side_sem,
    side_land_sem,
    lane_half_sem,
    lane_half_land_sem,
    side_half_sem,
    side_half_land_sem,
    core_sem,
    core_land_sem,
    *,
    groups,
    tensors,
):
    place = Place(groups, tensors)
    sides, layers, lanes = place.sides, place.layers, place.lanes
    me, mine, core = place.me, place.mine, place.core
    length = rows_buf.shape[1]
    width = rows_buf.shape[2]
    half = width // 2
    part_rows = length // tensors
    row_block = min(256, length)

    pairs = (
        (gate_ref, gate_w),
        (up_ref, up_w),
        (shared_gate_ref, shared_gate_w),
        (shared_up_ref, shared_up_w),
        (router_ref, router_w),
    )
    first_copies = (
        pltpu.make_async_copy(attention_ref, terms_buf, first_sem.at[0]),
        pltpu.make_async_copy(
            inputs_ref.at[pl.ds(pl.multiple_of(mine * part_rows, part_rows), part_rows), :],
            inputs_buf,
            first_sem.at[1],
        ),
    )
    for copy in first_copies:
        copy.start()
    weight_copies = [
        pltpu.make_async_copy(source, target, weight_sem.at[index])
        for index, (source, target) in enumerate(pairs)
    ]
    barrier, count = place.greet(True)

    def sequence_of(step):
        return place.expert_of(step // lanes, step % lanes)

    def load_copy(step):
        slot = step % 2
        return pltpu.make_async_copy(
            rows_ref.at[sequence_of(step)], rows_buf.at[slot], load_sem.at[slot]
        )

    def store_copies(step):
        slot = step % 2
        sequence = sequence_of(step)
        return (
            pltpu.make_async_copy(
                acts_buf.at[slot], acts_ref.at[:, sequence], store_sem.at[slot, 0]
            ),
            pltpu.make_async_copy(
                logits_buf.at[slot], logits_ref.at[sequence], store_sem.at[slot, 1]
            ),
        )

    def piece(layer_shift, lane_shift, tensor, columns=None):
        rows = pl.ds(pl.multiple_of(tensor * part_rows, part_rows), part_rows)
        sequence = place.expert_of(layer_shift, lane_shift)
        if columns is None:
            return rows_ref.at[sequence, rows, :]
        return rows_ref.at[sequence, rows, pl.ds(columns * half, half)]

    def await_bytes(view, sem):
        pltpu.make_async_copy(view, view, sem).wait()

    def layer_spread(shift):
        return remote(
            part_buf,
            piece(0, 0, mine),
            layer_sem.at[shift],
            layer_land_sem.at[shift],
            "expert",
            place.expert_of(layers - shift, 0),
        )

    def lane_spread(layer_shift, shift):
        view = piece(layer_shift, 0, mine)
        return remote(
            view,
            view,
            lane_sem.at[layer_shift, shift],
            lane_land_sem.at[layer_shift, shift],
            "expert",
            place.expert_of(0, lanes - shift),
        )

    def side_spread(layer_shift, shift):
        view = piece(layer_shift, 0, mine)
        return remote(
            view,
            view,
            side_sem.at[layer_shift, shift],
            side_land_sem.at[layer_shift, shift],
            "tensor",
            place.tensor_of(sides - shift),
        )

    def side_half_spread(layer_shift, lane_shift, shift):
        view = piece(layer_shift, lane_shift, mine, 0)
        return remote(
            view,
            view,
            side_half_sem.at[layer_shift, lane_shift, shift],
            side_half_land_sem.at[layer_shift, lane_shift, shift],
            "tensor",
            place.tensor_of(sides - shift),
        )

    def lane_half_spread(layer_shift, shift, side_shift):
        view = piece(layer_shift, 0, place.tensor_of(side_shift), 1)
        return remote(
            view,
            view,
            lane_half_sem.at[layer_shift, shift, side_shift],
            lane_half_land_sem.at[layer_shift, shift, side_shift],
            "expert",
            place.expert_of(0, lanes - shift),
        )

    def core_spread(layer_shift, lane_shift, side_shift):
        view = piece(layer_shift, lane_shift, place.tensor_of(side_shift))
        return remote(
            view,
            view,
            core_sem.at[layer_shift, lane_shift, side_shift],
            core_land_sem.at[layer_shift, lane_shift, side_shift],
            "tensor",
            place.sibling,
        )

    def first_hop(layer_shift, landed):
        if landed:
            await_bytes(piece(layer_shift, 0, mine), layer_land_sem.at[layer_shift])
        for shift in range(1, sides):
            side_spread(layer_shift, shift).start()
        for shift in range(1, lanes):
            lane_spread(layer_shift, shift).start()
        core_spread(layer_shift, 0, 0).start()

    def second_hop(layer_shift):
        for shift in range(1, sides):
            await_bytes(
                piece(layer_shift, 0, place.tensor_of(shift)),
                side_land_sem.at[layer_shift, shift],
            )
            core_spread(layer_shift, 0, shift).start()
            for lane_shift in range(1, lanes):
                lane_half_spread(layer_shift, lane_shift, shift).start()
        for lane_shift in range(1, lanes):
            await_bytes(
                piece(layer_shift, lane_shift, mine), lane_land_sem.at[layer_shift, lane_shift]
            )
            for shift in range(1, sides):
                side_half_spread(layer_shift, lane_shift, shift).start()
            core_spread(layer_shift, lane_shift, 0).start()

    def third_hop(layer_shift):
        for lane_shift in range(1, lanes):
            for shift in range(1, sides):
                tensor = place.tensor_of(shift)
                await_bytes(
                    piece(layer_shift, lane_shift, tensor, 0),
                    side_half_land_sem.at[layer_shift, lane_shift, shift],
                )
                await_bytes(
                    piece(layer_shift, lane_shift, tensor, 1),
                    lane_half_land_sem.at[layer_shift, lane_shift, shift],
                )
                core_spread(layer_shift, lane_shift, shift).start()

    def await_sibling(step):
        layer_shift = step // lanes
        lane_shift = step % lanes
        for shift in range(sides):
            tensor = place.side_of(shift) * 2 + (1 - core)
            await_bytes(
                piece(layer_shift, lane_shift, tensor),
                core_land_sem.at[layer_shift, lane_shift, shift],
            )

    for copy in first_copies:
        copy.wait()
    pl.semaphore_wait(barrier, count)
    for copy in weight_copies:
        copy.start()
    attention = sum_over_tensor(
        place,
        terms_buf,
        core_land,
        side_send,
        side_land,
        (sum_core_sem, sum_core_land_sem, sum_side_sem, sum_side_land_sem),
    )
    residual = inputs_buf[...].astype(jnp.float32) + attention
    residual_ref[...] = residual
    factor = lax.rsqrt(jnp.mean(residual * residual, axis=1, keepdims=True) + EPS)
    part_buf[...] = (residual * factor * gain_ref[...]).astype(jnp.bfloat16)

    own_copy = pltpu.make_async_copy(part_buf, piece(0, 0, mine), first_sem.at[2])
    own_copy.start()
    for shift in range(1, layers):
        layer_spread(shift).start()
    own_copy.wait()
    first_hop(0, False)
    second_hop(0)
    await_sibling(0)
    load_copy(0).start()
    for copy in weight_copies:
        copy.wait()

    def step_body(step, carry):
        slot = step % 2
        layer_shift = step // lanes
        lane_shift = step % lanes
        load_copy(step).wait()

        @pl.when(step > 1)
        def _():
            for copy in store_copies(step - 2):
                copy.wait()

        logits_buf[slot] = dot_plain(rows_buf[slot], router_w[...])

        def hidden_rows(block, inner):
            rows = pl.ds(pl.multiple_of(block * row_block, row_block), row_block)
            here = rows_buf[slot, rows, :]
            for index, weight in ((0, gate_w), (1, up_w)):
                acts_buf[slot, index, rows, :] = dot_rows(here, weight[...]).astype(jnp.bfloat16)
            return inner

        lax.fori_loop(0, length // row_block, hidden_rows, 0)

        @pl.when(lane_shift == 0)
        def _():
            third_hop(layer_shift)

            @pl.when(layer_shift + 1 < layers)
            def _():
                first_hop(layer_shift + 1, True)

        @pl.when((lane_shift == lanes - 1) & (layer_shift + 1 < layers))
        def _():
            second_hop(layer_shift + 1)

        def shared_rows(block, inner):
            rows = pl.ds(pl.multiple_of(block * row_block, row_block), row_block)
            here = rows_buf[slot, rows, :]
            for index, weight in ((2, shared_gate_w), (3, shared_up_w)):
                acts_buf[slot, index, rows, :] = dot_rows(here, weight[...]).astype(jnp.bfloat16)
            return inner

        lax.fori_loop(0, length // row_block, shared_rows, 0)

        @pl.when(step + 1 < groups)
        def _():
            await_sibling(step + 1)
            load_copy(step + 1).start()

        for copy in store_copies(step):
            copy.start()
        return carry

    lax.fori_loop(0, groups, step_body, 0)

    for step in range(max(groups - 2, 0), groups):
        for copy in store_copies(step):
            copy.wait()
    for shift in range(1, layers):
        layer_spread(shift).wait_send()
    for layer_shift in range(layers):
        for shift in range(1, sides):
            side_spread(layer_shift, shift).wait_send()
        for lane_shift in range(lanes):
            if lane_shift > 0:
                lane_spread(layer_shift, lane_shift).wait_send()
                for shift in range(1, sides):
                    side_half_spread(layer_shift, lane_shift, shift).wait_send()
                    lane_half_spread(layer_shift, lane_shift, shift).wait_send()
            for shift in range(sides):
                core_spread(layer_shift, lane_shift, shift).wait_send()


def backward_kernel(
    cotangent_ref,
    acts_ref,
    logits_ref,
    gate_ref,
    up_ref,
    down_ref,
    shared_gate_ref,
    shared_up_ref,
    shared_down_ref,
    router_ref,
    residual_ref,
    gain_ref,
    expert_hidden_ref,
    expert_dpre_ref,
    expert_dlin_ref,
    shared_hidden_ref,
    shared_dpre_ref,
    shared_dlin_ref,
    spread_ref,
    result_ref,
    grad_residual_ref,
    logit_ref,
    gain_grad_ref,
    gate_w,
    up_w,
    down_w,
    shared_gate_w,
    shared_up_w,
    shared_down_w,
    router_w,
    cotangent_buf,
    acts_buf,
    logits_buf,
    codes_buf,
    units_buf,
    gate_grad_buf,
    sum_buf,
    core_land,
    side_land,
    lane_send,
    lane_land,
    block_land,
    block_send,
    block_side_land,
    layer_send,
    layer_land,
    cotangent_part,
    code_part,
    gates_part,
    part_buf,
    weight_sem,
    load_sem,
    store_sem,
    part_sem,
    core_sem,
    core_land_sem,
    side_sem,
    side_land_sem,
    lane_sem,
    lane_land_sem,
    block_sem,
    block_land_sem,
    block_side_sem,
    block_side_land_sem,
    layer_sem,
    layer_land_sem,
    own_sem,
    spread_side_sem,
    spread_core_sem,
    arrive_sem,
    *,
    groups,
    tensors,
    local_experts,
):
    place = Place(groups, tensors)
    sides, layers, lanes = place.sides, place.layers, place.lanes
    me, mine, core, side = place.me, place.mine, place.core, place.side
    length = cotangent_buf.shape[0]
    width = cotangent_buf.shape[1]
    part_rows = length // tensors
    hidden = gate_w.shape[0]
    own_width = hidden // local_experts
    row_block = min(256, length)
    column_block = min(512, width)
    first = pl.ds(0, width)
    second = pl.ds(width, width + LANES)
    marks = pl.ds(width, LANES)

    pairs = (
        (down_ref, down_w),
        (shared_down_ref, shared_down_w),
        (gate_ref, gate_w),
        (up_ref, up_w),
        (shared_gate_ref, shared_gate_w),
        (shared_up_ref, shared_up_w),
        (router_ref, router_w),
    )
    weight_copies = [
        pltpu.make_async_copy(source, target, weight_sem.at[index])
        for index, (source, target) in enumerate(pairs)
    ]

    def shifts_of(step):
        return (step // lanes + 1) % layers, lanes - 1 - step % lanes

    def sequence_of(step):
        layer_shift, lane_shift = shifts_of(step)
        return place.expert_of(layer_shift, lane_shift)

    def load_copies(step):
        sequence = sequence_of(step)
        return (
            pltpu.make_async_copy(
                cotangent_ref.at[sequence, :, first], cotangent_buf, load_sem.at[0]
            ),
            pltpu.make_async_copy(acts_ref.at[:, sequence], acts_buf, load_sem.at[1]),
            pltpu.make_async_copy(logits_ref.at[sequence], logits_buf, load_sem.at[2]),
            pltpu.make_async_copy(cotangent_ref.at[sequence, :, marks], codes_buf, load_sem.at[3]),
        )

    unit_refs = (
        expert_hidden_ref,
        expert_dpre_ref,
        expert_dlin_ref,
        shared_hidden_ref,
        shared_dpre_ref,
        shared_dlin_ref,
    )

    def store_copies(step):
        sequence = sequence_of(step)
        return [
            pltpu.make_async_copy(units_buf.at[index], ref.at[sequence], store_sem.at[index])
            for index, ref in enumerate(unit_refs)
        ]

    part_slice = pl.ds(pl.multiple_of(mine * part_rows, part_rows), part_rows)
    part_copies = (
        pltpu.make_async_copy(
            cotangent_ref.at[me, part_slice, first], cotangent_part, part_sem.at[0]
        ),
        pltpu.make_async_copy(cotangent_ref.at[me, part_slice, marks], code_part, part_sem.at[1]),
        pltpu.make_async_copy(logits_ref.at[me, part_slice, :], gates_part, part_sem.at[2]),
    )
    for copy in load_copies(0):
        copy.start()
    for copy in weight_copies:
        copy.start()
    for copy in part_copies:
        copy.start()
    barrier, count = place.greet(True)

    def core_send(step):
        slot = step % 2
        return remote(
            sum_buf.at[slot, :, 1 - core],
            core_land.at[slot],
            core_sem.at[slot],
            core_land_sem.at[slot],
            "tensor",
            place.sibling,
        )

    def side_copy(step, shift):
        slot = step % 2
        return remote(
            sum_buf.at[slot, place.side_of(shift), core, :, first],
            side_land.at[slot, shift - 1],
            side_sem.at[slot, shift - 1],
            side_land_sem.at[slot, shift - 1],
            "tensor",
            place.tensor_of(shift),
        )

    def lane_copy(turn, lane_shift):
        slot = turn % 2
        return remote(
            lane_send.at[slot, lane_shift - 1],
            lane_land.at[slot, lane_shift - 1],
            lane_sem.at[slot, lane_shift - 1],
            lane_land_sem.at[slot, lane_shift - 1],
            "expert",
            place.expert_of(0, lane_shift),
        )

    def block_copy(step, lane_shift):
        slot = step % 2
        turn_slot = (step // lanes) % 2
        return remote(
            sum_buf.at[slot, :, core, :, second],
            block_land.at[turn_slot, lane_shift - 1],
            block_sem.at[slot],
            block_land_sem.at[turn_slot, lane_shift - 1],
            "expert",
            place.expert_of(0, lane_shift),
        )

    def block_side_copy(turn, shift):
        slot = turn % 2
        return remote(
            block_send.at[slot, shift - 1],
            block_side_land.at[slot, shift - 1],
            block_side_sem.at[slot, shift - 1],
            block_side_land_sem.at[slot, shift - 1],
            "tensor",
            place.tensor_of(shift),
        )

    def layer_copy(turn):
        slot = turn % 2
        return remote(
            layer_send.at[slot],
            layer_land.at[turn],
            layer_sem.at[slot],
            layer_land_sem.at[turn],
            "expert",
            place.expert_of((turn + 1) % layers, 0),
        )

    def per_lane(lane_shift, act):
        for value in range(1, lanes):

            @pl.when(lane_shift == value)
            def _():
                act(value)

    def combine_cores(step):
        slot = step % 2
        _, lane_shift = shifts_of(step)
        copy = core_send(step)
        copy.wait_recv()
        copy.wait_send()
        for shift in range(sides):
            other = place.side_of(shift)
            sum_buf[slot, other, core] = (
                sum_buf[slot, other, core].astype(jnp.float32)
                + core_land[slot, other].astype(jnp.float32)
            ).astype(jnp.bfloat16)
            if shift > 0:
                side_copy(step, shift).start()
        per_lane(lane_shift, lambda value: block_copy(step, value).start())

    def combine_sides(step):
        slot = step % 2
        turn = step // lanes
        _, lane_shift = shifts_of(step)
        total = sum_buf[slot, side, core, :, first].astype(jnp.float32)
        for shift in range(1, sides):
            side_copy(step, shift).wait_recv()
            side_copy(step, shift).wait_send()
            total = total + side_land[slot, shift - 1].astype(jnp.float32)
        total = total.astype(jnp.bfloat16)

        def pass_on(value):
            block_copy(step, value).wait_send()

            @pl.when(turn >= 2)
            def _():
                lane_copy(turn - 2, value).wait_send()

            lane_send[turn % 2, value - 1] = total
            lane_copy(turn, value).start()

        per_lane(lane_shift, pass_on)

        @pl.when(lane_shift == 0)
        def _():
            turn_slot = turn % 2

            @pl.when(turn >= 2)
            def _():
                layer_copy(turn - 2).wait_send()
                for shift in range(1, sides):
                    block_side_copy(turn - 2, shift).wait_send()

            layer_send[turn_slot, :, first] = total
            for value in range(1, lanes):
                block_copy(step, value).wait_recv()
            for shift in range(sides):
                other = place.side_of(shift)
                block = sum_buf[slot, other, core, :, second].astype(jnp.float32)
                for value in range(1, lanes):
                    block = block + block_land[turn_slot, value - 1, other].astype(jnp.float32)
                block = block.astype(jnp.bfloat16)
                if shift == 0:
                    layer_send[turn_slot, :, second] = block
                else:
                    block_send[turn_slot, shift - 1] = block
                    block_side_copy(turn, shift).start()

    def turn_total(turn):
        slot = turn % 2
        branch = layer_send[slot, :, first].astype(jnp.float32)
        for value in range(1, lanes):
            lane_copy(turn, value).wait_recv()
            branch = branch + lane_land[slot, value - 1].astype(jnp.float32)
        block = layer_send[slot, :, second].astype(jnp.float32)
        for shift in range(1, sides):
            block_side_copy(turn, shift).wait_recv()
            block = block + block_side_land[slot, shift - 1].astype(jnp.float32)
        return branch, block

    def combine_lanes(step):
        turn = step // lanes
        _, lane_shift = shifts_of(step)

        @pl.when(lane_shift == 0)
        def _():
            slot = turn % 2
            branch, block = turn_total(turn)
            layer_send[slot, :, first] = branch.astype(jnp.bfloat16)
            layer_send[slot, :, second] = block.astype(jnp.bfloat16)
            layer_copy(turn).start()

    for copy in weight_copies[:2]:
        copy.wait()
    for copy in part_copies:
        copy.wait()
    pl.semaphore_wait(barrier, count)

    def softmax_named(logits, code):
        named = code > 0.5
        highest = jnp.max(jnp.where(named, logits, -jnp.inf), axis=1, keepdims=True)
        raised = jnp.where(named, jnp.exp(logits - highest), 0.0)
        return raised / jnp.sum(raised, axis=1, keepdims=True)

    def services(step):
        @pl.when((step >= 3) & (step < groups + 2))
        def _():
            combine_lanes(step - 3)

        @pl.when((step >= 2) & (step < groups + 2))
        def _():
            combine_sides(step - 2)

        @pl.when((step >= 1) & (step < groups + 1))
        def _():
            combine_cores(step - 1)

    def step_body(step, carry):
        slot = step % 2
        running = step < groups

        @pl.when(running)
        def _():
            for copy in load_copies(step):
                copy.wait()

            @pl.when(step > 0)
            def _():
                for copy in store_copies(step - 1):
                    copy.wait()

            def hidden_rows(block, inner):
                rows = pl.ds(pl.multiple_of(block * row_block, row_block), row_block)
                back = cotangent_buf[rows, :]
                dhid = dot_rows(back, down_w[...])
                code = codes_buf[rows, :].astype(jnp.float32)
                lane = lax.broadcasted_iota(jnp.int32, code.shape, 1)
                gates = softmax_named(logits_buf[rows, :], code)
                gates = jnp.where(code > 1.5, gates, 0.0)
                pre = acts_buf[0, rows, :].astype(jnp.float32)
                lin = acts_buf[1, rows, :].astype(jnp.float32)
                unit = lax.broadcasted_iota(jnp.int32, pre.shape, 1)
                gate = None
                for member in range(local_experts):
                    chosen = jnp.sum(
                        jnp.where(lane == me * local_experts + member, gates, 0.0),
                        axis=1,
                        keepdims=True,
                    )
                    gate = (
                        jnp.broadcast_to(chosen, pre.shape)
                        if gate is None
                        else jnp.where(unit >= member * own_width, chosen, gate)
                    )
                sigmoid = jax.nn.sigmoid(pre)
                active = pre * sigmoid
                hid = active * lin
                product = hid * dhid
                units_buf[0, rows, :] = (hid * gate).astype(jnp.bfloat16)
                dhid = dhid * gate
                units_buf[1, rows, :] = (dhid * lin * (sigmoid + active * (1.0 - sigmoid))).astype(
                    jnp.bfloat16
                )
                units_buf[2, rows, :] = (dhid * active).astype(jnp.bfloat16)
                gate_grad = jnp.zeros(code.shape, jnp.float32)
                for member in range(local_experts):
                    inside = (unit >= member * own_width) & (unit < (member + 1) * own_width)
                    gate_grad = jnp.where(
                        lane == me * local_experts + member,
                        jnp.sum(jnp.where(inside, product, 0.0), axis=1, keepdims=True),
                        gate_grad,
                    )
                gate_grad_buf[rows, :] = gate_grad
                return inner

            lax.fori_loop(0, length // row_block, hidden_rows, 0)

            def shared_rows(block, inner):
                rows = pl.ds(pl.multiple_of(block * row_block, row_block), row_block)
                dhid = dot_rows(cotangent_buf[rows, :], shared_down_w[...])
                pre = acts_buf[2, rows, :].astype(jnp.float32)
                lin = acts_buf[3, rows, :].astype(jnp.float32)
                sigmoid = jax.nn.sigmoid(pre)
                active = pre * sigmoid
                units_buf[3, rows, :] = (active * lin).astype(jnp.bfloat16)
                units_buf[4, rows, :] = (dhid * lin * (sigmoid + active * (1.0 - sigmoid))).astype(
                    jnp.bfloat16
                )
                units_buf[5, rows, :] = (dhid * active).astype(jnp.bfloat16)
                return inner

            lax.fori_loop(0, length // row_block, shared_rows, 0)

            @pl.when(step + 1 < groups)
            def _():
                for copy in load_copies(step + 1):
                    copy.start()

            @pl.when(step == 0)
            def _():
                for copy in weight_copies[2:]:
                    copy.wait()

        services(step)

        @pl.when(running)
        def _():
            def mix_columns(block, inner):
                start = pl.multiple_of(block * column_block, column_block)
                columns = pl.ds(start, column_block)
                moved = pl.ds(pl.multiple_of(width + start, column_block), column_block)
                sum_buf[slot, :, :, :, columns] = (
                    dot_plain(units_buf[0], down_w[:, columns])
                    .astype(jnp.bfloat16)
                    .reshape(sides, 2, part_rows, column_block)
                )
                total = dot_plain(units_buf[1], gate_w[:, columns]) + dot_plain(
                    units_buf[2], up_w[:, columns]
                )
                sum_buf[slot, :, :, :, moved] = total.astype(jnp.bfloat16).reshape(
                    sides, 2, part_rows, column_block
                )
                return inner

            lax.fori_loop(0, width // column_block, mix_columns, 0)

            @pl.when(step == groups - 1)
            def _():
                def mix_shared(block, inner):
                    start = pl.multiple_of(block * column_block, column_block)
                    columns = pl.ds(start, column_block)
                    moved = pl.ds(pl.multiple_of(width + start, column_block), column_block)
                    for target, total in (
                        (columns, dot_plain(units_buf[3], shared_down_w[:, columns])),
                        (
                            moved,
                            dot_plain(units_buf[4], shared_gate_w[:, columns])
                            + dot_plain(units_buf[5], shared_up_w[:, columns]),
                        ),
                    ):
                        sum_buf[slot, :, :, :, target] = (
                            sum_buf[slot, :, :, :, target].astype(jnp.float32)
                            + total.reshape(sides, 2, part_rows, column_block)
                        ).astype(jnp.bfloat16)
                    return inner

                lax.fori_loop(0, width // column_block, mix_shared, 0)

            sum_buf[slot, :, :, :, pl.ds(2 * width, LANES)] = (
                gate_grad_buf[...].astype(jnp.bfloat16).reshape(sides, 2, part_rows, LANES)
            )
            core_send(step).start()
            for copy in store_copies(step):
                copy.start()

        return carry

    lax.fori_loop(0, groups + 2, step_body, 0)

    last = layers - 1
    last_slot = last % 2
    for value in range(1, lanes):
        lane_copy(last, value).wait_recv()
    for shift in range(1, sides):
        block_side_copy(last, shift).wait_recv()
    for turn in range(last):
        layer_copy(turn).wait_recv()
    gain_grad_ref[...] = jnp.zeros_like(gain_grad_ref)
    few_rows = min(32, part_rows)

    def finish_rows(index, inner):
        rows = pl.ds(pl.multiple_of(index * few_rows, few_rows), few_rows)
        branch = layer_send[last_slot, rows, first].astype(jnp.float32)
        for value in range(1, lanes):
            branch = branch + lane_land[last_slot, value - 1, rows, :].astype(jnp.float32)
        block = layer_send[last_slot, rows, second].astype(jnp.float32)
        for shift in range(1, sides):
            block = block + block_side_land[last_slot, shift - 1, rows, :].astype(jnp.float32)
        for turn in range(last):
            branch = branch + layer_land[turn, rows, first].astype(jnp.float32)
            block = block + layer_land[turn, rows, second].astype(jnp.float32)
        residual = residual_ref[rows, :]
        result_ref[rows, :] = (residual + branch).astype(jnp.bfloat16)

        code = code_part[rows, :].astype(jnp.float32)
        gates = softmax_named(gates_part[rows, :], code)
        gate_grad = jnp.where(code > 1.5, block[:, width:], 0.0)
        logit = (
            gates * (gate_grad - jnp.sum(gates * gate_grad, axis=1, keepdims=True))
        ).astype(jnp.bfloat16)
        logit_ref[rows, :] = logit
        upstream = block[:, :width] + dot_rows(logit, router_w[...])
        factor = lax.rsqrt(jnp.mean(residual * residual, axis=1, keepdims=True) + EPS)
        unit_rows = residual * factor
        scaled = upstream * gain_ref[...]
        inner_mean = jnp.mean(scaled * unit_rows, axis=1, keepdims=True)
        gain_grad_ref[...] += jnp.sum(upstream * unit_rows, axis=0, keepdims=True)
        grad_residual = cotangent_part[rows, :].astype(jnp.float32) + factor * (
            scaled - unit_rows * inner_mean
        )
        grad_residual_ref[rows, :] = grad_residual
        part_buf[rows, :] = grad_residual.astype(jnp.bfloat16)
        return inner

    lax.fori_loop(0, part_rows // few_rows, finish_rows, 0)
    spread_over_tensor(
        place, part_buf, spread_ref, (own_sem, spread_side_sem, spread_core_sem, arrive_sem)
    )

    for copy in store_copies(groups - 1):
        copy.wait()
    for turn in range(max(layers - 2, 0), layers):
        for value in range(1, lanes):
            lane_copy(turn, value).wait_send()
        for shift in range(1, sides):
            block_side_copy(turn, shift).wait_send()
    layer_copy(last - 1).wait_send()


ANYWHERE = pl.BlockSpec(memory_space=pl.ANY)
IN_VMEM = pl.BlockSpec(memory_space=pltpu.VMEM)


def run_forward(attention, inputs, gain, weights, router_padded):
    groups = lax.axis_size("expert")
    tensors = lax.axis_size("tensor")
    sides = tensors // 2
    layers = min(LAYERS, groups)
    lanes = groups // layers
    length, width = inputs.shape
    part_rows = length // tensors
    hidden = weights[0].shape[0]
    bf16 = jnp.bfloat16
    f32 = jnp.float32
    dma = pltpu.SemaphoreType.DMA
    block = pltpu.VMEM((hidden, width), bf16)
    return pl.pallas_call(
        functools.partial(forward_kernel, groups=groups, tensors=tensors),
        out_shape=(
            jax.ShapeDtypeStruct((groups, length, width), bf16),
            jax.ShapeDtypeStruct((4, groups, length, hidden), bf16),
            jax.ShapeDtypeStruct((groups, length, LANES), f32),
            jax.ShapeDtypeStruct((part_rows, width), f32),
        ),
        in_specs=[ANYWHERE, ANYWHERE, IN_VMEM] + [ANYWHERE] * 5,
        out_specs=(ANYWHERE,) * 3 + (IN_VMEM,),
        scratch_shapes=[block] * 4
        + [
            pltpu.VMEM((width, LANES), bf16),
            pltpu.VMEM((sides, 2, part_rows, width), bf16),
            pltpu.VMEM((sides, part_rows, width), bf16),
            pltpu.VMEM((sides - 1, part_rows, width), bf16),
            pltpu.VMEM((sides - 1, part_rows, width), bf16),
            pltpu.VMEM((part_rows, width), bf16),
            pltpu.VMEM((part_rows, width), bf16),
            pltpu.VMEM((2, length, width), bf16),
            pltpu.VMEM((2, length, LANES), f32),
            pltpu.VMEM((2, 4, length, hidden), bf16),
            dma((5,)),
            dma((3,)),
            dma((2,)),
            dma((2, 2)),
            dma(()),
            dma(()),
            dma((sides - 1,)),
            dma((sides - 1,)),
            dma((layers,)),
            dma((layers,)),
            dma((layers, lanes)),
            dma((layers, lanes)),
            dma((layers, sides)),
            dma((layers, sides)),
            dma((layers, lanes, sides)),
            dma((layers, lanes, sides)),
            dma((layers, lanes, sides)),
            dma((layers, lanes, sides)),
            dma((layers, lanes, sides)),
            dma((layers, lanes, sides)),
        ],
        compiler_params=pltpu.CompilerParams(
            collective_id=1, has_side_effects=True, vmem_limit_bytes=60 * 1024 * 1024
        ),
        cost_estimate=pl.CostEstimate(
            flops=8 * groups * length * width * hidden,
            bytes_accessed=100_000_000,
            transcendentals=0,
        ),
        name="experts_forward",
    )(
        attention.reshape(sides, 2, part_rows, width),
        inputs,
        gain.reshape(1, width),
        *weights,
        router_padded,
    )


def run_backward(
    cotangent_all, acts, logits, weights, router_padded, residual, gain, local_experts
):
    groups = lax.axis_size("expert")
    tensors = lax.axis_size("tensor")
    sides = tensors // 2
    layers = min(LAYERS, groups)
    lanes = groups // layers
    part_rows, width = residual.shape
    length = part_rows * tensors
    hidden = weights[0].shape[0]
    second = width + LANES
    packed = width + second
    bf16 = jnp.bfloat16
    f32 = jnp.float32
    dma = pltpu.SemaphoreType.DMA
    block = pltpu.VMEM((hidden, width), bf16)
    units = jax.ShapeDtypeStruct((groups, length, hidden), bf16)
    return pl.pallas_call(
        functools.partial(
            backward_kernel, groups=groups, tensors=tensors, local_experts=local_experts
        ),
        out_shape=(units,) * 6
        + (
            jax.ShapeDtypeStruct((tensors, part_rows, width), bf16),
            jax.ShapeDtypeStruct((part_rows, width), bf16),
            jax.ShapeDtypeStruct((part_rows, width), f32),
            jax.ShapeDtypeStruct((part_rows, LANES), bf16),
            jax.ShapeDtypeStruct((1, width), f32),
        ),
        in_specs=[ANYWHERE] * 10 + [IN_VMEM] * 2,
        out_specs=(ANYWHERE,) * 7 + (IN_VMEM,) * 4,
        scratch_shapes=[block] * 6
        + [
            pltpu.VMEM((width, LANES), bf16),
            pltpu.VMEM((length, width), bf16),
            pltpu.VMEM((4, length, hidden), bf16),
            pltpu.VMEM((length, LANES), f32),
            pltpu.VMEM((length, LANES), bf16),
            pltpu.VMEM((6, length, hidden), bf16),
            pltpu.VMEM((length, LANES), f32),
            pltpu.VMEM((2, sides, 2, part_rows, packed), bf16),
            pltpu.VMEM((2, sides, part_rows, packed), bf16),
            pltpu.VMEM((2, sides - 1, part_rows, width), bf16),
            pltpu.VMEM((2, lanes - 1, part_rows, width), bf16),
            pltpu.VMEM((2, lanes - 1, part_rows, width), bf16),
            pltpu.VMEM((2, lanes - 1, sides, part_rows, second), bf16),
            pltpu.VMEM((2, sides - 1, part_rows, second), bf16),
            pltpu.VMEM((2, sides - 1, part_rows, second), bf16),
            pltpu.VMEM((2, part_rows, packed), bf16),
            pltpu.VMEM((layers - 1, part_rows, packed), bf16),
            pltpu.VMEM((part_rows, width), bf16),
            pltpu.VMEM((part_rows, LANES), bf16),
            pltpu.VMEM((part_rows, LANES), f32),
            pltpu.VMEM((part_rows, width), bf16),
            dma((7,)),
            dma((4,)),
            dma((6,)),
            dma((3,)),
            dma((2,)),
            dma((2,)),
            dma((2, sides - 1)),
            dma((2, sides - 1)),
            dma((2, lanes - 1)),
            dma((2, lanes - 1)),
            dma((2,)),
            dma((2, lanes - 1)),
            dma((2, sides - 1)),
            dma((2, sides - 1)),
            dma((2,)),
            dma((layers - 1,)),
            dma(()),
            dma((sides,)),
            dma((sides,)),
            dma((tensors,)),
        ],
        compiler_params=pltpu.CompilerParams(
            collective_id=2, has_side_effects=True, vmem_limit_bytes=60 * 1024 * 1024
        ),
        cost_estimate=pl.CostEstimate(
            flops=10 * groups * length * width * hidden,
            bytes_accessed=100_000_000,
            transcendentals=0,
        ),
        name="experts_backward",
    )(
        cotangent_all.reshape(groups, length, width + LANES),
        acts,
        logits,
        *weights,
        router_padded,
        residual,
        gain.reshape(1, width),
    )


def weight_kernel(
    query_ref,
    latent_ref,
    out_ref,
    rest_ref,
    first_ref,
    residual_ref,
    inputs_ref,
    gain_ref,
    units_0,
    units_1,
    units_2,
    units_3,
    units_4,
    units_5,
    rows_ref,
    cotangent_ref,
    query_sum,
    latent_sum,
    out_sum,
    rest_spread,
    first_spread,
    grad_0,
    grad_1,
    grad_2,
    grad_3,
    grad_4,
    grad_5,
    query_own,
    latent_own,
    out_own,
    rest_own,
    query_lane,
    latent_lane,
    out_lane,
    rest_lane,
    query_layer,
    latent_layer,
    out_layer,
    rest_layer,
    rest_part,
    rest_block,
    first_core_land,
    first_send,
    first_land,
    first_part,
    sum_core_land,
    sum_send,
    sum_land,
    units_buf,
    turned_buf,
    rows_buf,
    grad_buf,
    own_sem,
    lane_sem,
    lane_land_sem,
    layer_sem,
    layer_land_sem,
    units_sem,
    rows_sem,
    grad_sem,
    spread_own_sem,
    spread_side_sem,
    spread_core_sem,
    arrive_sem,
    tensor_core_sem,
    tensor_core_land_sem,
    tensor_side_sem,
    tensor_side_land_sem,
    first_own_sem,
    first_side_sem,
    first_core_sem,
    first_arrive_sem,
    *,
    groups,
    tensors,
):
    place = Place(groups, tensors)
    layers, lanes = place.layers, place.lanes
    sides = place.sides
    columns = rest_part.shape[1]
    tokens = units_buf.shape[1]
    width = rows_ref.shape[1]
    column_block = rows_buf.shape[2]
    barrier, count = place.greet(True)

    sums = (query_sum, latent_sum, out_sum, None)
    owns = (query_own, latent_own, out_own, rest_own)
    lane_lands = (query_lane, latent_lane, out_lane, rest_lane)
    layer_lands = (query_layer, latent_layer, out_layer, rest_layer)

    def share(index, expert):
        if index == 0:
            return query_ref.at[expert]
        if index == 1:
            return latent_ref.at[expert]
        part = pl.ds(pl.multiple_of(expert * columns, columns), columns)
        return (out_ref if index == 2 else rest_block).at[:, part]

    def own_copies(turn, indices=range(4)):
        return [
            pltpu.make_async_copy(
                share(index, place.expert_of((turn + 1) % layers, 0)),
                owns[index].at[turn],
                own_sem.at[turn, index],
            )
            for index in indices
        ]

    def lane_copies(turn, indices=range(4)):
        return [
            remote(
                share(index, place.expert_of((turn + 1) % layers, shift)),
                lane_lands[index].at[turn, shift - 1],
                lane_sem.at[turn, shift - 1, index],
                lane_land_sem.at[turn, shift - 1, index],
                "expert",
                place.expert_of(0, shift),
            )
            for shift in range(1, lanes)
            for index in indices
        ]

    def layer_copies(turn, indices=range(4)):
        return [
            remote(
                owns[index].at[turn],
                layer_lands[index].at[turn],
                layer_sem.at[turn, index],
                layer_land_sem.at[turn, index],
                "expert",
                place.expert_of((turn + 1) % layers, 0),
            )
            for index in indices
        ]

    def lane_total(turn, index):
        total = owns[index][turn].astype(jnp.float32)
        for shift in range(1, lanes):
            total = total + lane_lands[index][turn, shift - 1].astype(jnp.float32)
        return total

    def combine(turn, indices=range(4)):
        for copy in own_copies(turn, indices):
            copy.wait()
        for copy in lane_copies(turn, indices):
            copy.wait_recv()
        if turn < layers - 1:
            for index, copy in zip(indices, layer_copies(turn, indices)):
                owns[index][turn] = lane_total(turn, index).astype(jnp.bfloat16)
                copy.start()

    units = (units_0, units_1, units_2, units_3, units_4, units_5)
    grads = (grad_0, grad_1, grad_2, grad_3, grad_4, grad_5)
    sources = (rows_ref, rows_ref, cotangent_ref, rows_ref, rows_ref, cotangent_ref)

    def units_copy(index):
        return pltpu.make_async_copy(units[index], units_buf.at[index % 2], units_sem.at[index % 2])

    def rows_copy(index, block, slot):
        if index < 3:
            start = pl.multiple_of(block * column_block, column_block)
            part = pl.ds(start, column_block)
            target = rows_buf.at[slot]
        else:
            part = pl.ds(pl.multiple_of(place.me * columns, columns), columns)
            target = rows_buf.at[slot, :, pl.ds(0, columns)]
        return pltpu.make_async_copy(sources[index].at[:, part], target, rows_sem.at[slot])

    def grad_copy(index, block, slot):
        if index < 3:
            start = pl.multiple_of(block * column_block, column_block)
            return pltpu.make_async_copy(
                grad_buf.at[slot], grads[index].at[:, pl.ds(start, column_block)], grad_sem.at[slot]
            )
        return pltpu.make_async_copy(
            grad_buf.at[slot, :, pl.ds(0, columns)], grads[index], grad_sem.at[slot]
        )

    turn_rows = min(512, tokens)

    def turn_units(index):
        units_copy(index).wait()

        def body(block, inner):
            rows = pl.ds(pl.multiple_of(block * turn_rows, turn_rows), turn_rows)
            turned_buf[:, rows] = units_buf[index % 2, rows, :].T
            return inner

        lax.fori_loop(0, tokens // turn_rows, body, 0)
        if index + 2 < 6:
            units_copy(index + 2).start()

    blocks = width // column_block

    def routed(index):
        rows_copy(index, 0, 0).start()
        turn_units(index)

        def body(block, inner):
            slot = block % 2

            @pl.when(block + 1 < blocks)
            def _():
                rows_copy(index, block + 1, 1 - slot).start()

            rows_copy(index, block, slot).wait()

            @pl.when(block >= 2)
            def _():
                grad_copy(index, block - 2, slot).wait()

            grad_buf[slot] = dot_plain(turned_buf[...], rows_buf[slot])
            grad_copy(index, block, slot).start()
            return inner

        lax.fori_loop(0, blocks, body, 0)
        for block in range(max(blocks - 2, 0), blocks):
            grad_copy(index, block, block % 2).wait()

    def shared(index):
        slot = index % 2
        rows_copy(index, 0, slot).start()
        turn_units(index)
        rows_copy(index, 0, slot).wait()
        part = pl.ds(0, columns)
        grad_buf[slot, :, part] = dot_plain(turned_buf[...], rows_buf[slot, :, part])
        grad_copy(index, 0, slot).start()
        grad_copy(index, 0, slot).wait()

    tensor_sums = (
        (first_ref, first_core_land, first_send, first_land),
        (rest_ref, sum_core_land, sum_send, sum_land),
    )

    def core_exchange(which):
        source, land, _, _ = tensor_sums[which]
        return remote(
            source.at[:, 1 - place.core],
            land,
            tensor_core_sem.at[which],
            tensor_core_land_sem.at[which],
            "tensor",
            place.sibling,
        )

    def side_exchange(which, shift):
        _, _, send, land = tensor_sums[which]
        return remote(
            send.at[shift - 1],
            land.at[shift - 1],
            tensor_side_sem.at[which, shift - 1],
            tensor_side_land_sem.at[which, shift - 1],
            "tensor",
            place.tensor_of(shift),
        )

    def core_sum(which, other):
        source, land, _, _ = tensor_sums[which]
        return source[other, place.core].astype(jnp.float32) + land[other].astype(jnp.float32)

    def send_sides(which):
        core_exchange(which).wait_recv()
        for shift in range(1, sides):
            tensor_sums[which][2][shift - 1] = core_sum(which, place.side_of(shift)).astype(
                jnp.bfloat16
            )
            side_exchange(which, shift).start()

    def tensor_total(which):
        total = core_sum(which, place.side)
        for shift in range(1, sides):
            side_exchange(which, shift).wait_recv()
            total = total + tensor_sums[which][3][shift - 1].astype(jnp.float32)
        return total

    first_own = pltpu.make_async_copy(first_part, first_spread.at[place.mine], first_own_sem)

    def first_piece(tensor):
        return first_spread.at[tensor]

    def first_copy(view, sem, tensor, target):
        return remote(
            view, first_piece(tensor), sem, first_arrive_sem.at[tensor], "tensor", target
        )

    first_sends = [
        first_copy(first_part, first_side_sem.at[shift], place.mine, place.tensor_of(shift))
        for shift in range(1, sides)
    ]
    first_sends.append(
        first_copy(first_part, first_core_sem.at[0], place.mine, place.sibling)
    )
    first_forwards = [
        first_copy(
            first_piece(place.tensor_of(shift)),
            first_core_sem.at[shift],
            place.tensor_of(shift),
            place.sibling,
        )
        for shift in range(1, sides)
    ]

    def await_first(tensor):
        view = first_piece(tensor)
        pltpu.make_async_copy(view, view, first_arrive_sem.at[tensor]).wait()

    def finish_first():
        upstream = tensor_total(0)
        rows = inputs_ref[...].astype(jnp.float32)
        factor = lax.rsqrt(jnp.mean(rows * rows, axis=1, keepdims=True) + EPS)
        unit_rows = rows * factor
        scaled = upstream * gain_ref[...]
        inner_mean = jnp.mean(scaled * unit_rows, axis=1, keepdims=True)
        first_part[...] = (
            residual_ref[...] + factor * (scaled - unit_rows * inner_mean)
        ).astype(jnp.bfloat16)
        first_own.start()
        for copy in first_sends:
            copy.start()
        gain_grad = jnp.sum(upstream * unit_rows, axis=0, keepdims=True)
        summed_rows = rest_block.shape[0] - 16
        rest_block[pl.ds(0, summed_rows), :] = tensor_total(1).astype(jnp.bfloat16)
        row = lax.broadcasted_iota(jnp.int32, (16, width), 0)
        rest_block[pl.ds(summed_rows, 16), :] = jnp.where(row == 0, gain_grad, 0.0).astype(
            jnp.bfloat16
        )
        for turn in range(layers):
            for copy in lane_copies(turn, (3,)) + own_copies(turn, (3,)):
                copy.start()

    def forward_first():
        for shift in range(1, sides):
            await_first(place.tensor_of(shift))
            first_forwards[shift - 1].start()

    units_copy(0).start()
    units_copy(1).start()
    pl.semaphore_wait(barrier, count)
    for which in range(2):
        core_exchange(which).start()
    for turn in range(layers):
        for copy in lane_copies(turn, range(3)) + own_copies(turn, range(3)):
            copy.start()
    for which in range(2):
        send_sides(which)
    routed(0)
    combine(0, range(3))
    finish_first()
    routed(1)
    if layers > 2:
        combine(1, range(3))
    forward_first()
    routed(2)
    for turn in range(2, layers - 1):
        combine(turn, range(3))
    for turn in range(layers - 1):
        combine(turn, (3,))
    for index in range(3, 6):
        shared(index)
    combine(layers - 1)

    last = layers - 1
    for turn in range(last):
        for copy in layer_copies(turn):
            copy.wait_recv()
    for index in range(4):
        total = lane_total(last, index)
        for turn in range(last):
            total = total + layer_lands[index][turn].astype(jnp.float32)
        if index < 3:
            sums[index][...] = total
        else:
            rest_part[...] = total.astype(jnp.bfloat16)
    spread_over_tensor(
        place,
        rest_part,
        rest_spread,
        (spread_own_sem, spread_side_sem, spread_core_sem, arrive_sem),
    )
    for shift in range(sides):
        await_first(place.side_of(shift) * 2 + (1 - place.core))
    first_own.wait()
    for copy in first_sends + first_forwards:
        copy.wait_send()
    for which in range(2):
        core_exchange(which).wait_send()
        for shift in range(1, sides):
            side_exchange(which, shift).wait_send()
    for turn in range(layers):
        for copy in lane_copies(turn):
            copy.wait_send()
        if turn < last:
            for copy in layer_copies(turn):
                copy.wait_send()


def run_weights(
    query, latent, out, rest, first, residual, inputs_part, gain, units, rows, cotangent
):
    groups = lax.axis_size("expert")
    tensors = lax.axis_size("tensor")
    layers = min(LAYERS, groups)
    lanes = groups // layers
    sides = tensors // 2
    part_rows = residual.shape[0]
    rest_rows = rest.shape[0] // tensors
    tokens, width = rows.shape
    hidden = units[0].shape[1]
    columns = width // groups
    column_block = min(256, width)
    bf16 = jnp.bfloat16
    f32 = jnp.float32
    dma = pltpu.SemaphoreType.DMA
    query = query.reshape(groups, query.shape[0] // groups, query.shape[1])
    latent = latent.reshape(groups, latent.shape[0] // groups, latent.shape[1])
    shapes = (
        query.shape[1:],
        latent.shape[1:],
        (out.shape[0], columns),
        (rest_rows + 16, columns),
    )
    routed = jax.ShapeDtypeStruct((hidden, width), f32)
    shared = jax.ShapeDtypeStruct((hidden, columns), f32)
    return pl.pallas_call(
        functools.partial(weight_kernel, groups=groups, tensors=tensors),
        out_shape=tuple(jax.ShapeDtypeStruct(shape, f32) for shape in shapes[:3])
        + (jax.ShapeDtypeStruct((tensors,) + shapes[3], bf16),)
        + (jax.ShapeDtypeStruct((tensors, part_rows, width), bf16),)
        + (routed,) * 3
        + (shared,) * 3,
        in_specs=[ANYWHERE] * 3 + [IN_VMEM] * 5 + [ANYWHERE] * 8,
        out_specs=(IN_VMEM,) * 3 + (ANYWHERE,) * 8,
        scratch_shapes=[pltpu.VMEM((layers,) + shape, bf16) for shape in shapes]
        + [pltpu.VMEM((layers, lanes - 1) + shape, bf16) for shape in shapes]
        + [pltpu.VMEM((layers - 1,) + shape, bf16) for shape in shapes]
        + [
            pltpu.VMEM(shapes[3], bf16),
            pltpu.VMEM((rest_rows + 16, width), bf16),
            pltpu.VMEM((sides, part_rows, width), bf16),
            pltpu.VMEM((sides - 1, part_rows, width), bf16),
            pltpu.VMEM((sides - 1, part_rows, width), bf16),
            pltpu.VMEM((part_rows, width), bf16),
            pltpu.VMEM((sides, rest_rows, width), bf16),
            pltpu.VMEM((sides - 1, rest_rows, width), bf16),
            pltpu.VMEM((sides - 1, rest_rows, width), bf16),
            pltpu.VMEM((2, tokens, hidden), bf16),
            pltpu.VMEM((hidden, tokens), bf16),
            pltpu.VMEM((2, tokens, column_block), bf16),
            pltpu.VMEM((2, hidden, column_block), f32),
            dma((layers, 4)),
            dma((layers, lanes - 1, 4)),
            dma((layers, lanes - 1, 4)),
            dma((layers - 1, 4)),
            dma((layers - 1, 4)),
            dma((2,)),
            dma((2,)),
            dma((2,)),
            dma(()),
            dma((sides,)),
            dma((sides,)),
            dma((tensors,)),
            dma((2,)),
            dma((2,)),
            dma((2, sides - 1)),
            dma((2, sides - 1)),
            dma(()),
            dma((sides,)),
            dma((sides,)),
            dma((tensors,)),
        ],
        compiler_params=pltpu.CompilerParams(
            collective_id=4, has_side_effects=True, vmem_limit_bytes=60 * 1024 * 1024
        ),
        cost_estimate=pl.CostEstimate(
            flops=7 * tokens * width * hidden, bytes_accessed=100_000_000, transcendentals=0
        ),
        name="weights",
    )(
        query,
        latent,
        out,
        rest.reshape(sides, 2, rest_rows, width),
        first.reshape(sides, 2, part_rows, width),
        residual,
        inputs_part,
        gain.reshape(1, width),
        *units,
        rows,
        cotangent,
    )


def on_device(
    inputs,
    cotangent,
    positions,
    routes,
    slot_index,
    attention_gain,
    feedforward_gain,
    latent_gain,
    query_weight,
    latent_down,
    latent_up,
    out_weight,
    router_weight,
    shared_gate,
    shared_up,
    shared_down,
    expert_gate,
    expert_up,
    expert_down,
):
    length, model_width = inputs.shape
    tensor_count = lax.axis_size("tensor")
    group_count = lax.axis_size("expert")
    tensor_index = lax.axis_index("tensor")
    group_index = lax.axis_index("expert")
    head_width = NOPE + ROPE
    local_heads = query_weight.shape[1] // head_width
    local_experts, _, expert_hidden_width = expert_gate.shape
    shared_width = shared_gate.shape[1]
    experts_all = local_experts * group_count
    capacity = max(
        tensor_count, length * TOP * 4 // (3 * experts_all) // tensor_count * tensor_count
    )
    score_scale = 1.0 / math.sqrt(head_width)
    part_rows = length // tensor_count
    part_start = tensor_index * part_rows
    shard_columns = model_width // group_count

    def own_part(rows):
        return lax.dynamic_slice_in_dim(rows, part_start, part_rows, 0)

    def own_sequence(rows):
        return lax.dynamic_slice_in_dim(rows, group_index * length, length, 0)

    def own_columns(rows):
        return lax.dynamic_slice_in_dim(rows, group_index * shard_columns, shard_columns, 1)

    marks = expert_table(routes, jnp.where(slot_index < capacity, 2.0, 1.0), LANES)
    cotangent_all = gather_rows(
        jnp.concatenate([own_part(cotangent), own_part(marks).astype(jnp.bfloat16)], axis=1)
    )

    rows_in = inputs.astype(jnp.float32)
    normed_one, unit_one, factor_one = normalize(rows_in, attention_gain)
    first_norm = normed_one.astype(jnp.bfloat16)
    cosine, sine_table = rope_tables(positions)
    query_raw = plain_dot(first_norm, query_weight).reshape(length, local_heads, head_width)
    queries = jnp.concatenate(
        [
            query_raw[..., :NOPE],
            rotate(query_raw[..., NOPE:], cosine[:, None], sine_table[:, None]),
        ],
        axis=-1,
    ).astype(jnp.bfloat16)
    latent_raw = plain_dot(first_norm, latent_down)
    latent_normed, unit_latent, factor_latent = normalize(latent_raw[:, :KVR], latent_gain)
    latent = latent_normed.astype(jnp.bfloat16)
    key_rope = rotate(latent_raw[:, KVR:], cosine, sine_table).astype(jnp.bfloat16)
    key_value = (
        plain_dot(latent, latent_up).astype(jnp.bfloat16).reshape(length, local_heads, NOPE + VD)
    )
    key_rows = jnp.concatenate(
        [
            key_value[..., :NOPE],
            jnp.broadcast_to(key_rope[:, None, :], (length, local_heads, ROPE)),
        ],
        axis=-1,
    )
    values = key_value[..., NOPE:]
    visible = visible_mask(positions, length)
    scores = jnp.where(
        visible[None],
        jnp.einsum("qhd,khd->hqk", queries, key_rows, preferred_element_type=jnp.float32)
        * score_scale,
        -jnp.inf,
    )
    weights = jax.nn.softmax(scores, axis=-1)
    weights_low = weights.astype(jnp.bfloat16)
    head_out = (
        jnp.einsum("hqk,khd->qhd", weights_low, values, preferred_element_type=jnp.float32)
        .astype(jnp.bfloat16)
        .reshape(length, local_heads * VD)
    )
    gate_stored = expert_gate.swapaxes(1, 2).reshape(shared_width, model_width)
    up_stored = expert_up.swapaxes(1, 2).reshape(shared_width, model_width)
    down_stored = expert_down.reshape(shared_width, model_width)
    router_padded = jnp.pad(router_weight, ((0, 0), (0, LANES - experts_all)))
    second_all, acts, logits_all, residual = run_forward(
        plain_dot(head_out, out_weight).astype(jnp.bfloat16),
        inputs,
        feedforward_gain,
        (gate_stored, up_stored, shared_gate.T, shared_up.T),
        router_padded,
    )
    (
        expert_hidden,
        expert_dpre,
        expert_dlin,
        shared_hidden,
        shared_dpre,
        shared_dlin,
        attention_grad,
        result_part,
        grad_residual,
        logit_low,
        grad_feedforward_gain,
    ) = run_backward(
        cotangent_all,
        acts,
        logits_all,
        (gate_stored, up_stored, down_stored, shared_gate.T, shared_up.T, shared_down),
        router_padded,
        residual,
        feedforward_gain,
        local_experts,
    )
    result = lax.all_gather(result_part, "tensor", axis=0, tiled=True)
    tokens = group_count * length
    second_all = second_all.reshape(tokens, model_width)

    attention_grad = attention_grad.reshape(length, model_width)
    second_part = lax.dynamic_slice_in_dim(
        second_all, group_index * length + part_start, part_rows, 0
    )
    grad_out_weight = lead_dot(head_out, attention_grad)
    head_grad = (
        tail_dot(attention_grad, out_weight).astype(jnp.bfloat16).reshape(length, local_heads, VD)
    )
    weight_grad = jnp.einsum("qhd,khd->hqk", head_grad, values, preferred_element_type=jnp.float32)
    score_grad = (
        weights * (weight_grad - jnp.sum(weights * weight_grad, axis=-1, keepdims=True))
    ).astype(jnp.bfloat16)
    query_grad = (
        jnp.einsum("hqk,khd->qhd", score_grad, key_rows, preferred_element_type=jnp.float32)
        * score_scale
    )
    key_grad = (
        jnp.einsum("hqk,qhd->khd", score_grad, queries, preferred_element_type=jnp.float32)
        * score_scale
    )
    value_grad = jnp.einsum(
        "hqk,qhd->khd", weights_low, head_grad, preferred_element_type=jnp.float32
    )
    query_low = (
        jnp.concatenate(
            [
                query_grad[..., :NOPE],
                rotate_back(query_grad[..., NOPE:], cosine[:, None], sine_table[:, None]),
            ],
            axis=-1,
        )
        .astype(jnp.bfloat16)
        .reshape(length, local_heads * head_width)
    )
    grad_query = lead_dot(first_norm, query_low)
    keyvalue_low = (
        jnp.concatenate([key_grad[..., :NOPE], value_grad], axis=-1)
        .astype(jnp.bfloat16)
        .reshape(length, local_heads * (NOPE + VD))
    )
    grad_latent_up = lead_dot(latent, keyvalue_low)
    latent_grad = tail_dot(keyvalue_low, latent_up)
    latent_back, grad_latent_gain = norm_back(latent_grad, unit_latent, factor_latent, latent_gain)
    rope_back = rotate_back(jnp.sum(key_grad[..., NOPE:], axis=1), cosine, sine_table)
    down_low = jnp.concatenate([latent_back, rope_back], axis=1).astype(jnp.bfloat16)
    first_terms = (tail_dot(query_low, query_weight) + tail_dot(down_low, latent_down)).astype(
        jnp.bfloat16
    )
    latent_width = latent_down.shape[1]
    latent_gain_rows = jnp.pad(
        grad_latent_gain.reshape(group_count, -1),
        ((0, 0), (0, shard_columns - KVR // group_count)),
    ).reshape(1, model_width)
    gain_start = latent_width + -(-experts_all // 16) * 16
    rest_count = gain_start + 16
    rest_rows = -(-rest_count // (16 * tensor_count)) * 16 * tensor_count

    def at_row(start, rows):
        return jnp.pad(rows, ((start, rest_rows - start - rows.shape[0]), (0, 0)))

    rest = (
        lead_dot(jnp.pad(down_low, ((0, 0), (0, rest_rows - latent_width))), first_norm)
        + at_row(latent_width, lead_dot(logit_low[:, :experts_all], second_part))
        + at_row(gain_start, grad_feedforward_gain)
        + at_row(gain_start + 1, latent_gain_rows)
    ).astype(jnp.bfloat16)
    (
        grad_query,
        grad_latent_up,
        grad_out_weight,
        rest,
        grad_input,
        grad_expert_gate,
        grad_expert_up,
        grad_expert_down,
        grad_shared_gate,
        grad_shared_up,
        grad_shared_down,
    ) = run_weights(
        grad_query.astype(jnp.bfloat16),
        grad_latent_up.astype(jnp.bfloat16),
        grad_out_weight.astype(jnp.bfloat16),
        rest,
        first_terms,
        grad_residual,
        own_part(inputs),
        attention_gain,
        [
            units.reshape(tokens, shared_width)
            for units in (
                expert_dpre,
                expert_dlin,
                expert_hidden,
                shared_dpre,
                shared_dlin,
                shared_hidden,
            )
        ],
        second_all,
        cotangent_all,
    )
    grad_input = grad_input.reshape(length, model_width).astype(jnp.float32)
    rest = rest.astype(jnp.float32)
    grad_attention_gain = jnp.sum(rest[:, -16], axis=0)
    rest = rest[:, :-16].reshape(-1, shard_columns)
    gain_rows = rest[gain_start:rest_count]

    def stored_experts(rows):
        return rows.reshape(local_experts, expert_hidden_width, model_width)

    return (
        result,
        grad_input,
        grad_attention_gain,
        gain_rows[0],
        gain_rows[1, : KVR // group_count],
        grad_query,
        rest[:latent_width].T,
        grad_latent_up,
        grad_out_weight,
        rest[latent_width : latent_width + experts_all].T,
        grad_shared_gate.T,
        grad_shared_up.T,
        grad_shared_down,
        stored_experts(grad_expert_gate).swapaxes(1, 2),
        stored_experts(grad_expert_up).swapaxes(1, 2),
        stored_experts(grad_expert_down),
    )


def solution(mesh):
    placed = (
        P("expert", None),
        P("expert", None),
        P("expert"),
        P("expert", None),
        P("expert", None),
        P(),
        P(),
        P(),
        P(None, "tensor"),
        P(),
        P(None, "tensor"),
        P("tensor", None),
        P(),
        P(None, "tensor"),
        P(None, "tensor"),
        P("tensor", None),
        P("expert", None, "tensor"),
        P("expert", None, "tensor"),
        P("expert", "tensor", None),
    )
    return jax.shard_map(
        on_device,
        mesh=mesh,
        in_specs=placed,
        out_specs=(
            P("expert", None),
            P("expert", None),
            P("expert"),
            P("expert"),
            P("expert"),
            P("expert", "tensor"),
            P("expert", None),
            P("expert", "tensor"),
            P("tensor", "expert"),
            P("expert", None),
            P("expert", "tensor"),
            P("expert", "tensor"),
            P("tensor", "expert"),
            P("expert", None, "tensor"),
            P("expert", None, "tensor"),
            P("expert", "tensor", None),
        ),
        check_vma=False,
    )
```

```python
import functools
import math

import jax
import jax.numpy as jnp
from jax import lax
from jax.experimental import pallas as pl
from jax.experimental.pallas import tpu as pltpu
from jax.sharding import PartitionSpec as P

NOPE = 128
ROPE = 64
VD = 128
KVR = 512
TOP = 6


EPSILON = 1e-06


def plain_dot(left_side, right_side):
    return jnp.dot(left_side, right_side, preferred_element_type=jnp.float32)


def lead_dot(left_side, right_side):
    return lax.dot_general(
        left_side, right_side, (((0,), (0,)), ((), ())), preferred_element_type=jnp.float32
    )


def tail_dot(left_side, right_side):
    return lax.dot_general(
        left_side, right_side, (((1,), (1,)), ((), ())), preferred_element_type=jnp.float32
    )


def normalize(values, gain_vector):
    factor = lax.rsqrt(jnp.mean(values * values, axis=-1, keepdims=True) + EPSILON)
    unit_rows = values * factor
    return (unit_rows * gain_vector, unit_rows, factor)


def norm_back(upstream, unit_rows, factor, gain_vector):
    scaled = upstream * gain_vector
    inner_mean = jnp.mean(scaled * unit_rows, axis=-1, keepdims=True)
    return (factor * (scaled - unit_rows * inner_mean), jnp.sum(upstream * unit_rows, axis=0))


def rope_tables(positions):
    half_width = ROPE // 2
    frequency = 10000.0 ** (-2.0 * jnp.arange(half_width, dtype=jnp.float32) / ROPE)
    angles = positions.astype(jnp.float32)[:, None] * frequency[None, :]
    return (jnp.cos(angles), jnp.sin(angles))


def rotate(values, cosine, sine_table):
    half_width = values.shape[-1] // 2
    front_half = values[..., :half_width]
    back_half = values[..., half_width:]
    return jnp.concatenate(
        [
            front_half * cosine - back_half * sine_table,
            back_half * cosine + front_half * sine_table,
        ],
        axis=-1,
    )


def rotate_back(values, cosine, sine_table):
    half_width = values.shape[-1] // 2
    front_half = values[..., :half_width]
    back_half = values[..., half_width:]
    return jnp.concatenate(
        [
            front_half * cosine + back_half * sine_table,
            back_half * cosine - front_half * sine_table,
        ],
        axis=-1,
    )


BOTH = ("expert", "tensor")


def visible_mask(positions, length):
    rows = jnp.arange(length, dtype=jnp.int32)
    starts = rows - positions
    return (rows[None, :] <= rows[:, None]) & (rows[None, :] >= starts[:, None])


def gather_rows(rows):
    return lax.all_gather(rows, BOTH, axis=0, tiled=True)


def scatter_rows(rows):
    return lax.psum_scatter(rows, BOTH, scatter_dimension=0, tiled=True)


def expert_table(routes, values, expert_total):
    ids = jnp.arange(expert_total, dtype=jnp.int32)
    table = jnp.zeros((routes.shape[0], expert_total), jnp.float32)
    for member in range(TOP):
        table = table + jnp.where(
            routes[:, member : member + 1] == ids[None, :], values[:, member : member + 1], 0.0
        )
    return table


MESH = pl.DeviceIdType.MESH
LANES = 128
LAYERS = 4
EPS = EPSILON


def dot_rows(left_side, right_side):
    return lax.dot_general(
        left_side, right_side, (((1,), (1,)), ((), ())), preferred_element_type=jnp.float32
    )


def dot_plain(left_side, right_side):
    return jnp.dot(left_side, right_side, preferred_element_type=jnp.float32)


class Place:
    def __init__(self, groups, tensors):
        self.groups = groups
        self.tensors = tensors
        self.layers = min(LAYERS, groups)
        self.lanes = groups // self.layers
        self.sides = tensors // 2
        self.me = lax.axis_index("expert")
        self.mine = lax.axis_index("tensor")
        self.layer = self.me // self.lanes
        self.lane = self.me % self.lanes
        self.side = self.mine // 2
        self.core = self.mine % 2
        self.sibling = self.side * 2 + (1 - self.core)

    def side_of(self, shift):
        return (self.side + shift) % self.sides

    def tensor_of(self, shift):
        return self.side_of(shift) * 2 + self.core

    def expert_of(self, layer_shift, lane_shift):
        return ((self.layer + layer_shift) % self.layers) * self.lanes + (
            self.lane + lane_shift
        ) % self.lanes

    def greet(self, peers):
        barrier = pltpu.get_barrier_semaphore()
        count = self.sides
        if peers:
            count = count + self.layers + self.lanes - 2
            partners = [self.expert_of(shift, 0) for shift in range(1, self.layers)]
            partners += [self.expert_of(0, shift) for shift in range(1, self.lanes)]
            for partner in partners:
                pl.semaphore_signal(
                    barrier, inc=1, device_id={"expert": partner}, device_id_type=MESH
                )
        for shift in range(1, self.sides):
            pl.semaphore_signal(
                barrier, inc=1, device_id={"tensor": self.tensor_of(shift)}, device_id_type=MESH
            )
        pl.semaphore_signal(
            barrier, inc=1, device_id={"tensor": self.sibling}, device_id_type=MESH
        )
        return barrier, count


def remote(source, target, send_sem, recv_sem, axis, index):
    return pltpu.make_async_remote_copy(
        src_ref=source,
        dst_ref=target,
        send_sem=send_sem,
        recv_sem=recv_sem,
        device_id={axis: index},
        device_id_type=MESH,
    )


def sum_over_tensor(place, terms, core_land, side_send, side_land, sems):
    core_send_sem, core_land_sem, side_send_sem, side_land_sem = sems
    core_copy = remote(
        terms.at[:, 1 - place.core],
        core_land,
        core_send_sem,
        core_land_sem,
        "tensor",
        place.sibling,
    )
    core_copy.start()
    core_copy.wait_recv()
    copies = []
    for shift in range(1, place.sides):
        other = place.side_of(shift)
        side_send[shift - 1] = (
            terms[other, place.core].astype(jnp.float32) + core_land[other].astype(jnp.float32)
        ).astype(jnp.bfloat16)
        copy = remote(
            side_send.at[shift - 1],
            side_land.at[shift - 1],
            side_send_sem.at[shift - 1],
            side_land_sem.at[shift - 1],
            "tensor",
            place.tensor_of(shift),
        )
        copy.start()
        copies.append(copy)
    total = terms[place.side, place.core].astype(jnp.float32) + core_land[place.side].astype(
        jnp.float32
    )
    for copy in copies:
        copy.wait_recv()
    for shift in range(1, place.sides):
        total = total + side_land[shift - 1].astype(jnp.float32)
    core_copy.wait_send()
    for copy in copies:
        copy.wait_send()
    return total


def spread_over_tensor(place, part, whole, sems):
    own_sem, side_sem, core_sem, arrive_sem = sems
    own_copy = pltpu.make_async_copy(part, whole.at[place.mine], own_sem)
    own_copy.start()
    sends = []
    for shift in range(1, place.sides):
        sends.append(
            remote(
                part,
                whole.at[place.mine],
                side_sem.at[shift],
                arrive_sem.at[place.mine],
                "tensor",
                place.tensor_of(shift),
            )
        )
    sends.append(
        remote(
            part,
            whole.at[place.mine],
            core_sem.at[0],
            arrive_sem.at[place.mine],
            "tensor",
            place.sibling,
        )
    )
    for copy in sends:
        copy.start()

    def wait_piece(tensor):
        view = whole.at[tensor]
        pltpu.make_async_copy(view, view, arrive_sem.at[tensor]).wait()

    for shift in range(1, place.sides):
        tensor = place.tensor_of(shift)
        wait_piece(tensor)
        copy = remote(
            whole.at[tensor],
            whole.at[tensor],
            core_sem.at[shift],
            arrive_sem.at[tensor],
            "tensor",
            place.sibling,
        )
        copy.start()
        sends.append(copy)
    for shift in range(place.sides):
        wait_piece(place.side_of(shift) * 2 + (1 - place.core))
    own_copy.wait()
    for copy in sends:
        copy.wait_send()


def forward_kernel(
    attention_ref,
    inputs_ref,
    gain_ref,
    gate_ref,
    up_ref,
    shared_gate_ref,
    shared_up_ref,
    router_ref,
    rows_ref,
    acts_ref,
    logits_ref,
    residual_ref,
    gate_w,
    up_w,
    shared_gate_w,
    shared_up_w,
    router_w,
    terms_buf,
    core_land,
    side_send,
    side_land,
    inputs_buf,
    part_buf,
    rows_buf,
    logits_buf,
    acts_buf,
    weight_sem,
    first_sem,
    load_sem,
    store_sem,
    sum_core_sem,
    sum_core_land_sem,
    sum_side_sem,
    sum_side_land_sem,
    layer_sem,
    layer_land_sem,
    lane_sem,
    lane_land_sem,
    side_sem,
    side_land_sem,
    lane_half_sem,
    lane_half_land_sem,
    side_half_sem,
    side_half_land_sem,
    core_sem,
    core_land_sem,
    *,
    groups,
    tensors,
):
    place = Place(groups, tensors)
    sides, layers, lanes = place.sides, place.layers, place.lanes
    me, mine, core = place.me, place.mine, place.core
    length = rows_buf.shape[1]
    width = rows_buf.shape[2]
    half = width // 2
    part_rows = length // tensors
    row_block = min(256, length)

    pairs = (
        (gate_ref, gate_w),
        (up_ref, up_w),
        (shared_gate_ref, shared_gate_w),
        (shared_up_ref, shared_up_w),
        (router_ref, router_w),
    )
    first_copies = (
        pltpu.make_async_copy(attention_ref, terms_buf, first_sem.at[0]),
        pltpu.make_async_copy(
            inputs_ref.at[pl.ds(pl.multiple_of(mine * part_rows, part_rows), part_rows), :],
            inputs_buf,
            first_sem.at[1],
        ),
    )
    for copy in first_copies:
        copy.start()
    weight_copies = [
        pltpu.make_async_copy(source, target, weight_sem.at[index])
        for index, (source, target) in enumerate(pairs)
    ]
    barrier, count = place.greet(True)

    def sequence_of(step):
        return place.expert_of(step // lanes, step % lanes)

    def load_copy(step):
        slot = step % 2
        return pltpu.make_async_copy(
            rows_ref.at[sequence_of(step)], rows_buf.at[slot], load_sem.at[slot]
        )

    def store_copies(step):
        slot = step % 2
        sequence = sequence_of(step)
        return (
            pltpu.make_async_copy(
                acts_buf.at[slot], acts_ref.at[:, sequence], store_sem.at[slot, 0]
            ),
            pltpu.make_async_copy(
                logits_buf.at[slot], logits_ref.at[sequence], store_sem.at[slot, 1]
            ),
        )

    def piece(layer_shift, lane_shift, tensor, columns=None):
        rows = pl.ds(pl.multiple_of(tensor * part_rows, part_rows), part_rows)
        sequence = place.expert_of(layer_shift, lane_shift)
        if columns is None:
            return rows_ref.at[sequence, rows, :]
        return rows_ref.at[sequence, rows, pl.ds(columns * half, half)]

    def await_bytes(view, sem):
        pltpu.make_async_copy(view, view, sem).wait()

    def layer_spread(shift):
        return remote(
            part_buf,
            piece(0, 0, mine),
            layer_sem.at[shift],
            layer_land_sem.at[shift],
            "expert",
            place.expert_of(layers - shift, 0),
        )

    def lane_spread(layer_shift, shift):
        view = piece(layer_shift, 0, mine)
        return remote(
            view,
            view,
            lane_sem.at[layer_shift, shift],
            lane_land_sem.at[layer_shift, shift],
            "expert",
            place.expert_of(0, lanes - shift),
        )

    def side_spread(layer_shift, shift):
        view = piece(layer_shift, 0, mine)
        return remote(
            view,
            view,
            side_sem.at[layer_shift, shift],
            side_land_sem.at[layer_shift, shift],
            "tensor",
            place.tensor_of(sides - shift),
        )

    def side_half_spread(layer_shift, lane_shift, shift):
        view = piece(layer_shift, lane_shift, mine, 0)
        return remote(
            view,
            view,
            side_half_sem.at[layer_shift, lane_shift, shift],
            side_half_land_sem.at[layer_shift, lane_shift, shift],
            "tensor",
            place.tensor_of(sides - shift),
        )

    def lane_half_spread(layer_shift, shift, side_shift):
        view = piece(layer_shift, 0, place.tensor_of(side_shift), 1)
        return remote(
            view,
            view,
            lane_half_sem.at[layer_shift, shift, side_shift],
            lane_half_land_sem.at[layer_shift, shift, side_shift],
            "expert",
            place.expert_of(0, lanes - shift),
        )

    def core_spread(layer_shift, lane_shift, side_shift):
        view = piece(layer_shift, lane_shift, place.tensor_of(side_shift))
        return remote(
            view,
            view,
            core_sem.at[layer_shift, lane_shift, side_shift],
            core_land_sem.at[layer_shift, lane_shift, side_shift],
            "tensor",
            place.sibling,
        )

    def first_hop(layer_shift, landed):
        if landed:
            await_bytes(piece(layer_shift, 0, mine), layer_land_sem.at[layer_shift])
        for shift in range(1, sides):
            side_spread(layer_shift, shift).start()
        for shift in range(1, lanes):
            lane_spread(layer_shift, shift).start()
        core_spread(layer_shift, 0, 0).start()

    def second_hop(layer_shift):
        for shift in range(1, sides):
            await_bytes(
                piece(layer_shift, 0, place.tensor_of(shift)),
                side_land_sem.at[layer_shift, shift],
            )
            core_spread(layer_shift, 0, shift).start()
            for lane_shift in range(1, lanes):
                lane_half_spread(layer_shift, lane_shift, shift).start()
        for lane_shift in range(1, lanes):
            await_bytes(
                piece(layer_shift, lane_shift, mine), lane_land_sem.at[layer_shift, lane_shift]
            )
            for shift in range(1, sides):
                side_half_spread(layer_shift, lane_shift, shift).start()
            core_spread(layer_shift, lane_shift, 0).start()

    def third_hop(layer_shift):
        for lane_shift in range(1, lanes):
            for shift in range(1, sides):
                tensor = place.tensor_of(shift)
                await_bytes(
                    piece(layer_shift, lane_shift, tensor, 0),
                    side_half_land_sem.at[layer_shift, lane_shift, shift],
                )
                await_bytes(
                    piece(layer_shift, lane_shift, tensor, 1),
                    lane_half_land_sem.at[layer_shift, lane_shift, shift],
                )
                core_spread(layer_shift, lane_shift, shift).start()

    def await_sibling(step):
        layer_shift = step // lanes
        lane_shift = step % lanes
        for shift in range(sides):
            tensor = place.side_of(shift) * 2 + (1 - core)
            await_bytes(
                piece(layer_shift, lane_shift, tensor),
                core_land_sem.at[layer_shift, lane_shift, shift],
            )

    for copy in first_copies:
        copy.wait()
    pl.semaphore_wait(barrier, count)
    for copy in weight_copies:
        copy.start()
    attention = sum_over_tensor(
        place,
        terms_buf,
        core_land,
        side_send,
        side_land,
        (sum_core_sem, sum_core_land_sem, sum_side_sem, sum_side_land_sem),
    )
    residual = inputs_buf[...].astype(jnp.float32) + attention
    residual_ref[...] = residual
    factor = lax.rsqrt(jnp.mean(residual * residual, axis=1, keepdims=True) + EPS)
    part_buf[...] = (residual * factor * gain_ref[...]).astype(jnp.bfloat16)

    own_copy = pltpu.make_async_copy(part_buf, piece(0, 0, mine), first_sem.at[2])
    own_copy.start()
    for shift in range(1, layers):
        layer_spread(shift).start()
    own_copy.wait()
    first_hop(0, False)
    second_hop(0)
    await_sibling(0)
    load_copy(0).start()
    for copy in weight_copies:
        copy.wait()

    def step_body(step, carry):
        slot = step % 2
        layer_shift = step // lanes
        lane_shift = step % lanes
        load_copy(step).wait()

        @pl.when(step > 1)
        def _():
            for copy in store_copies(step - 2):
                copy.wait()

        logits_buf[slot] = dot_plain(rows_buf[slot], router_w[...])

        def hidden_rows(block, inner):
            rows = pl.ds(pl.multiple_of(block * row_block, row_block), row_block)
            here = rows_buf[slot, rows, :]
            for index, weight in ((0, gate_w), (1, up_w)):
                acts_buf[slot, index, rows, :] = dot_rows(here, weight[...]).astype(jnp.bfloat16)
            return inner

        lax.fori_loop(0, length // row_block, hidden_rows, 0)

        @pl.when(lane_shift == 0)
        def _():
            third_hop(layer_shift)

            @pl.when(layer_shift + 1 < layers)
            def _():
                first_hop(layer_shift + 1, True)

        @pl.when((lane_shift == lanes - 1) & (layer_shift + 1 < layers))
        def _():
            second_hop(layer_shift + 1)

        def shared_rows(block, inner):
            rows = pl.ds(pl.multiple_of(block * row_block, row_block), row_block)
            here = rows_buf[slot, rows, :]
            for index, weight in ((2, shared_gate_w), (3, shared_up_w)):
                acts_buf[slot, index, rows, :] = dot_rows(here, weight[...]).astype(jnp.bfloat16)
            return inner

        lax.fori_loop(0, length // row_block, shared_rows, 0)

        @pl.when(step + 1 < groups)
        def _():
            await_sibling(step + 1)
            load_copy(step + 1).start()

        for copy in store_copies(step):
            copy.start()
        return carry

    lax.fori_loop(0, groups, step_body, 0)

    for step in range(max(groups - 2, 0), groups):
        for copy in store_copies(step):
            copy.wait()
    for shift in range(1, layers):
        layer_spread(shift).wait_send()
    for layer_shift in range(layers):
        for shift in range(1, sides):
            side_spread(layer_shift, shift).wait_send()
        for lane_shift in range(lanes):
            if lane_shift > 0:
                lane_spread(layer_shift, lane_shift).wait_send()
                for shift in range(1, sides):
                    side_half_spread(layer_shift, lane_shift, shift).wait_send()
                    lane_half_spread(layer_shift, lane_shift, shift).wait_send()
            for shift in range(sides):
                core_spread(layer_shift, lane_shift, shift).wait_send()


def backward_kernel(
    cotangent_ref,
    acts_ref,
    logits_ref,
    gate_ref,
    up_ref,
    down_ref,
    shared_gate_ref,
    shared_up_ref,
    shared_down_ref,
    router_ref,
    residual_ref,
    gain_ref,
    expert_hidden_ref,
    expert_dpre_ref,
    expert_dlin_ref,
    shared_hidden_ref,
    shared_dpre_ref,
    shared_dlin_ref,
    spread_ref,
    result_ref,
    grad_residual_ref,
    logit_ref,
    gain_grad_ref,
    gate_w,
    up_w,
    down_w,
    shared_gate_w,
    shared_up_w,
    shared_down_w,
    router_w,
    cotangent_buf,
    acts_buf,
    logits_buf,
    codes_buf,
    units_buf,
    gate_grad_buf,
    sum_buf,
    core_land,
    side_land,
    lane_send,
    lane_land,
    block_land,
    block_send,
    block_side_land,
    layer_send,
    layer_land,
    cotangent_part,
    code_part,
    gates_part,
    part_buf,
    weight_sem,
    load_sem,
    store_sem,
    part_sem,
    core_sem,
    core_land_sem,
    side_sem,
    side_land_sem,
    lane_sem,
    lane_land_sem,
    block_sem,
    block_land_sem,
    block_side_sem,
    block_side_land_sem,
    layer_sem,
    layer_land_sem,
    own_sem,
    spread_side_sem,
    spread_core_sem,
    arrive_sem,
    *,
    groups,
    tensors,
    local_experts,
):
    place = Place(groups, tensors)
    sides, layers, lanes = place.sides, place.layers, place.lanes
    me, mine, core, side = place.me, place.mine, place.core, place.side
    length = cotangent_buf.shape[0]
    width = cotangent_buf.shape[1]
    part_rows = length // tensors
    hidden = gate_w.shape[0]
    own_width = hidden // local_experts
    row_block = min(256, length)
    column_block = min(512, width)
    first = pl.ds(0, width)
    second = pl.ds(width, width + LANES)
    marks = pl.ds(width, LANES)

    pairs = (
        (down_ref, down_w),
        (shared_down_ref, shared_down_w),
        (gate_ref, gate_w),
        (up_ref, up_w),
        (shared_gate_ref, shared_gate_w),
        (shared_up_ref, shared_up_w),
        (router_ref, router_w),
    )
    weight_copies = [
        pltpu.make_async_copy(source, target, weight_sem.at[index])
        for index, (source, target) in enumerate(pairs)
    ]

    def shifts_of(step):
        return (step // lanes + 1) % layers, lanes - 1 - step % lanes

    def sequence_of(step):
        layer_shift, lane_shift = shifts_of(step)
        return place.expert_of(layer_shift, lane_shift)

    def load_copies(step):
        sequence = sequence_of(step)
        return (
            pltpu.make_async_copy(
                cotangent_ref.at[sequence, :, first], cotangent_buf, load_sem.at[0]
            ),
            pltpu.make_async_copy(acts_ref.at[:, sequence], acts_buf, load_sem.at[1]),
            pltpu.make_async_copy(logits_ref.at[sequence], logits_buf, load_sem.at[2]),
            pltpu.make_async_copy(cotangent_ref.at[sequence, :, marks], codes_buf, load_sem.at[3]),
        )

    unit_refs = (
        expert_hidden_ref,
        expert_dpre_ref,
        expert_dlin_ref,
        shared_hidden_ref,
        shared_dpre_ref,
        shared_dlin_ref,
    )

    def store_copies(step):
        sequence = sequence_of(step)
        return [
            pltpu.make_async_copy(units_buf.at[index], ref.at[sequence], store_sem.at[index])
            for index, ref in enumerate(unit_refs)
        ]

    part_slice = pl.ds(pl.multiple_of(mine * part_rows, part_rows), part_rows)
    part_copies = (
        pltpu.make_async_copy(
            cotangent_ref.at[me, part_slice, first], cotangent_part, part_sem.at[0]
        ),
        pltpu.make_async_copy(cotangent_ref.at[me, part_slice, marks], code_part, part_sem.at[1]),
        pltpu.make_async_copy(logits_ref.at[me, part_slice, :], gates_part, part_sem.at[2]),
    )
    for copy in load_copies(0):
        copy.start()
    for copy in weight_copies:
        copy.start()
    for copy in part_copies:
        copy.start()
    barrier, count = place.greet(True)

    def core_send(step):
        slot = step % 2
        return remote(
            sum_buf.at[slot, :, 1 - core],
            core_land.at[slot],
            core_sem.at[slot],
            core_land_sem.at[slot],
            "tensor",
            place.sibling,
        )

    def side_copy(step, shift):
        slot = step % 2
        return remote(
            sum_buf.at[slot, place.side_of(shift), core, :, first],
            side_land.at[slot, shift - 1],
            side_sem.at[slot, shift - 1],
            side_land_sem.at[slot, shift - 1],
            "tensor",
            place.tensor_of(shift),
        )

    def lane_copy(turn, lane_shift):
        slot = turn % 2
        return remote(
            lane_send.at[slot, lane_shift - 1],
            lane_land.at[slot, lane_shift - 1],
            lane_sem.at[slot, lane_shift - 1],
            lane_land_sem.at[slot, lane_shift - 1],
            "expert",
            place.expert_of(0, lane_shift),
        )

    def block_copy(step, lane_shift):
        slot = step % 2
        turn_slot = (step // lanes) % 2
        return remote(
            sum_buf.at[slot, :, core, :, second],
            block_land.at[turn_slot, lane_shift - 1],
            block_sem.at[slot],
            block_land_sem.at[turn_slot, lane_shift - 1],
            "expert",
            place.expert_of(0, lane_shift),
        )

    def block_side_copy(turn, shift):
        slot = turn % 2
        return remote(
            block_send.at[slot, shift - 1],
            block_side_land.at[slot, shift - 1],
            block_side_sem.at[slot, shift - 1],
            block_side_land_sem.at[slot, shift - 1],
            "tensor",
            place.tensor_of(shift),
        )

    def layer_copy(turn):
        slot = turn % 2
        return remote(
            layer_send.at[slot],
            layer_land.at[turn],
            layer_sem.at[slot],
            layer_land_sem.at[turn],
            "expert",
            place.expert_of((turn + 1) % layers, 0),
        )

    def per_lane(lane_shift, act):
        for value in range(1, lanes):

            @pl.when(lane_shift == value)
            def _():
                act(value)

    def combine_cores(step):
        slot = step % 2
        _, lane_shift = shifts_of(step)
        copy = core_send(step)
        copy.wait_recv()
        copy.wait_send()
        for shift in range(sides):
            other = place.side_of(shift)
            sum_buf[slot, other, core] = (
                sum_buf[slot, other, core].astype(jnp.float32)
                + core_land[slot, other].astype(jnp.float32)
            ).astype(jnp.bfloat16)
            if shift > 0:
                side_copy(step, shift).start()
        per_lane(lane_shift, lambda value: block_copy(step, value).start())

    def combine_sides(step):
        slot = step % 2
        turn = step // lanes
        _, lane_shift = shifts_of(step)
        total = sum_buf[slot, side, core, :, first].astype(jnp.float32)
        for shift in range(1, sides):
            side_copy(step, shift).wait_recv()
            side_copy(step, shift).wait_send()
            total = total + side_land[slot, shift - 1].astype(jnp.float32)
        total = total.astype(jnp.bfloat16)

        def pass_on(value):
            block_copy(step, value).wait_send()

            @pl.when(turn >= 2)
            def _():
                lane_copy(turn - 2, value).wait_send()

            lane_send[turn % 2, value - 1] = total
            lane_copy(turn, value).start()

        per_lane(lane_shift, pass_on)

        @pl.when(lane_shift == 0)
        def _():
            turn_slot = turn % 2

            @pl.when(turn >= 2)
            def _():
                layer_copy(turn - 2).wait_send()
                for shift in range(1, sides):
                    block_side_copy(turn - 2, shift).wait_send()

            layer_send[turn_slot, :, first] = total
            for value in range(1, lanes):
                block_copy(step, value).wait_recv()
            for shift in range(sides):
                other = place.side_of(shift)
                block = sum_buf[slot, other, core, :, second].astype(jnp.float32)
                for value in range(1, lanes):
                    block = block + block_land[turn_slot, value - 1, other].astype(jnp.float32)
                block = block.astype(jnp.bfloat16)
                if shift == 0:
                    layer_send[turn_slot, :, second] = block
                else:
                    block_send[turn_slot, shift - 1] = block
                    block_side_copy(turn, shift).start()

    def turn_total(turn):
        slot = turn % 2
        branch = layer_send[slot, :, first].astype(jnp.float32)
        for value in range(1, lanes):
            lane_copy(turn, value).wait_recv()
            branch = branch + lane_land[slot, value - 1].astype(jnp.float32)
        block = layer_send[slot, :, second].astype(jnp.float32)
        for shift in range(1, sides):
            block_side_copy(turn, shift).wait_recv()
            block = block + block_side_land[slot, shift - 1].astype(jnp.float32)
        return branch, block

    def combine_lanes(step):
        turn = step // lanes
        _, lane_shift = shifts_of(step)

        @pl.when(lane_shift == 0)
        def _():
            slot = turn % 2
            branch, block = turn_total(turn)
            layer_send[slot, :, first] = branch.astype(jnp.bfloat16)
            layer_send[slot, :, second] = block.astype(jnp.bfloat16)
            layer_copy(turn).start()

    for copy in weight_copies[:2]:
        copy.wait()
    for copy in part_copies:
        copy.wait()
    pl.semaphore_wait(barrier, count)

    def softmax_named(logits, code):
        named = code > 0.5
        highest = jnp.max(jnp.where(named, logits, -jnp.inf), axis=1, keepdims=True)
        raised = jnp.where(named, jnp.exp(logits - highest), 0.0)
        return raised / jnp.sum(raised, axis=1, keepdims=True)

    def services(step):
        @pl.when((step >= 3) & (step < groups + 2))
        def _():
            combine_lanes(step - 3)

        @pl.when((step >= 2) & (step < groups + 2))
        def _():
            combine_sides(step - 2)

        @pl.when((step >= 1) & (step < groups + 1))
        def _():
            combine_cores(step - 1)

    def step_body(step, carry):
        slot = step % 2
        running = step < groups
        services(step)

        @pl.when(running)
        def _():
            for copy in load_copies(step):
                copy.wait()

            @pl.when(step > 0)
            def _():
                for copy in store_copies(step - 1):
                    copy.wait()

            def hidden_rows(block, inner):
                rows = pl.ds(pl.multiple_of(block * row_block, row_block), row_block)
                back = cotangent_buf[rows, :]
                dhid = dot_rows(back, down_w[...])
                code = codes_buf[rows, :].astype(jnp.float32)
                lane = lax.broadcasted_iota(jnp.int32, code.shape, 1)
                gates = softmax_named(logits_buf[rows, :], code)
                gates = jnp.where(code > 1.5, gates, 0.0)
                pre = acts_buf[0, rows, :].astype(jnp.float32)
                lin = acts_buf[1, rows, :].astype(jnp.float32)
                unit = lax.broadcasted_iota(jnp.int32, pre.shape, 1)
                gate = None
                for member in range(local_experts):
                    chosen = jnp.sum(
                        jnp.where(lane == me * local_experts + member, gates, 0.0),
                        axis=1,
                        keepdims=True,
                    )
                    gate = (
                        jnp.broadcast_to(chosen, pre.shape)
                        if gate is None
                        else jnp.where(unit >= member * own_width, chosen, gate)
                    )
                sigmoid = jax.nn.sigmoid(pre)
                active = pre * sigmoid
                hid = active * lin
                product = hid * dhid
                units_buf[0, rows, :] = (hid * gate).astype(jnp.bfloat16)
                dhid = dhid * gate
                units_buf[1, rows, :] = (dhid * lin * (sigmoid + active * (1.0 - sigmoid))).astype(
                    jnp.bfloat16
                )
                units_buf[2, rows, :] = (dhid * active).astype(jnp.bfloat16)
                gate_grad = jnp.zeros(code.shape, jnp.float32)
                for member in range(local_experts):
                    inside = (unit >= member * own_width) & (unit < (member + 1) * own_width)
                    gate_grad = jnp.where(
                        lane == me * local_experts + member,
                        jnp.sum(jnp.where(inside, product, 0.0), axis=1, keepdims=True),
                        gate_grad,
                    )
                gate_grad_buf[rows, :] = gate_grad
                return inner

            lax.fori_loop(0, length // row_block, hidden_rows, 0)

            def shared_rows(block, inner):
                rows = pl.ds(pl.multiple_of(block * row_block, row_block), row_block)
                dhid = dot_rows(cotangent_buf[rows, :], shared_down_w[...])
                pre = acts_buf[2, rows, :].astype(jnp.float32)
                lin = acts_buf[3, rows, :].astype(jnp.float32)
                sigmoid = jax.nn.sigmoid(pre)
                active = pre * sigmoid
                units_buf[3, rows, :] = (active * lin).astype(jnp.bfloat16)
                units_buf[4, rows, :] = (dhid * lin * (sigmoid + active * (1.0 - sigmoid))).astype(
                    jnp.bfloat16
                )
                units_buf[5, rows, :] = (dhid * active).astype(jnp.bfloat16)
                return inner

            lax.fori_loop(0, length // row_block, shared_rows, 0)

            @pl.when(step + 1 < groups)
            def _():
                for copy in load_copies(step + 1):
                    copy.start()

            @pl.when(step == 0)
            def _():
                for copy in weight_copies[2:]:
                    copy.wait()

        @pl.when(running)
        def _():
            def mix_columns(block, inner):
                start = pl.multiple_of(block * column_block, column_block)
                columns = pl.ds(start, column_block)
                moved = pl.ds(pl.multiple_of(width + start, column_block), column_block)
                sum_buf[slot, :, :, :, columns] = (
                    dot_plain(units_buf[0], down_w[:, columns])
                    .astype(jnp.bfloat16)
                    .reshape(sides, 2, part_rows, column_block)
                )
                total = dot_plain(units_buf[1], gate_w[:, columns]) + dot_plain(
                    units_buf[2], up_w[:, columns]
                )
                sum_buf[slot, :, :, :, moved] = total.astype(jnp.bfloat16).reshape(
                    sides, 2, part_rows, column_block
                )
                return inner

            lax.fori_loop(0, width // column_block, mix_columns, 0)

            @pl.when(step == groups - 1)
            def _():
                def mix_shared(block, inner):
                    start = pl.multiple_of(block * column_block, column_block)
                    columns = pl.ds(start, column_block)
                    moved = pl.ds(pl.multiple_of(width + start, column_block), column_block)
                    for target, total in (
                        (columns, dot_plain(units_buf[3], shared_down_w[:, columns])),
                        (
                            moved,
                            dot_plain(units_buf[4], shared_gate_w[:, columns])
                            + dot_plain(units_buf[5], shared_up_w[:, columns]),
                        ),
                    ):
                        sum_buf[slot, :, :, :, target] = (
                            sum_buf[slot, :, :, :, target].astype(jnp.float32)
                            + total.reshape(sides, 2, part_rows, column_block)
                        ).astype(jnp.bfloat16)
                    return inner

                lax.fori_loop(0, width // column_block, mix_shared, 0)

            sum_buf[slot, :, :, :, pl.ds(2 * width, LANES)] = (
                gate_grad_buf[...].astype(jnp.bfloat16).reshape(sides, 2, part_rows, LANES)
            )
            core_send(step).start()
            for copy in store_copies(step):
                copy.start()

        return carry

    lax.fori_loop(0, groups + 2, step_body, 0)

    last = layers - 1
    last_slot = last % 2
    for value in range(1, lanes):
        lane_copy(last, value).wait_recv()
    for shift in range(1, sides):
        block_side_copy(last, shift).wait_recv()
    for turn in range(last):
        layer_copy(turn).wait_recv()
    gain_grad_ref[...] = jnp.zeros_like(gain_grad_ref)
    few_rows = min(32, part_rows)

    def finish_rows(index, inner):
        rows = pl.ds(pl.multiple_of(index * few_rows, few_rows), few_rows)
        branch = layer_send[last_slot, rows, first].astype(jnp.float32)
        for value in range(1, lanes):
            branch = branch + lane_land[last_slot, value - 1, rows, :].astype(jnp.float32)
        block = layer_send[last_slot, rows, second].astype(jnp.float32)
        for shift in range(1, sides):
            block = block + block_side_land[last_slot, shift - 1, rows, :].astype(jnp.float32)
        for turn in range(last):
            branch = branch + layer_land[turn, rows, first].astype(jnp.float32)
            block = block + layer_land[turn, rows, second].astype(jnp.float32)
        residual = residual_ref[rows, :]
        result_ref[rows, :] = (residual + branch).astype(jnp.bfloat16)

        code = code_part[rows, :].astype(jnp.float32)
        gates = softmax_named(gates_part[rows, :], code)
        gate_grad = jnp.where(code > 1.5, block[:, width:], 0.0)
        logit = (
            gates * (gate_grad - jnp.sum(gates * gate_grad, axis=1, keepdims=True))
        ).astype(jnp.bfloat16)
        logit_ref[rows, :] = logit
        upstream = block[:, :width] + dot_rows(logit, router_w[...])
        factor = lax.rsqrt(jnp.mean(residual * residual, axis=1, keepdims=True) + EPS)
        unit_rows = residual * factor
        scaled = upstream * gain_ref[...]
        inner_mean = jnp.mean(scaled * unit_rows, axis=1, keepdims=True)
        gain_grad_ref[...] += jnp.sum(upstream * unit_rows, axis=0, keepdims=True)
        grad_residual = cotangent_part[rows, :].astype(jnp.float32) + factor * (
            scaled - unit_rows * inner_mean
        )
        grad_residual_ref[rows, :] = grad_residual
        part_buf[rows, :] = grad_residual.astype(jnp.bfloat16)
        return inner

    lax.fori_loop(0, part_rows // few_rows, finish_rows, 0)
    spread_over_tensor(
        place, part_buf, spread_ref, (own_sem, spread_side_sem, spread_core_sem, arrive_sem)
    )

    for copy in store_copies(groups - 1):
        copy.wait()
    for turn in range(max(layers - 2, 0), layers):
        for value in range(1, lanes):
            lane_copy(turn, value).wait_send()
        for shift in range(1, sides):
            block_side_copy(turn, shift).wait_send()
    layer_copy(last - 1).wait_send()


ANYWHERE = pl.BlockSpec(memory_space=pl.ANY)
IN_VMEM = pl.BlockSpec(memory_space=pltpu.VMEM)


def run_forward(attention, inputs, gain, weights, router_padded):
    groups = lax.axis_size("expert")
    tensors = lax.axis_size("tensor")
    sides = tensors // 2
    layers = min(LAYERS, groups)
    lanes = groups // layers
    length, width = inputs.shape
    part_rows = length // tensors
    hidden = weights[0].shape[0]
    bf16 = jnp.bfloat16
    f32 = jnp.float32
    dma = pltpu.SemaphoreType.DMA
    block = pltpu.VMEM((hidden, width), bf16)
    return pl.pallas_call(
        functools.partial(forward_kernel, groups=groups, tensors=tensors),
        out_shape=(
            jax.ShapeDtypeStruct((groups, length, width), bf16),
            jax.ShapeDtypeStruct((4, groups, length, hidden), bf16),
            jax.ShapeDtypeStruct((groups, length, LANES), f32),
            jax.ShapeDtypeStruct((part_rows, width), f32),
        ),
        in_specs=[ANYWHERE, ANYWHERE, IN_VMEM] + [ANYWHERE] * 5,
        out_specs=(ANYWHERE,) * 3 + (IN_VMEM,),
        scratch_shapes=[block] * 4
        + [
            pltpu.VMEM((width, LANES), bf16),
            pltpu.VMEM((sides, 2, part_rows, width), bf16),
            pltpu.VMEM((sides, part_rows, width), bf16),
            pltpu.VMEM((sides - 1, part_rows, width), bf16),
            pltpu.VMEM((sides - 1, part_rows, width), bf16),
            pltpu.VMEM((part_rows, width), bf16),
            pltpu.VMEM((part_rows, width), bf16),
            pltpu.VMEM((2, length, width), bf16),
            pltpu.VMEM((2, length, LANES), f32),
            pltpu.VMEM((2, 4, length, hidden), bf16),
            dma((5,)),
            dma((3,)),
            dma((2,)),
            dma((2, 2)),
            dma(()),
            dma(()),
            dma((sides - 1,)),
            dma((sides - 1,)),
            dma((layers,)),
            dma((layers,)),
            dma((layers, lanes)),
            dma((layers, lanes)),
            dma((layers, sides)),
            dma((layers, sides)),
            dma((layers, lanes, sides)),
            dma((layers, lanes, sides)),
            dma((layers, lanes, sides)),
            dma((layers, lanes, sides)),
            dma((layers, lanes, sides)),
            dma((layers, lanes, sides)),
        ],
        compiler_params=pltpu.CompilerParams(
            collective_id=1, has_side_effects=True, vmem_limit_bytes=60 * 1024 * 1024
        ),
        cost_estimate=pl.CostEstimate(
            flops=8 * groups * length * width * hidden,
            bytes_accessed=100_000_000,
            transcendentals=0,
        ),
        name="experts_forward",
    )(
        attention.reshape(sides, 2, part_rows, width),
        inputs,
        gain.reshape(1, width),
        *weights,
        router_padded,
    )


def run_backward(
    cotangent_all, acts, logits, weights, router_padded, residual, gain, local_experts
):
    groups = lax.axis_size("expert")
    tensors = lax.axis_size("tensor")
    sides = tensors // 2
    layers = min(LAYERS, groups)
    lanes = groups // layers
    part_rows, width = residual.shape
    length = part_rows * tensors
    hidden = weights[0].shape[0]
    second = width + LANES
    packed = width + second
    bf16 = jnp.bfloat16
    f32 = jnp.float32
    dma = pltpu.SemaphoreType.DMA
    block = pltpu.VMEM((hidden, width), bf16)
    units = jax.ShapeDtypeStruct((groups, length, hidden), bf16)
    return pl.pallas_call(
        functools.partial(
            backward_kernel, groups=groups, tensors=tensors, local_experts=local_experts
        ),
        out_shape=(units,) * 6
        + (
            jax.ShapeDtypeStruct((tensors, part_rows, width), bf16),
            jax.ShapeDtypeStruct((part_rows, width), bf16),
            jax.ShapeDtypeStruct((part_rows, width), f32),
            jax.ShapeDtypeStruct((part_rows, LANES), bf16),
            jax.ShapeDtypeStruct((1, width), f32),
        ),
        in_specs=[ANYWHERE] * 10 + [IN_VMEM] * 2,
        out_specs=(ANYWHERE,) * 7 + (IN_VMEM,) * 4,
        scratch_shapes=[block] * 6
        + [
            pltpu.VMEM((width, LANES), bf16),
            pltpu.VMEM((length, width), bf16),
            pltpu.VMEM((4, length, hidden), bf16),
            pltpu.VMEM((length, LANES), f32),
            pltpu.VMEM((length, LANES), bf16),
            pltpu.VMEM((6, length, hidden), bf16),
            pltpu.VMEM((length, LANES), f32),
            pltpu.VMEM((2, sides, 2, part_rows, packed), bf16),
            pltpu.VMEM((2, sides, part_rows, packed), bf16),
            pltpu.VMEM((2, sides - 1, part_rows, width), bf16),
            pltpu.VMEM((2, lanes - 1, part_rows, width), bf16),
            pltpu.VMEM((2, lanes - 1, part_rows, width), bf16),
            pltpu.VMEM((2, lanes - 1, sides, part_rows, second), bf16),
            pltpu.VMEM((2, sides - 1, part_rows, second), bf16),
            pltpu.VMEM((2, sides - 1, part_rows, second), bf16),
            pltpu.VMEM((2, part_rows, packed), bf16),
            pltpu.VMEM((layers - 1, part_rows, packed), bf16),
            pltpu.VMEM((part_rows, width), bf16),
            pltpu.VMEM((part_rows, LANES), bf16),
            pltpu.VMEM((part_rows, LANES), f32),
            pltpu.VMEM((part_rows, width), bf16),
            dma((7,)),
            dma((4,)),
            dma((6,)),
            dma((3,)),
            dma((2,)),
            dma((2,)),
            dma((2, sides - 1)),
            dma((2, sides - 1)),
            dma((2, lanes - 1)),
            dma((2, lanes - 1)),
            dma((2,)),
            dma((2, lanes - 1)),
            dma((2, sides - 1)),
            dma((2, sides - 1)),
            dma((2,)),
            dma((layers - 1,)),
            dma(()),
            dma((sides,)),
            dma((sides,)),
            dma((tensors,)),
        ],
        compiler_params=pltpu.CompilerParams(
            collective_id=2, has_side_effects=True, vmem_limit_bytes=60 * 1024 * 1024
        ),
        cost_estimate=pl.CostEstimate(
            flops=10 * groups * length * width * hidden,
            bytes_accessed=100_000_000,
            transcendentals=0,
        ),
        name="experts_backward",
    )(
        cotangent_all.reshape(groups, length, width + LANES),
        acts,
        logits,
        *weights,
        router_padded,
        residual,
        gain.reshape(1, width),
    )


def weight_kernel(
    query_ref,
    latent_ref,
    out_ref,
    rest_ref,
    first_ref,
    residual_ref,
    inputs_ref,
    gain_ref,
    units_0,
    units_1,
    units_2,
    units_3,
    units_4,
    units_5,
    rows_ref,
    cotangent_ref,
    query_sum,
    latent_sum,
    out_sum,
    rest_spread,
    first_spread,
    grad_0,
    grad_1,
    grad_2,
    grad_3,
    grad_4,
    grad_5,
    query_own,
    latent_own,
    out_own,
    rest_own,
    query_lane,
    latent_lane,
    out_lane,
    rest_lane,
    query_layer,
    latent_layer,
    out_layer,
    rest_layer,
    rest_part,
    rest_block,
    first_core_land,
    first_send,
    first_land,
    first_part,
    sum_core_land,
    sum_send,
    sum_land,
    units_buf,
    turned_buf,
    rows_buf,
    grad_buf,
    own_sem,
    lane_sem,
    lane_land_sem,
    layer_sem,
    layer_land_sem,
    units_sem,
    rows_sem,
    grad_sem,
    spread_own_sem,
    spread_side_sem,
    spread_core_sem,
    arrive_sem,
    tensor_core_sem,
    tensor_core_land_sem,
    tensor_side_sem,
    tensor_side_land_sem,
    first_own_sem,
    first_side_sem,
    first_core_sem,
    first_arrive_sem,
    *,
    groups,
    tensors,
):
    place = Place(groups, tensors)
    layers, lanes = place.layers, place.lanes
    sides = place.sides
    columns = rest_part.shape[1]
    tokens = units_buf.shape[1]
    width = rows_ref.shape[1]
    column_block = rows_buf.shape[2]
    barrier, count = place.greet(True)

    sums = (query_sum, latent_sum, out_sum, None)
    owns = (query_own, latent_own, out_own, rest_own)
    lane_lands = (query_lane, latent_lane, out_lane, rest_lane)
    layer_lands = (query_layer, latent_layer, out_layer, rest_layer)

    def share(index, expert):
        if index == 0:
            return query_ref.at[expert]
        if index == 1:
            return latent_ref.at[expert]
        part = pl.ds(pl.multiple_of(expert * columns, columns), columns)
        return (out_ref if index == 2 else rest_block).at[:, part]

    def own_copies(turn, indices=range(4)):
        return [
            pltpu.make_async_copy(
                share(index, place.expert_of((turn + 1) % layers, 0)),
                owns[index].at[turn],
                own_sem.at[turn, index],
            )
            for index in indices
        ]

    def lane_copies(turn, indices=range(4)):
        return [
            remote(
                share(index, place.expert_of((turn + 1) % layers, shift)),
                lane_lands[index].at[turn, shift - 1],
                lane_sem.at[turn, shift - 1, index],
                lane_land_sem.at[turn, shift - 1, index],
                "expert",
                place.expert_of(0, shift),
            )
            for shift in range(1, lanes)
            for index in indices
        ]

    def layer_copies(turn, indices=range(4)):
        return [
            remote(
                owns[index].at[turn],
                layer_lands[index].at[turn],
                layer_sem.at[turn, index],
                layer_land_sem.at[turn, index],
                "expert",
                place.expert_of((turn + 1) % layers, 0),
            )
            for index in indices
        ]

    def lane_total(turn, index):
        total = owns[index][turn].astype(jnp.float32)
        for shift in range(1, lanes):
            total = total + lane_lands[index][turn, shift - 1].astype(jnp.float32)
        return total

    def combine(turn, indices=range(4)):
        for copy in own_copies(turn, indices):
            copy.wait()
        for copy in lane_copies(turn, indices):
            copy.wait_recv()
        if turn < layers - 1:
            for index, copy in zip(indices, layer_copies(turn, indices)):
                owns[index][turn] = lane_total(turn, index).astype(jnp.bfloat16)
                copy.start()

    units = (units_0, units_1, units_2, units_3, units_4, units_5)
    grads = (grad_0, grad_1, grad_2, grad_3, grad_4, grad_5)
    sources = (rows_ref, rows_ref, cotangent_ref, rows_ref, rows_ref, cotangent_ref)

    def units_copy(index):
        return pltpu.make_async_copy(units[index], units_buf.at[index % 2], units_sem.at[index % 2])

    def rows_copy(index, block, slot):
        if index < 3:
            start = pl.multiple_of(block * column_block, column_block)
            part = pl.ds(start, column_block)
            target = rows_buf.at[slot]
        else:
            part = pl.ds(pl.multiple_of(place.me * columns, columns), columns)
            target = rows_buf.at[slot, :, pl.ds(0, columns)]
        return pltpu.make_async_copy(sources[index].at[:, part], target, rows_sem.at[slot])

    def grad_copy(index, block, slot):
        if index < 3:
            start = pl.multiple_of(block * column_block, column_block)
            return pltpu.make_async_copy(
                grad_buf.at[slot], grads[index].at[:, pl.ds(start, column_block)], grad_sem.at[slot]
            )
        return pltpu.make_async_copy(
            grad_buf.at[slot, :, pl.ds(0, columns)], grads[index], grad_sem.at[slot]
        )

    turn_rows = min(512, tokens)

    def turn_units(index):
        units_copy(index).wait()

        def body(block, inner):
            rows = pl.ds(pl.multiple_of(block * turn_rows, turn_rows), turn_rows)
            turned_buf[:, rows] = units_buf[index % 2, rows, :].T
            return inner

        lax.fori_loop(0, tokens // turn_rows, body, 0)
        if index + 2 < 6:
            units_copy(index + 2).start()

    blocks = width // column_block

    def routed(index):
        rows_copy(index, 0, 0).start()
        turn_units(index)

        def body(block, inner):
            slot = block % 2

            @pl.when(block + 1 < blocks)
            def _():
                rows_copy(index, block + 1, 1 - slot).start()

            rows_copy(index, block, slot).wait()

            @pl.when(block >= 2)
            def _():
                grad_copy(index, block - 2, slot).wait()

            grad_buf[slot] = dot_plain(turned_buf[...], rows_buf[slot])
            grad_copy(index, block, slot).start()
            return inner

        lax.fori_loop(0, blocks, body, 0)
        for block in range(max(blocks - 2, 0), blocks):
            grad_copy(index, block, block % 2).wait()

    def shared(index):
        slot = index % 2
        rows_copy(index, 0, slot).start()
        turn_units(index)
        rows_copy(index, 0, slot).wait()
        part = pl.ds(0, columns)
        grad_buf[slot, :, part] = dot_plain(turned_buf[...], rows_buf[slot, :, part])
        grad_copy(index, 0, slot).start()
        grad_copy(index, 0, slot).wait()

    tensor_sums = (
        (first_ref, first_core_land, first_send, first_land),
        (rest_ref, sum_core_land, sum_send, sum_land),
    )

    def core_exchange(which):
        source, land, _, _ = tensor_sums[which]
        return remote(
            source.at[:, 1 - place.core],
            land,
            tensor_core_sem.at[which],
            tensor_core_land_sem.at[which],
            "tensor",
            place.sibling,
        )

    def side_exchange(which, shift):
        _, _, send, land = tensor_sums[which]
        return remote(
            send.at[shift - 1],
            land.at[shift - 1],
            tensor_side_sem.at[which, shift - 1],
            tensor_side_land_sem.at[which, shift - 1],
            "tensor",
            place.tensor_of(shift),
        )

    def core_sum(which, other):
        source, land, _, _ = tensor_sums[which]
        return source[other, place.core].astype(jnp.float32) + land[other].astype(jnp.float32)

    def send_sides(which):
        core_exchange(which).wait_recv()
        for shift in range(1, sides):
            tensor_sums[which][2][shift - 1] = core_sum(which, place.side_of(shift)).astype(
                jnp.bfloat16
            )
            side_exchange(which, shift).start()

    def tensor_total(which):
        total = core_sum(which, place.side)
        for shift in range(1, sides):
            side_exchange(which, shift).wait_recv()
            total = total + tensor_sums[which][3][shift - 1].astype(jnp.float32)
        return total

    first_own = pltpu.make_async_copy(first_part, first_spread.at[place.mine], first_own_sem)

    def first_piece(tensor):
        return first_spread.at[tensor]

    def first_copy(view, sem, tensor, target):
        return remote(
            view, first_piece(tensor), sem, first_arrive_sem.at[tensor], "tensor", target
        )

    first_sends = [
        first_copy(first_part, first_side_sem.at[shift], place.mine, place.tensor_of(shift))
        for shift in range(1, sides)
    ]
    first_sends.append(
        first_copy(first_part, first_core_sem.at[0], place.mine, place.sibling)
    )
    first_forwards = [
        first_copy(
            first_piece(place.tensor_of(shift)),
            first_core_sem.at[shift],
            place.tensor_of(shift),
            place.sibling,
        )
        for shift in range(1, sides)
    ]

    def await_first(tensor):
        view = first_piece(tensor)
        pltpu.make_async_copy(view, view, first_arrive_sem.at[tensor]).wait()

    def finish_first():
        upstream = tensor_total(0)
        rows = inputs_ref[...].astype(jnp.float32)
        factor = lax.rsqrt(jnp.mean(rows * rows, axis=1, keepdims=True) + EPS)
        unit_rows = rows * factor
        scaled = upstream * gain_ref[...]
        inner_mean = jnp.mean(scaled * unit_rows, axis=1, keepdims=True)
        first_part[...] = (
            residual_ref[...] + factor * (scaled - unit_rows * inner_mean)
        ).astype(jnp.bfloat16)
        first_own.start()
        for copy in first_sends:
            copy.start()
        gain_grad = jnp.sum(upstream * unit_rows, axis=0, keepdims=True)
        summed_rows = rest_block.shape[0] - 16
        rest_block[pl.ds(0, summed_rows), :] = tensor_total(1).astype(jnp.bfloat16)
        row = lax.broadcasted_iota(jnp.int32, (16, width), 0)
        rest_block[pl.ds(summed_rows, 16), :] = jnp.where(row == 0, gain_grad, 0.0).astype(
            jnp.bfloat16
        )
        for turn in range(layers):
            for copy in lane_copies(turn, (3,)) + own_copies(turn, (3,)):
                copy.start()

    def forward_first():
        for shift in range(1, sides):
            await_first(place.tensor_of(shift))
            first_forwards[shift - 1].start()

    units_copy(0).start()
    units_copy(1).start()
    pl.semaphore_wait(barrier, count)
    for which in range(2):
        core_exchange(which).start()
    for turn in range(layers):
        for copy in lane_copies(turn, range(3)) + own_copies(turn, range(3)):
            copy.start()
    for which in range(2):
        send_sides(which)
    routed(0)
    combine(0, range(3))
    finish_first()
    routed(1)
    if layers > 2:
        combine(1, range(3))
    forward_first()
    routed(2)
    for turn in range(2, layers - 1):
        combine(turn, range(3))
    for turn in range(layers - 1):
        combine(turn, (3,))
    for index in range(3, 6):
        shared(index)
    combine(layers - 1)

    last = layers - 1
    for turn in range(last):
        for copy in layer_copies(turn):
            copy.wait_recv()
    for index in range(4):
        total = lane_total(last, index)
        for turn in range(last):
            total = total + layer_lands[index][turn].astype(jnp.float32)
        if index < 3:
            sums[index][...] = total
        else:
            rest_part[...] = total.astype(jnp.bfloat16)
    spread_over_tensor(
        place,
        rest_part,
        rest_spread,
        (spread_own_sem, spread_side_sem, spread_core_sem, arrive_sem),
    )
    for shift in range(sides):
        await_first(place.side_of(shift) * 2 + (1 - place.core))
    first_own.wait()
    for copy in first_sends + first_forwards:
        copy.wait_send()
    for which in range(2):
        core_exchange(which).wait_send()
        for shift in range(1, sides):
            side_exchange(which, shift).wait_send()
    for turn in range(layers):
        for copy in lane_copies(turn):
            copy.wait_send()
        if turn < last:
            for copy in layer_copies(turn):
                copy.wait_send()


def run_weights(
    query, latent, out, rest, first, residual, inputs_part, gain, units, rows, cotangent
):
    groups = lax.axis_size("expert")
    tensors = lax.axis_size("tensor")
    layers = min(LAYERS, groups)
    lanes = groups // layers
    sides = tensors // 2
    part_rows = residual.shape[0]
    rest_rows = rest.shape[0] // tensors
    tokens, width = rows.shape
    hidden = units[0].shape[1]
    columns = width // groups
    column_block = min(256, width)
    bf16 = jnp.bfloat16
    f32 = jnp.float32
    dma = pltpu.SemaphoreType.DMA
    query = query.reshape(groups, query.shape[0] // groups, query.shape[1])
    latent = latent.reshape(groups, latent.shape[0] // groups, latent.shape[1])
    shapes = (
        query.shape[1:],
        latent.shape[1:],
        (out.shape[0], columns),
        (rest_rows + 16, columns),
    )
    routed = jax.ShapeDtypeStruct((hidden, width), f32)
    shared = jax.ShapeDtypeStruct((hidden, columns), f32)
    return pl.pallas_call(
        functools.partial(weight_kernel, groups=groups, tensors=tensors),
        out_shape=tuple(jax.ShapeDtypeStruct(shape, f32) for shape in shapes[:3])
        + (jax.ShapeDtypeStruct((tensors,) + shapes[3], bf16),)
        + (jax.ShapeDtypeStruct((tensors, part_rows, width), bf16),)
        + (routed,) * 3
        + (shared,) * 3,
        in_specs=[ANYWHERE] * 3 + [IN_VMEM] * 5 + [ANYWHERE] * 8,
        out_specs=(IN_VMEM,) * 3 + (ANYWHERE,) * 8,
        scratch_shapes=[pltpu.VMEM((layers,) + shape, bf16) for shape in shapes]
        + [pltpu.VMEM((layers, lanes - 1) + shape, bf16) for shape in shapes]
        + [pltpu.VMEM((layers - 1,) + shape, bf16) for shape in shapes]
        + [
            pltpu.VMEM(shapes[3], bf16),
            pltpu.VMEM((rest_rows + 16, width), bf16),
            pltpu.VMEM((sides, part_rows, width), bf16),
            pltpu.VMEM((sides - 1, part_rows, width), bf16),
            pltpu.VMEM((sides - 1, part_rows, width), bf16),
            pltpu.VMEM((part_rows, width), bf16),
            pltpu.VMEM((sides, rest_rows, width), bf16),
            pltpu.VMEM((sides - 1, rest_rows, width), bf16),
            pltpu.VMEM((sides - 1, rest_rows, width), bf16),
            pltpu.VMEM((2, tokens, hidden), bf16),
            pltpu.VMEM((hidden, tokens), bf16),
            pltpu.VMEM((2, tokens, column_block), bf16),
            pltpu.VMEM((2, hidden, column_block), f32),
            dma((layers, 4)),
            dma((layers, lanes - 1, 4)),
            dma((layers, lanes - 1, 4)),
            dma((layers - 1, 4)),
            dma((layers - 1, 4)),
            dma((2,)),
            dma((2,)),
            dma((2,)),
            dma(()),
            dma((sides,)),
            dma((sides,)),
            dma((tensors,)),
            dma((2,)),
            dma((2,)),
            dma((2, sides - 1)),
            dma((2, sides - 1)),
            dma(()),
            dma((sides,)),
            dma((sides,)),
            dma((tensors,)),
        ],
        compiler_params=pltpu.CompilerParams(
            collective_id=4, has_side_effects=True, vmem_limit_bytes=60 * 1024 * 1024
        ),
        cost_estimate=pl.CostEstimate(
            flops=7 * tokens * width * hidden, bytes_accessed=100_000_000, transcendentals=0
        ),
        name="weights",
    )(
        query,
        latent,
        out,
        rest.reshape(sides, 2, rest_rows, width),
        first.reshape(sides, 2, part_rows, width),
        residual,
        inputs_part,
        gain.reshape(1, width),
        *units,
        rows,
        cotangent,
    )


def on_device(
    inputs,
    cotangent,
    positions,
    routes,
    slot_index,
    attention_gain,
    feedforward_gain,
    latent_gain,
    query_weight,
    latent_down,
    latent_up,
    out_weight,
    router_weight,
    shared_gate,
    shared_up,
    shared_down,
    expert_gate,
    expert_up,
    expert_down,
):
    length, model_width = inputs.shape
    tensor_count = lax.axis_size("tensor")
    group_count = lax.axis_size("expert")
    tensor_index = lax.axis_index("tensor")
    group_index = lax.axis_index("expert")
    head_width = NOPE + ROPE
    local_heads = query_weight.shape[1] // head_width
    local_experts, _, expert_hidden_width = expert_gate.shape
    shared_width = shared_gate.shape[1]
    experts_all = local_experts * group_count
    capacity = max(
        tensor_count, length * TOP * 4 // (3 * experts_all) // tensor_count * tensor_count
    )
    score_scale = 1.0 / math.sqrt(head_width)
    part_rows = length // tensor_count
    part_start = tensor_index * part_rows
    shard_columns = model_width // group_count

    def own_part(rows):
        return lax.dynamic_slice_in_dim(rows, part_start, part_rows, 0)

    def own_sequence(rows):
        return lax.dynamic_slice_in_dim(rows, group_index * length, length, 0)

    def own_columns(rows):
        return lax.dynamic_slice_in_dim(rows, group_index * shard_columns, shard_columns, 1)

    marks = expert_table(routes, jnp.where(slot_index < capacity, 2.0, 1.0), LANES)
    cotangent_all = gather_rows(
        jnp.concatenate([own_part(cotangent), own_part(marks).astype(jnp.bfloat16)], axis=1)
    )

    rows_in = inputs.astype(jnp.float32)
    normed_one, unit_one, factor_one = normalize(rows_in, attention_gain)
    first_norm = normed_one.astype(jnp.bfloat16)
    cosine, sine_table = rope_tables(positions)
    query_raw = plain_dot(first_norm, query_weight).reshape(length, local_heads, head_width)
    queries = jnp.concatenate(
        [
            query_raw[..., :NOPE],
            rotate(query_raw[..., NOPE:], cosine[:, None], sine_table[:, None]),
        ],
        axis=-1,
    ).astype(jnp.bfloat16)
    latent_raw = plain_dot(first_norm, latent_down)
    latent_normed, unit_latent, factor_latent = normalize(latent_raw[:, :KVR], latent_gain)
    latent = latent_normed.astype(jnp.bfloat16)
    key_rope = rotate(latent_raw[:, KVR:], cosine, sine_table).astype(jnp.bfloat16)
    key_value = (
        plain_dot(latent, latent_up).astype(jnp.bfloat16).reshape(length, local_heads, NOPE + VD)
    )
    key_rows = jnp.concatenate(
        [
            key_value[..., :NOPE],
            jnp.broadcast_to(key_rope[:, None, :], (length, local_heads, ROPE)),
        ],
        axis=-1,
    )
    values = key_value[..., NOPE:]
    visible = visible_mask(positions, length)
    scores = jnp.where(
        visible[None],
        jnp.einsum("qhd,khd->hqk", queries, key_rows, preferred_element_type=jnp.float32)
        * score_scale,
        -jnp.inf,
    )
    weights = jax.nn.softmax(scores, axis=-1)
    weights_low = weights.astype(jnp.bfloat16)
    head_out = (
        jnp.einsum("hqk,khd->qhd", weights_low, values, preferred_element_type=jnp.float32)
        .astype(jnp.bfloat16)
        .reshape(length, local_heads * VD)
    )
    gate_stored = expert_gate.swapaxes(1, 2).reshape(shared_width, model_width)
    up_stored = expert_up.swapaxes(1, 2).reshape(shared_width, model_width)
    down_stored = expert_down.reshape(shared_width, model_width)
    router_padded = jnp.pad(router_weight, ((0, 0), (0, LANES - experts_all)))
    second_all, acts, logits_all, residual = run_forward(
        plain_dot(head_out, out_weight).astype(jnp.bfloat16),
        inputs,
        feedforward_gain,
        (gate_stored, up_stored, shared_gate.T, shared_up.T),
        router_padded,
    )
    (
        expert_hidden,
        expert_dpre,
        expert_dlin,
        shared_hidden,
        shared_dpre,
        shared_dlin,
        attention_grad,
        result_part,
        grad_residual,
        logit_low,
        grad_feedforward_gain,
    ) = run_backward(
        cotangent_all,
        acts,
        logits_all,
        (gate_stored, up_stored, down_stored, shared_gate.T, shared_up.T, shared_down),
        router_padded,
        residual,
        feedforward_gain,
        local_experts,
    )
    result = lax.all_gather(result_part, "tensor", axis=0, tiled=True)
    tokens = group_count * length
    second_all = second_all.reshape(tokens, model_width)

    attention_grad = attention_grad.reshape(length, model_width)
    second_part = lax.dynamic_slice_in_dim(
        second_all, group_index * length + part_start, part_rows, 0
    )
    grad_out_weight = lead_dot(head_out, attention_grad)
    head_grad = (
        tail_dot(attention_grad, out_weight).astype(jnp.bfloat16).reshape(length, local_heads, VD)
    )
    weight_grad = jnp.einsum("qhd,khd->hqk", head_grad, values, preferred_element_type=jnp.float32)
    score_grad = (
        weights * (weight_grad - jnp.sum(weights * weight_grad, axis=-1, keepdims=True))
    ).astype(jnp.bfloat16)
    query_grad = (
        jnp.einsum("hqk,khd->qhd", score_grad, key_rows, preferred_element_type=jnp.float32)
        * score_scale
    )
    key_grad = (
        jnp.einsum("hqk,qhd->khd", score_grad, queries, preferred_element_type=jnp.float32)
        * score_scale
    )
    value_grad = jnp.einsum(
        "hqk,qhd->khd", weights_low, head_grad, preferred_element_type=jnp.float32
    )
    query_low = (
        jnp.concatenate(
            [
                query_grad[..., :NOPE],
                rotate_back(query_grad[..., NOPE:], cosine[:, None], sine_table[:, None]),
            ],
            axis=-1,
        )
        .astype(jnp.bfloat16)
        .reshape(length, local_heads * head_width)
    )
    grad_query = lead_dot(first_norm, query_low)
    keyvalue_low = (
        jnp.concatenate([key_grad[..., :NOPE], value_grad], axis=-1)
        .astype(jnp.bfloat16)
        .reshape(length, local_heads * (NOPE + VD))
    )
    grad_latent_up = lead_dot(latent, keyvalue_low)
    latent_grad = tail_dot(keyvalue_low, latent_up)
    latent_back, grad_latent_gain = norm_back(latent_grad, unit_latent, factor_latent, latent_gain)
    rope_back = rotate_back(jnp.sum(key_grad[..., NOPE:], axis=1), cosine, sine_table)
    down_low = jnp.concatenate([latent_back, rope_back], axis=1).astype(jnp.bfloat16)
    first_terms = (tail_dot(query_low, query_weight) + tail_dot(down_low, latent_down)).astype(
        jnp.bfloat16
    )
    latent_width = latent_down.shape[1]
    latent_gain_rows = jnp.pad(
        grad_latent_gain.reshape(group_count, -1),
        ((0, 0), (0, shard_columns - KVR // group_count)),
    ).reshape(1, model_width)
    gain_start = latent_width + -(-experts_all // 16) * 16
    rest_count = gain_start + 16
    rest_rows = -(-rest_count // (16 * tensor_count)) * 16 * tensor_count

    def at_row(start, rows):
        return jnp.pad(rows, ((start, rest_rows - start - rows.shape[0]), (0, 0)))

    rest = (
        lead_dot(jnp.pad(down_low, ((0, 0), (0, rest_rows - latent_width))), first_norm)
        + at_row(latent_width, lead_dot(logit_low[:, :experts_all], second_part))
        + at_row(gain_start, grad_feedforward_gain)
        + at_row(gain_start + 1, latent_gain_rows)
    ).astype(jnp.bfloat16)
    (
        grad_query,
        grad_latent_up,
        grad_out_weight,
        rest,
        grad_input,
        grad_expert_gate,
        grad_expert_up,
        grad_expert_down,
        grad_shared_gate,
        grad_shared_up,
        grad_shared_down,
    ) = run_weights(
        grad_query.astype(jnp.bfloat16),
        grad_latent_up.astype(jnp.bfloat16),
        grad_out_weight.astype(jnp.bfloat16),
        rest,
        first_terms,
        grad_residual,
        own_part(inputs),
        attention_gain,
        [
            units.reshape(tokens, shared_width)
            for units in (
                expert_dpre,
                expert_dlin,
                expert_hidden,
                shared_dpre,
                shared_dlin,
                shared_hidden,
            )
        ],
        second_all,
        cotangent_all,
    )
    grad_input = grad_input.reshape(length, model_width).astype(jnp.float32)
    rest = rest.astype(jnp.float32)
    grad_attention_gain = jnp.sum(rest[:, -16], axis=0)
    rest = rest[:, :-16].reshape(-1, shard_columns)
    gain_rows = rest[gain_start:rest_count]

    def stored_experts(rows):
        return rows.reshape(local_experts, expert_hidden_width, model_width)

    return (
        result,
        grad_input,
        grad_attention_gain,
        gain_rows[0],
        gain_rows[1, : KVR // group_count],
        grad_query,
        rest[:latent_width].T,
        grad_latent_up,
        grad_out_weight,
        rest[latent_width : latent_width + experts_all].T,
        grad_shared_gate.T,
        grad_shared_up.T,
        grad_shared_down,
        stored_experts(grad_expert_gate).swapaxes(1, 2),
        stored_experts(grad_expert_up).swapaxes(1, 2),
        stored_experts(grad_expert_down),
    )


def solution(mesh):
    placed = (
        P("expert", None),
        P("expert", None),
        P("expert"),
        P("expert", None),
        P("expert", None),
        P(),
        P(),
        P(),
        P(None, "tensor"),
        P(),
        P(None, "tensor"),
        P("tensor", None),
        P(),
        P(None, "tensor"),
        P(None, "tensor"),
        P("tensor", None),
        P("expert", None, "tensor"),
        P("expert", None, "tensor"),
        P("expert", "tensor", None),
    )
    return jax.shard_map(
        on_device,
        mesh=mesh,
        in_specs=placed,
        out_specs=(
            P("expert", None),
            P("expert", None),
            P("expert"),
            P("expert"),
            P("expert"),
            P("expert", "tensor"),
            P("expert", None),
            P("expert", "tensor"),
            P("tensor", "expert"),
            P("expert", None),
            P("expert", "tensor"),
            P("expert", "tensor"),
            P("tensor", "expert"),
            P("expert", None, "tensor"),
            P("expert", None, "tensor"),
            P("expert", "tensor", None),
        ),
        check_vma=False,
    )
```

```python
import functools
import math

import jax
import jax.numpy as jnp
from jax import lax
from jax.experimental import pallas as pl
from jax.experimental.pallas import tpu as pltpu
from jax.sharding import PartitionSpec as P

NOPE = 128
ROPE = 64
VD = 128
KVR = 512
TOP = 6


EPSILON = 1e-06


def plain_dot(left_side, right_side):
    return jnp.dot(left_side, right_side, preferred_element_type=jnp.float32)


def lead_dot(left_side, right_side):
    return lax.dot_general(
        left_side, right_side, (((0,), (0,)), ((), ())), preferred_element_type=jnp.float32
    )


def tail_dot(left_side, right_side):
    return lax.dot_general(
        left_side, right_side, (((1,), (1,)), ((), ())), preferred_element_type=jnp.float32
    )


def normalize(values, gain_vector):
    factor = lax.rsqrt(jnp.mean(values * values, axis=-1, keepdims=True) + EPSILON)
    unit_rows = values * factor
    return (unit_rows * gain_vector, unit_rows, factor)


def norm_back(upstream, unit_rows, factor, gain_vector):
    scaled = upstream * gain_vector
    inner_mean = jnp.mean(scaled * unit_rows, axis=-1, keepdims=True)
    return (factor * (scaled - unit_rows * inner_mean), jnp.sum(upstream * unit_rows, axis=0))


def rope_tables(positions):
    half_width = ROPE // 2
    frequency = 10000.0 ** (-2.0 * jnp.arange(half_width, dtype=jnp.float32) / ROPE)
    angles = positions.astype(jnp.float32)[:, None] * frequency[None, :]
    return (jnp.cos(angles), jnp.sin(angles))


def rotate(values, cosine, sine_table):
    half_width = values.shape[-1] // 2
    front_half = values[..., :half_width]
    back_half = values[..., half_width:]
    return jnp.concatenate(
        [
            front_half * cosine - back_half * sine_table,
            back_half * cosine + front_half * sine_table,
        ],
        axis=-1,
    )


def rotate_back(values, cosine, sine_table):
    half_width = values.shape[-1] // 2
    front_half = values[..., :half_width]
    back_half = values[..., half_width:]
    return jnp.concatenate(
        [
            front_half * cosine + back_half * sine_table,
            back_half * cosine - front_half * sine_table,
        ],
        axis=-1,
    )


BOTH = ("expert", "tensor")


def visible_mask(positions, length):
    rows = jnp.arange(length, dtype=jnp.int32)
    starts = rows - positions
    return (rows[None, :] <= rows[:, None]) & (rows[None, :] >= starts[:, None])


def gather_rows(rows):
    return lax.all_gather(rows, BOTH, axis=0, tiled=True)


def scatter_rows(rows):
    return lax.psum_scatter(rows, BOTH, scatter_dimension=0, tiled=True)


def expert_table(routes, values, expert_total):
    ids = jnp.arange(expert_total, dtype=jnp.int32)
    table = jnp.zeros((routes.shape[0], expert_total), jnp.float32)
    for member in range(TOP):
        table = table + jnp.where(
            routes[:, member : member + 1] == ids[None, :], values[:, member : member + 1], 0.0
        )
    return table


MESH = pl.DeviceIdType.MESH
LANES = 128
LAYERS = 4
EPS = EPSILON


def dot_rows(left_side, right_side):
    return lax.dot_general(
        left_side, right_side, (((1,), (1,)), ((), ())), preferred_element_type=jnp.float32
    )


def dot_plain(left_side, right_side):
    return jnp.dot(left_side, right_side, preferred_element_type=jnp.float32)


class Place:
    def __init__(self, groups, tensors):
        self.groups = groups
        self.tensors = tensors
        self.layers = min(LAYERS, groups)
        self.lanes = groups // self.layers
        self.sides = tensors // 2
        self.me = lax.axis_index("expert")
        self.mine = lax.axis_index("tensor")
        self.layer = self.me // self.lanes
        self.lane = self.me % self.lanes
        self.side = self.mine // 2
        self.core = self.mine % 2
        self.sibling = self.side * 2 + (1 - self.core)

    def side_of(self, shift):
        return (self.side + shift) % self.sides

    def tensor_of(self, shift):
        return self.side_of(shift) * 2 + self.core

    def expert_of(self, layer_shift, lane_shift):
        return ((self.layer + layer_shift) % self.layers) * self.lanes + (
            self.lane + lane_shift
        ) % self.lanes

    def greet(self, peers):
        barrier = pltpu.get_barrier_semaphore()
        count = self.sides
        if peers:
            count = count + self.layers + self.lanes - 2
            partners = [self.expert_of(shift, 0) for shift in range(1, self.layers)]
            partners += [self.expert_of(0, shift) for shift in range(1, self.lanes)]
            for partner in partners:
                pl.semaphore_signal(
                    barrier, inc=1, device_id={"expert": partner}, device_id_type=MESH
                )
        for shift in range(1, self.sides):
            pl.semaphore_signal(
                barrier, inc=1, device_id={"tensor": self.tensor_of(shift)}, device_id_type=MESH
            )
        pl.semaphore_signal(
            barrier, inc=1, device_id={"tensor": self.sibling}, device_id_type=MESH
        )
        return barrier, count


def remote(source, target, send_sem, recv_sem, axis, index):
    return pltpu.make_async_remote_copy(
        src_ref=source,
        dst_ref=target,
        send_sem=send_sem,
        recv_sem=recv_sem,
        device_id={axis: index},
        device_id_type=MESH,
    )


def sum_over_tensor(place, terms, core_land, side_send, side_land, sems):
    core_send_sem, core_land_sem, side_send_sem, side_land_sem = sems
    core_copy = remote(
        terms.at[:, 1 - place.core],
        core_land,
        core_send_sem,
        core_land_sem,
        "tensor",
        place.sibling,
    )
    core_copy.start()
    core_copy.wait_recv()
    copies = []
    for shift in range(1, place.sides):
        other = place.side_of(shift)
        side_send[shift - 1] = (
            terms[other, place.core].astype(jnp.float32) + core_land[other].astype(jnp.float32)
        ).astype(jnp.bfloat16)
        copy = remote(
            side_send.at[shift - 1],
            side_land.at[shift - 1],
            side_send_sem.at[shift - 1],
            side_land_sem.at[shift - 1],
            "tensor",
            place.tensor_of(shift),
        )
        copy.start()
        copies.append(copy)
    total = terms[place.side, place.core].astype(jnp.float32) + core_land[place.side].astype(
        jnp.float32
    )
    for copy in copies:
        copy.wait_recv()
    for shift in range(1, place.sides):
        total = total + side_land[shift - 1].astype(jnp.float32)
    core_copy.wait_send()
    for copy in copies:
        copy.wait_send()
    return total


def spread_over_tensor(place, part, whole, sems):
    own_sem, side_sem, core_sem, arrive_sem = sems
    own_copy = pltpu.make_async_copy(part, whole.at[place.mine], own_sem)
    own_copy.start()
    sends = []
    for shift in range(1, place.sides):
        sends.append(
            remote(
                part,
                whole.at[place.mine],
                side_sem.at[shift],
                arrive_sem.at[place.mine],
                "tensor",
                place.tensor_of(shift),
            )
        )
    sends.append(
        remote(
            part,
            whole.at[place.mine],
            core_sem.at[0],
            arrive_sem.at[place.mine],
            "tensor",
            place.sibling,
        )
    )
    for copy in sends:
        copy.start()

    def wait_piece(tensor):
        view = whole.at[tensor]
        pltpu.make_async_copy(view, view, arrive_sem.at[tensor]).wait()

    for shift in range(1, place.sides):
        tensor = place.tensor_of(shift)
        wait_piece(tensor)
        copy = remote(
            whole.at[tensor],
            whole.at[tensor],
            core_sem.at[shift],
            arrive_sem.at[tensor],
            "tensor",
            place.sibling,
        )
        copy.start()
        sends.append(copy)
    for shift in range(place.sides):
        wait_piece(place.side_of(shift) * 2 + (1 - place.core))
    own_copy.wait()
    for copy in sends:
        copy.wait_send()


def forward_kernel(
    attention_ref,
    inputs_ref,
    gain_ref,
    gate_ref,
    up_ref,
    shared_gate_ref,
    shared_up_ref,
    router_ref,
    rows_ref,
    acts_ref,
    logits_ref,
    residual_ref,
    gate_w,
    up_w,
    shared_gate_w,
    shared_up_w,
    router_w,
    terms_buf,
    core_land,
    side_send,
    side_land,
    inputs_buf,
    part_buf,
    rows_buf,
    logits_buf,
    acts_buf,
    weight_sem,
    first_sem,
    load_sem,
    store_sem,
    sum_core_sem,
    sum_core_land_sem,
    sum_side_sem,
    sum_side_land_sem,
    layer_sem,
    layer_land_sem,
    lane_sem,
    lane_land_sem,
    side_sem,
    side_land_sem,
    lane_half_sem,
    lane_half_land_sem,
    side_half_sem,
    side_half_land_sem,
    core_sem,
    core_land_sem,
    *,
    groups,
    tensors,
):
    place = Place(groups, tensors)
    sides, layers, lanes = place.sides, place.layers, place.lanes
    me, mine, core = place.me, place.mine, place.core
    length = rows_buf.shape[1]
    width = rows_buf.shape[2]
    half = width * 3 // 4
    part_rows = length // tensors
    row_block = min(256, length)

    pairs = (
        (gate_ref, gate_w),
        (up_ref, up_w),
        (shared_gate_ref, shared_gate_w),
        (shared_up_ref, shared_up_w),
        (router_ref, router_w),
    )
    first_copies = (
        pltpu.make_async_copy(attention_ref, terms_buf, first_sem.at[0]),
        pltpu.make_async_copy(
            inputs_ref.at[pl.ds(pl.multiple_of(mine * part_rows, part_rows), part_rows), :],
            inputs_buf,
            first_sem.at[1],
        ),
    )
    for copy in first_copies:
        copy.start()
    weight_copies = [
        pltpu.make_async_copy(source, target, weight_sem.at[index])
        for index, (source, target) in enumerate(pairs)
    ]
    barrier, count = place.greet(True)

    def sequence_of(step):
        return place.expert_of(step // lanes, step % lanes)

    def load_copy(step):
        slot = step % 2
        return pltpu.make_async_copy(
            rows_ref.at[sequence_of(step)], rows_buf.at[slot], load_sem.at[slot]
        )

    def store_copies(step):
        slot = step % 2
        sequence = sequence_of(step)
        return (
            pltpu.make_async_copy(
                acts_buf.at[slot], acts_ref.at[:, sequence], store_sem.at[slot, 0]
            ),
            pltpu.make_async_copy(
                logits_buf.at[slot], logits_ref.at[sequence], store_sem.at[slot, 1]
            ),
        )

    def piece(layer_shift, lane_shift, tensor, columns=None):
        rows = pl.ds(pl.multiple_of(tensor * part_rows, part_rows), part_rows)
        sequence = place.expert_of(layer_shift, lane_shift)
        if columns is None:
            return rows_ref.at[sequence, rows, :]
        return rows_ref.at[
            sequence, rows, pl.ds(0, half) if columns == 0 else pl.ds(half, width - half)
        ]

    def await_bytes(view, sem):
        pltpu.make_async_copy(view, view, sem).wait()

    def layer_spread(shift):
        return remote(
            part_buf,
            piece(0, 0, mine),
            layer_sem.at[shift],
            layer_land_sem.at[shift],
            "expert",
            place.expert_of(layers - shift, 0),
        )

    def lane_spread(layer_shift, shift):
        view = piece(layer_shift, 0, mine)
        return remote(
            view,
            view,
            lane_sem.at[layer_shift, shift],
            lane_land_sem.at[layer_shift, shift],
            "expert",
            place.expert_of(0, lanes - shift),
        )

    def side_spread(layer_shift, shift):
        view = piece(layer_shift, 0, mine)
        return remote(
            view,
            view,
            side_sem.at[layer_shift, shift],
            side_land_sem.at[layer_shift, shift],
            "tensor",
            place.tensor_of(sides - shift),
        )

    def side_half_spread(layer_shift, lane_shift, shift):
        view = piece(layer_shift, lane_shift, mine, 0)
        return remote(
            view,
            view,
            side_half_sem.at[layer_shift, lane_shift, shift],
            side_half_land_sem.at[layer_shift, lane_shift, shift],
            "tensor",
            place.tensor_of(sides - shift),
        )

    def lane_half_spread(layer_shift, shift, side_shift):
        view = piece(layer_shift, 0, place.tensor_of(side_shift), 1)
        return remote(
            view,
            view,
            lane_half_sem.at[layer_shift, shift, side_shift],
            lane_half_land_sem.at[layer_shift, shift, side_shift],
            "expert",
            place.expert_of(0, lanes - shift),
        )

    def core_spread(layer_shift, lane_shift, side_shift):
        view = piece(layer_shift, lane_shift, place.tensor_of(side_shift))
        return remote(
            view,
            view,
            core_sem.at[layer_shift, lane_shift, side_shift],
            core_land_sem.at[layer_shift, lane_shift, side_shift],
            "tensor",
            place.sibling,
        )

    def first_hop(layer_shift, landed):
        if landed:
            await_bytes(piece(layer_shift, 0, mine), layer_land_sem.at[layer_shift])
        for shift in range(1, sides):
            side_spread(layer_shift, shift).start()
        for shift in range(1, lanes):
            lane_spread(layer_shift, shift).start()
        core_spread(layer_shift, 0, 0).start()

    def second_hop(layer_shift):
        for shift in range(1, sides):
            await_bytes(
                piece(layer_shift, 0, place.tensor_of(shift)),
                side_land_sem.at[layer_shift, shift],
            )
            core_spread(layer_shift, 0, shift).start()
            for lane_shift in range(1, lanes):
                lane_half_spread(layer_shift, lane_shift, shift).start()
        for lane_shift in range(1, lanes):
            await_bytes(
                piece(layer_shift, lane_shift, mine), lane_land_sem.at[layer_shift, lane_shift]
            )
            for shift in range(1, sides):
                side_half_spread(layer_shift, lane_shift, shift).start()
            core_spread(layer_shift, lane_shift, 0).start()

    def third_hop(layer_shift):
        for lane_shift in range(1, lanes):
            for shift in range(1, sides):
                tensor = place.tensor_of(shift)
                await_bytes(
                    piece(layer_shift, lane_shift, tensor, 0),
                    side_half_land_sem.at[layer_shift, lane_shift, shift],
                )
                await_bytes(
                    piece(layer_shift, lane_shift, tensor, 1),
                    lane_half_land_sem.at[layer_shift, lane_shift, shift],
                )
                core_spread(layer_shift, lane_shift, shift).start()

    def await_sibling(step):
        layer_shift = step // lanes
        lane_shift = step % lanes
        for shift in range(sides):
            tensor = place.side_of(shift) * 2 + (1 - core)
            await_bytes(
                piece(layer_shift, lane_shift, tensor),
                core_land_sem.at[layer_shift, lane_shift, shift],
            )

    for copy in first_copies:
        copy.wait()
    pl.semaphore_wait(barrier, count)
    for copy in weight_copies:
        copy.start()
    attention = sum_over_tensor(
        place,
        terms_buf,
        core_land,
        side_send,
        side_land,
        (sum_core_sem, sum_core_land_sem, sum_side_sem, sum_side_land_sem),
    )
    residual = inputs_buf[...].astype(jnp.float32) + attention
    residual_ref[...] = residual
    factor = lax.rsqrt(jnp.mean(residual * residual, axis=1, keepdims=True) + EPS)
    part_buf[...] = (residual * factor * gain_ref[...]).astype(jnp.bfloat16)

    own_copy = pltpu.make_async_copy(part_buf, piece(0, 0, mine), first_sem.at[2])
    own_copy.start()
    for shift in range(1, layers):
        layer_spread(shift).start()
    own_copy.wait()
    first_hop(0, False)
    second_hop(0)
    await_sibling(0)
    load_copy(0).start()
    for copy in weight_copies:
        copy.wait()

    def step_body(step, carry):
        slot = step % 2
        layer_shift = step // lanes
        lane_shift = step % lanes
        load_copy(step).wait()

        @pl.when(step > 1)
        def _():
            for copy in store_copies(step - 2):
                copy.wait()

        logits_buf[slot] = dot_plain(rows_buf[slot], router_w[...])

        def hidden_rows(block, inner):
            rows = pl.ds(pl.multiple_of(block * row_block, row_block), row_block)
            here = rows_buf[slot, rows, :]
            for index, weight in ((0, gate_w), (1, up_w)):
                acts_buf[slot, index, rows, :] = dot_rows(here, weight[...]).astype(jnp.bfloat16)
            return inner

        lax.fori_loop(0, length // row_block, hidden_rows, 0)

        @pl.when(lane_shift == 0)
        def _():
            third_hop(layer_shift)

            @pl.when(layer_shift + 1 < layers)
            def _():
                first_hop(layer_shift + 1, True)

        @pl.when((lane_shift == lanes - 1) & (layer_shift + 1 < layers))
        def _():
            second_hop(layer_shift + 1)

        def shared_rows(block, inner):
            rows = pl.ds(pl.multiple_of(block * row_block, row_block), row_block)
            here = rows_buf[slot, rows, :]
            for index, weight in ((2, shared_gate_w), (3, shared_up_w)):
                acts_buf[slot, index, rows, :] = dot_rows(here, weight[...]).astype(jnp.bfloat16)
            return inner

        lax.fori_loop(0, length // row_block, shared_rows, 0)

        @pl.when(step + 1 < groups)
        def _():
            await_sibling(step + 1)
            load_copy(step + 1).start()

        for copy in store_copies(step):
            copy.start()
        return carry

    lax.fori_loop(0, groups, step_body, 0)

    for step in range(max(groups - 2, 0), groups):
        for copy in store_copies(step):
            copy.wait()
    for shift in range(1, layers):
        layer_spread(shift).wait_send()
    for layer_shift in range(layers):
        for shift in range(1, sides):
            side_spread(layer_shift, shift).wait_send()
        for lane_shift in range(lanes):
            if lane_shift > 0:
                lane_spread(layer_shift, lane_shift).wait_send()
                for shift in range(1, sides):
                    side_half_spread(layer_shift, lane_shift, shift).wait_send()
                    lane_half_spread(layer_shift, lane_shift, shift).wait_send()
            for shift in range(sides):
                core_spread(layer_shift, lane_shift, shift).wait_send()


def backward_kernel(
    cotangent_ref,
    acts_ref,
    logits_ref,
    gate_ref,
    up_ref,
    down_ref,
    shared_gate_ref,
    shared_up_ref,
    shared_down_ref,
    router_ref,
    residual_ref,
    gain_ref,
    expert_hidden_ref,
    expert_dpre_ref,
    expert_dlin_ref,
    shared_hidden_ref,
    shared_dpre_ref,
    shared_dlin_ref,
    spread_ref,
    result_ref,
    grad_residual_ref,
    logit_ref,
    gain_grad_ref,
    gate_w,
    up_w,
    down_w,
    shared_gate_w,
    shared_up_w,
    shared_down_w,
    router_w,
    cotangent_buf,
    acts_buf,
    logits_buf,
    codes_buf,
    units_buf,
    gate_grad_buf,
    sum_buf,
    core_land,
    side_land,
    lane_send,
    lane_land,
    block_land,
    block_send,
    block_side_land,
    layer_send,
    layer_land,
    cotangent_part,
    code_part,
    gates_part,
    part_buf,
    weight_sem,
    load_sem,
    store_sem,
    part_sem,
    core_sem,
    core_land_sem,
    side_sem,
    side_land_sem,
    lane_sem,
    lane_land_sem,
    block_sem,
    block_land_sem,
    block_side_sem,
    block_side_land_sem,
    layer_sem,
    layer_land_sem,
    own_sem,
    spread_side_sem,
    spread_core_sem,
    arrive_sem,
    *,
    groups,
    tensors,
    local_experts,
):
    place = Place(groups, tensors)
    sides, layers, lanes = place.sides, place.layers, place.lanes
    me, mine, core, side = place.me, place.mine, place.core, place.side
    length = cotangent_buf.shape[0]
    width = cotangent_buf.shape[1]
    part_rows = length // tensors
    hidden = gate_w.shape[0]
    own_width = hidden // local_experts
    row_block = min(256, length)
    column_block = min(512, width)
    first = pl.ds(0, width)
    second = pl.ds(width, width + LANES)
    marks = pl.ds(width, LANES)

    pairs = (
        (down_ref, down_w),
        (shared_down_ref, shared_down_w),
        (gate_ref, gate_w),
        (up_ref, up_w),
        (shared_gate_ref, shared_gate_w),
        (shared_up_ref, shared_up_w),
        (router_ref, router_w),
    )
    weight_copies = [
        pltpu.make_async_copy(source, target, weight_sem.at[index])
        for index, (source, target) in enumerate(pairs)
    ]

    def shifts_of(step):
        return (step // lanes + 1) % layers, lanes - 1 - step % lanes

    def sequence_of(step):
        layer_shift, lane_shift = shifts_of(step)
        return place.expert_of(layer_shift, lane_shift)

    def load_copies(step):
        sequence = sequence_of(step)
        return (
            pltpu.make_async_copy(
                cotangent_ref.at[sequence, :, first], cotangent_buf, load_sem.at[0]
            ),
            pltpu.make_async_copy(acts_ref.at[:, sequence], acts_buf, load_sem.at[1]),
            pltpu.make_async_copy(logits_ref.at[sequence], logits_buf, load_sem.at[2]),
            pltpu.make_async_copy(cotangent_ref.at[sequence, :, marks], codes_buf, load_sem.at[3]),
        )

    unit_refs = (
        expert_hidden_ref,
        expert_dpre_ref,
        expert_dlin_ref,
        shared_hidden_ref,
        shared_dpre_ref,
        shared_dlin_ref,
    )

    def store_copies(step):
        sequence = sequence_of(step)
        return [
            pltpu.make_async_copy(units_buf.at[index], ref.at[sequence], store_sem.at[index])
            for index, ref in enumerate(unit_refs)
        ]

    part_slice = pl.ds(pl.multiple_of(mine * part_rows, part_rows), part_rows)
    part_copies = (
        pltpu.make_async_copy(
            cotangent_ref.at[me, part_slice, first], cotangent_part, part_sem.at[0]
        ),
        pltpu.make_async_copy(cotangent_ref.at[me, part_slice, marks], code_part, part_sem.at[1]),
        pltpu.make_async_copy(logits_ref.at[me, part_slice, :], gates_part, part_sem.at[2]),
    )
    for copy in load_copies(0):
        copy.start()
    for copy in weight_copies:
        copy.start()
    for copy in part_copies:
        copy.start()
    barrier, count = place.greet(True)

    def core_send(step):
        slot = step % 2
        return remote(
            sum_buf.at[slot, :, 1 - core],
            core_land.at[slot],
            core_sem.at[slot],
            core_land_sem.at[slot],
            "tensor",
            place.sibling,
        )

    def side_copy(step, shift):
        slot = step % 2
        return remote(
            sum_buf.at[slot, place.side_of(shift), core, :, first],
            side_land.at[slot, shift - 1],
            side_sem.at[slot, shift - 1],
            side_land_sem.at[slot, shift - 1],
            "tensor",
            place.tensor_of(shift),
        )

    def lane_copy(turn, lane_shift):
        slot = turn % 2
        return remote(
            lane_send.at[slot, lane_shift - 1],
            lane_land.at[slot, lane_shift - 1],
            lane_sem.at[slot, lane_shift - 1],
            lane_land_sem.at[slot, lane_shift - 1],
            "expert",
            place.expert_of(0, lane_shift),
        )

    def block_copy(step, lane_shift):
        slot = step % 2
        turn_slot = (step // lanes) % 2
        return remote(
            sum_buf.at[slot, :, core, :, second],
            block_land.at[turn_slot, lane_shift - 1],
            block_sem.at[slot],
            block_land_sem.at[turn_slot, lane_shift - 1],
            "expert",
            place.expert_of(0, lane_shift),
        )

    def block_side_copy(turn, shift):
        slot = turn % 2
        return remote(
            block_send.at[slot, shift - 1],
            block_side_land.at[slot, shift - 1],
            block_side_sem.at[slot, shift - 1],
            block_side_land_sem.at[slot, shift - 1],
            "tensor",
            place.tensor_of(shift),
        )

    def layer_copy(turn):
        slot = turn % 2
        return remote(
            layer_send.at[slot],
            layer_land.at[turn],
            layer_sem.at[slot],
            layer_land_sem.at[turn],
            "expert",
            place.expert_of((turn + 1) % layers, 0),
        )

    def per_lane(lane_shift, act):
        for value in range(1, lanes):

            @pl.when(lane_shift == value)
            def _():
                act(value)

    def combine_cores(step):
        slot = step % 2
        _, lane_shift = shifts_of(step)
        copy = core_send(step)
        copy.wait_recv()
        copy.wait_send()
        for shift in range(sides):
            other = place.side_of(shift)
            sum_buf[slot, other, core] = (
                sum_buf[slot, other, core].astype(jnp.float32)
                + core_land[slot, other].astype(jnp.float32)
            ).astype(jnp.bfloat16)
            if shift > 0:
                side_copy(step, shift).start()
        per_lane(lane_shift, lambda value: block_copy(step, value).start())

    def combine_sides(step):
        slot = step % 2
        turn = step // lanes
        _, lane_shift = shifts_of(step)
        total = sum_buf[slot, side, core, :, first].astype(jnp.float32)
        for shift in range(1, sides):
            side_copy(step, shift).wait_recv()
            side_copy(step, shift).wait_send()
            total = total + side_land[slot, shift - 1].astype(jnp.float32)
        total = total.astype(jnp.bfloat16)

        def pass_on(value):
            block_copy(step, value).wait_send()

            @pl.when(turn >= 2)
            def _():
                lane_copy(turn - 2, value).wait_send()

            lane_send[turn % 2, value - 1] = total
            lane_copy(turn, value).start()

        per_lane(lane_shift, pass_on)

        @pl.when(lane_shift == 0)
        def _():
            turn_slot = turn % 2

            @pl.when(turn >= 2)
            def _():
                layer_copy(turn - 2).wait_send()
                for shift in range(1, sides):
                    block_side_copy(turn - 2, shift).wait_send()

            layer_send[turn_slot, :, first] = total
            for value in range(1, lanes):
                block_copy(step, value).wait_recv()
            for shift in range(sides):
                other = place.side_of(shift)
                block = sum_buf[slot, other, core, :, second].astype(jnp.float32)
                for value in range(1, lanes):
                    block = block + block_land[turn_slot, value - 1, other].astype(jnp.float32)
                block = block.astype(jnp.bfloat16)
                if shift == 0:
                    layer_send[turn_slot, :, second] = block
                else:
                    block_send[turn_slot, shift - 1] = block
                    block_side_copy(turn, shift).start()

    def turn_total(turn):
        slot = turn % 2
        branch = layer_send[slot, :, first].astype(jnp.float32)
        for value in range(1, lanes):
            lane_copy(turn, value).wait_recv()
            branch = branch + lane_land[slot, value - 1].astype(jnp.float32)
        block = layer_send[slot, :, second].astype(jnp.float32)
        for shift in range(1, sides):
            block_side_copy(turn, shift).wait_recv()
            block = block + block_side_land[slot, shift - 1].astype(jnp.float32)
        return branch, block

    def combine_lanes(step):
        turn = step // lanes
        _, lane_shift = shifts_of(step)

        @pl.when(lane_shift == 0)
        def _():
            slot = turn % 2
            branch, block = turn_total(turn)
            layer_send[slot, :, first] = branch.astype(jnp.bfloat16)
            layer_send[slot, :, second] = block.astype(jnp.bfloat16)
            layer_copy(turn).start()

    for copy in weight_copies[:2]:
        copy.wait()
    for copy in part_copies:
        copy.wait()
    pl.semaphore_wait(barrier, count)

    def softmax_named(logits, code):
        named = code > 0.5
        highest = jnp.max(jnp.where(named, logits, -jnp.inf), axis=1, keepdims=True)
        raised = jnp.where(named, jnp.exp(logits - highest), 0.0)
        return raised / jnp.sum(raised, axis=1, keepdims=True)

    def services(step):
        @pl.when((step >= 3) & (step < groups + 2))
        def _():
            combine_lanes(step - 3)

        @pl.when((step >= 2) & (step < groups + 2))
        def _():
            combine_sides(step - 2)

        @pl.when((step >= 1) & (step < groups + 1))
        def _():
            combine_cores(step - 1)

    def step_body(step, carry):
        slot = step % 2
        running = step < groups

        @pl.when(running)
        def _():
            for copy in load_copies(step):
                copy.wait()

            @pl.when(step > 0)
            def _():
                for copy in store_copies(step - 1):
                    copy.wait()

            def hidden_rows(block, inner):
                rows = pl.ds(pl.multiple_of(block * row_block, row_block), row_block)
                back = cotangent_buf[rows, :]
                dhid = dot_rows(back, down_w[...])
                code = codes_buf[rows, :].astype(jnp.float32)
                lane = lax.broadcasted_iota(jnp.int32, code.shape, 1)
                gates = softmax_named(logits_buf[rows, :], code)
                gates = jnp.where(code > 1.5, gates, 0.0)
                pre = acts_buf[0, rows, :].astype(jnp.float32)
                lin = acts_buf[1, rows, :].astype(jnp.float32)
                unit = lax.broadcasted_iota(jnp.int32, pre.shape, 1)
                gate = None
                for member in range(local_experts):
                    chosen = jnp.sum(
                        jnp.where(lane == me * local_experts + member, gates, 0.0),
                        axis=1,
                        keepdims=True,
                    )
                    gate = (
                        jnp.broadcast_to(chosen, pre.shape)
                        if gate is None
                        else jnp.where(unit >= member * own_width, chosen, gate)
                    )
                sigmoid = jax.nn.sigmoid(pre)
                active = pre * sigmoid
                hid = active * lin
                product = hid * dhid
                units_buf[0, rows, :] = (hid * gate).astype(jnp.bfloat16)
                dhid = dhid * gate
                units_buf[1, rows, :] = (dhid * lin * (sigmoid + active * (1.0 - sigmoid))).astype(
                    jnp.bfloat16
                )
                units_buf[2, rows, :] = (dhid * active).astype(jnp.bfloat16)
                gate_grad = jnp.zeros(code.shape, jnp.float32)
                for member in range(local_experts):
                    inside = (unit >= member * own_width) & (unit < (member + 1) * own_width)
                    gate_grad = jnp.where(
                        lane == me * local_experts + member,
                        jnp.sum(jnp.where(inside, product, 0.0), axis=1, keepdims=True),
                        gate_grad,
                    )
                gate_grad_buf[rows, :] = gate_grad
                return inner

            lax.fori_loop(0, length // row_block, hidden_rows, 0)

            def shared_rows(block, inner):
                rows = pl.ds(pl.multiple_of(block * row_block, row_block), row_block)
                dhid = dot_rows(cotangent_buf[rows, :], shared_down_w[...])
                pre = acts_buf[2, rows, :].astype(jnp.float32)
                lin = acts_buf[3, rows, :].astype(jnp.float32)
                sigmoid = jax.nn.sigmoid(pre)
                active = pre * sigmoid
                units_buf[3, rows, :] = (active * lin).astype(jnp.bfloat16)
                units_buf[4, rows, :] = (dhid * lin * (sigmoid + active * (1.0 - sigmoid))).astype(
                    jnp.bfloat16
                )
                units_buf[5, rows, :] = (dhid * active).astype(jnp.bfloat16)
                return inner

            lax.fori_loop(0, length // row_block, shared_rows, 0)

            @pl.when(step + 1 < groups)
            def _():
                for copy in load_copies(step + 1):
                    copy.start()

            @pl.when(step == 0)
            def _():
                for copy in weight_copies[2:]:
                    copy.wait()

        services(step)

        @pl.when(running)
        def _():
            def mix_columns(block, inner):
                start = pl.multiple_of(block * column_block, column_block)
                columns = pl.ds(start, column_block)
                moved = pl.ds(pl.multiple_of(width + start, column_block), column_block)
                sum_buf[slot, :, :, :, columns] = (
                    dot_plain(units_buf[0], down_w[:, columns])
                    .astype(jnp.bfloat16)
                    .reshape(sides, 2, part_rows, column_block)
                )
                total = dot_plain(units_buf[1], gate_w[:, columns]) + dot_plain(
                    units_buf[2], up_w[:, columns]
                )
                sum_buf[slot, :, :, :, moved] = total.astype(jnp.bfloat16).reshape(
                    sides, 2, part_rows, column_block
                )
                return inner

            lax.fori_loop(0, width // column_block, mix_columns, 0)

            @pl.when(step == groups - 1)
            def _():
                def mix_shared(block, inner):
                    start = pl.multiple_of(block * column_block, column_block)
                    columns = pl.ds(start, column_block)
                    moved = pl.ds(pl.multiple_of(width + start, column_block), column_block)
                    for target, total in (
                        (columns, dot_plain(units_buf[3], shared_down_w[:, columns])),
                        (
                            moved,
                            dot_plain(units_buf[4], shared_gate_w[:, columns])
                            + dot_plain(units_buf[5], shared_up_w[:, columns]),
                        ),
                    ):
                        sum_buf[slot, :, :, :, target] = (
                            sum_buf[slot, :, :, :, target].astype(jnp.float32)
                            + total.reshape(sides, 2, part_rows, column_block)
                        ).astype(jnp.bfloat16)
                    return inner

                lax.fori_loop(0, width // column_block, mix_shared, 0)

            sum_buf[slot, :, :, :, pl.ds(2 * width, LANES)] = (
                gate_grad_buf[...].astype(jnp.bfloat16).reshape(sides, 2, part_rows, LANES)
            )
            core_send(step).start()
            for copy in store_copies(step):
                copy.start()

        return carry

    lax.fori_loop(0, groups + 2, step_body, 0)

    last = layers - 1
    last_slot = last % 2
    for value in range(1, lanes):
        lane_copy(last, value).wait_recv()
    for shift in range(1, sides):
        block_side_copy(last, shift).wait_recv()
    for turn in range(last):
        layer_copy(turn).wait_recv()
    gain_grad_ref[...] = jnp.zeros_like(gain_grad_ref)
    few_rows = min(32, part_rows)

    def finish_rows(index, inner):
        rows = pl.ds(pl.multiple_of(index * few_rows, few_rows), few_rows)
        branch = layer_send[last_slot, rows, first].astype(jnp.float32)
        for value in range(1, lanes):
            branch = branch + lane_land[last_slot, value - 1, rows, :].astype(jnp.float32)
        block = layer_send[last_slot, rows, second].astype(jnp.float32)
        for shift in range(1, sides):
            block = block + block_side_land[last_slot, shift - 1, rows, :].astype(jnp.float32)
        for turn in range(last):
            branch = branch + layer_land[turn, rows, first].astype(jnp.float32)
            block = block + layer_land[turn, rows, second].astype(jnp.float32)
        residual = residual_ref[rows, :]
        result_ref[rows, :] = (residual + branch).astype(jnp.bfloat16)

        code = code_part[rows, :].astype(jnp.float32)
        gates = softmax_named(gates_part[rows, :], code)
        gate_grad = jnp.where(code > 1.5, block[:, width:], 0.0)
        logit = (
            gates * (gate_grad - jnp.sum(gates * gate_grad, axis=1, keepdims=True))
        ).astype(jnp.bfloat16)
        logit_ref[rows, :] = logit
        upstream = block[:, :width] + dot_rows(logit, router_w[...])
        factor = lax.rsqrt(jnp.mean(residual * residual, axis=1, keepdims=True) + EPS)
        unit_rows = residual * factor
        scaled = upstream * gain_ref[...]
        inner_mean = jnp.mean(scaled * unit_rows, axis=1, keepdims=True)
        gain_grad_ref[...] += jnp.sum(upstream * unit_rows, axis=0, keepdims=True)
        grad_residual = cotangent_part[rows, :].astype(jnp.float32) + factor * (
            scaled - unit_rows * inner_mean
        )
        grad_residual_ref[rows, :] = grad_residual
        part_buf[rows, :] = grad_residual.astype(jnp.bfloat16)
        return inner

    lax.fori_loop(0, part_rows // few_rows, finish_rows, 0)
    spread_over_tensor(
        place, part_buf, spread_ref, (own_sem, spread_side_sem, spread_core_sem, arrive_sem)
    )

    for copy in store_copies(groups - 1):
        copy.wait()
    for turn in range(max(layers - 2, 0), layers):
        for value in range(1, lanes):
            lane_copy(turn, value).wait_send()
        for shift in range(1, sides):
            block_side_copy(turn, shift).wait_send()
    layer_copy(last - 1).wait_send()


ANYWHERE = pl.BlockSpec(memory_space=pl.ANY)
IN_VMEM = pl.BlockSpec(memory_space=pltpu.VMEM)


def run_forward(attention, inputs, gain, weights, router_padded):
    groups = lax.axis_size("expert")
    tensors = lax.axis_size("tensor")
    sides = tensors // 2
    layers = min(LAYERS, groups)
    lanes = groups // layers
    length, width = inputs.shape
    part_rows = length // tensors
    hidden = weights[0].shape[0]
    bf16 = jnp.bfloat16
    f32 = jnp.float32
    dma = pltpu.SemaphoreType.DMA
    block = pltpu.VMEM((hidden, width), bf16)
    return pl.pallas_call(
        functools.partial(forward_kernel, groups=groups, tensors=tensors),
        out_shape=(
            jax.ShapeDtypeStruct((groups, length, width), bf16),
            jax.ShapeDtypeStruct((4, groups, length, hidden), bf16),
            jax.ShapeDtypeStruct((groups, length, LANES), f32),
            jax.ShapeDtypeStruct((part_rows, width), f32),
        ),
        in_specs=[ANYWHERE, ANYWHERE, IN_VMEM] + [ANYWHERE] * 5,
        out_specs=(ANYWHERE,) * 3 + (IN_VMEM,),
        scratch_shapes=[block] * 4
        + [
            pltpu.VMEM((width, LANES), bf16),
            pltpu.VMEM((sides, 2, part_rows, width), bf16),
            pltpu.VMEM((sides, part_rows, width), bf16),
            pltpu.VMEM((sides - 1, part_rows, width), bf16),
            pltpu.VMEM((sides - 1, part_rows, width), bf16),
            pltpu.VMEM((part_rows, width), bf16),
            pltpu.VMEM((part_rows, width), bf16),
            pltpu.VMEM((2, length, width), bf16),
            pltpu.VMEM((2, length, LANES), f32),
            pltpu.VMEM((2, 4, length, hidden), bf16),
            dma((5,)),
            dma((3,)),
            dma((2,)),
            dma((2, 2)),
            dma(()),
            dma(()),
            dma((sides - 1,)),
            dma((sides - 1,)),
            dma((layers,)),
            dma((layers,)),
            dma((layers, lanes)),
            dma((layers, lanes)),
            dma((layers, sides)),
            dma((layers, sides)),
            dma((layers, lanes, sides)),
            dma((layers, lanes, sides)),
            dma((layers, lanes, sides)),
            dma((layers, lanes, sides)),
            dma((layers, lanes, sides)),
            dma((layers, lanes, sides)),
        ],
        compiler_params=pltpu.CompilerParams(
            collective_id=1, has_side_effects=True, vmem_limit_bytes=60 * 1024 * 1024
        ),
        cost_estimate=pl.CostEstimate(
            flops=8 * groups * length * width * hidden,
            bytes_accessed=100_000_000,
            transcendentals=0,
        ),
        name="experts_forward",
    )(
        attention.reshape(sides, 2, part_rows, width),
        inputs,
        gain.reshape(1, width),
        *weights,
        router_padded,
    )


def run_backward(
    cotangent_all, acts, logits, weights, router_padded, residual, gain, local_experts
):
    groups = lax.axis_size("expert")
    tensors = lax.axis_size("tensor")
    sides = tensors // 2
    layers = min(LAYERS, groups)
    lanes = groups // layers
    part_rows, width = residual.shape
    length = part_rows * tensors
    hidden = weights[0].shape[0]
    second = width + LANES
    packed = width + second
    bf16 = jnp.bfloat16
    f32 = jnp.float32
    dma = pltpu.SemaphoreType.DMA
    block = pltpu.VMEM((hidden, width), bf16)
    units = jax.ShapeDtypeStruct((groups, length, hidden), bf16)
    return pl.pallas_call(
        functools.partial(
            backward_kernel, groups=groups, tensors=tensors, local_experts=local_experts
        ),
        out_shape=(units,) * 6
        + (
            jax.ShapeDtypeStruct((tensors, part_rows, width), bf16),
            jax.ShapeDtypeStruct((part_rows, width), bf16),
            jax.ShapeDtypeStruct((part_rows, width), f32),
            jax.ShapeDtypeStruct((part_rows, LANES), bf16),
            jax.ShapeDtypeStruct((1, width), f32),
        ),
        in_specs=[ANYWHERE] * 10 + [IN_VMEM] * 2,
        out_specs=(ANYWHERE,) * 7 + (IN_VMEM,) * 4,
        scratch_shapes=[block] * 6
        + [
            pltpu.VMEM((width, LANES), bf16),
            pltpu.VMEM((length, width), bf16),
            pltpu.VMEM((4, length, hidden), bf16),
            pltpu.VMEM((length, LANES), f32),
            pltpu.VMEM((length, LANES), bf16),
            pltpu.VMEM((6, length, hidden), bf16),
            pltpu.VMEM((length, LANES), f32),
            pltpu.VMEM((2, sides, 2, part_rows, packed), bf16),
            pltpu.VMEM((2, sides, part_rows, packed), bf16),
            pltpu.VMEM((2, sides - 1, part_rows, width), bf16),
            pltpu.VMEM((2, lanes - 1, part_rows, width), bf16),
            pltpu.VMEM((2, lanes - 1, part_rows, width), bf16),
            pltpu.VMEM((2, lanes - 1, sides, part_rows, second), bf16),
            pltpu.VMEM((2, sides - 1, part_rows, second), bf16),
            pltpu.VMEM((2, sides - 1, part_rows, second), bf16),
            pltpu.VMEM((2, part_rows, packed), bf16),
            pltpu.VMEM((layers - 1, part_rows, packed), bf16),
            pltpu.VMEM((part_rows, width), bf16),
            pltpu.VMEM((part_rows, LANES), bf16),
            pltpu.VMEM((part_rows, LANES), f32),
            pltpu.VMEM((part_rows, width), bf16),
            dma((7,)),
            dma((4,)),
            dma((6,)),
            dma((3,)),
            dma((2,)),
            dma((2,)),
            dma((2, sides - 1)),
            dma((2, sides - 1)),
            dma((2, lanes - 1)),
            dma((2, lanes - 1)),
            dma((2,)),
            dma((2, lanes - 1)),
            dma((2, sides - 1)),
            dma((2, sides - 1)),
            dma((2,)),
            dma((layers - 1,)),
            dma(()),
            dma((sides,)),
            dma((sides,)),
            dma((tensors,)),
        ],
        compiler_params=pltpu.CompilerParams(
            collective_id=2, has_side_effects=True, vmem_limit_bytes=60 * 1024 * 1024
        ),
        cost_estimate=pl.CostEstimate(
            flops=10 * groups * length * width * hidden,
            bytes_accessed=100_000_000,
            transcendentals=0,
        ),
        name="experts_backward",
    )(
        cotangent_all.reshape(groups, length, width + LANES),
        acts,
        logits,
        *weights,
        router_padded,
        residual,
        gain.reshape(1, width),
    )


def weight_kernel(
    query_ref,
    latent_ref,
    out_ref,
    rest_ref,
    first_ref,
    residual_ref,
    inputs_ref,
    gain_ref,
    units_0,
    units_1,
    units_2,
    units_3,
    units_4,
    units_5,
    rows_ref,
    cotangent_ref,
    query_sum,
    latent_sum,
    out_sum,
    rest_spread,
    first_spread,
    grad_0,
    grad_1,
    grad_2,
    grad_3,
    grad_4,
    grad_5,
    query_own,
    latent_own,
    out_own,
    rest_own,
    query_lane,
    latent_lane,
    out_lane,
    rest_lane,
    query_layer,
    latent_layer,
    out_layer,
    rest_layer,
    rest_part,
    rest_block,
    first_core_land,
    first_send,
    first_land,
    first_part,
    sum_core_land,
    sum_send,
    sum_land,
    units_buf,
    turned_buf,
    rows_buf,
    grad_buf,
    own_sem,
    lane_sem,
    lane_land_sem,
    layer_sem,
    layer_land_sem,
    units_sem,
    rows_sem,
    grad_sem,
    spread_own_sem,
    spread_side_sem,
    spread_core_sem,
    arrive_sem,
    tensor_core_sem,
    tensor_core_land_sem,
    tensor_side_sem,
    tensor_side_land_sem,
    first_own_sem,
    first_side_sem,
    first_core_sem,
    first_arrive_sem,
    *,
    groups,
    tensors,
):
    place = Place(groups, tensors)
    layers, lanes = place.layers, place.lanes
    sides = place.sides
    columns = rest_part.shape[1]
    tokens = units_buf.shape[1]
    width = rows_ref.shape[1]
    column_block = rows_buf.shape[2]
    barrier, count = place.greet(True)

    sums = (query_sum, latent_sum, out_sum, None)
    owns = (query_own, latent_own, out_own, rest_own)
    lane_lands = (query_lane, latent_lane, out_lane, rest_lane)
    layer_lands = (query_layer, latent_layer, out_layer, rest_layer)

    def share(index, expert):
        if index == 0:
            return query_ref.at[expert]
        if index == 1:
            return latent_ref.at[expert]
        part = pl.ds(pl.multiple_of(expert * columns, columns), columns)
        return (out_ref if index == 2 else rest_block).at[:, part]

    def own_copies(turn, indices=range(4)):
        return [
            pltpu.make_async_copy(
                share(index, place.expert_of((turn + 1) % layers, 0)),
                owns[index].at[turn],
                own_sem.at[turn, index],
            )
            for index in indices
        ]

    def lane_copies(turn, indices=range(4)):
        return [
            remote(
                share(index, place.expert_of((turn + 1) % layers, shift)),
                lane_lands[index].at[turn, shift - 1],
                lane_sem.at[turn, shift - 1, index],
                lane_land_sem.at[turn, shift - 1, index],
                "expert",
                place.expert_of(0, shift),
            )
            for shift in range(1, lanes)
            for index in indices
        ]

    def layer_copies(turn, indices=range(4)):
        return [
            remote(
                owns[index].at[turn],
                layer_lands[index].at[turn],
                layer_sem.at[turn, index],
                layer_land_sem.at[turn, index],
                "expert",
                place.expert_of((turn + 1) % layers, 0),
            )
            for index in indices
        ]

    def lane_total(turn, index):
        total = owns[index][turn].astype(jnp.float32)
        for shift in range(1, lanes):
            total = total + lane_lands[index][turn, shift - 1].astype(jnp.float32)
        return total

    def combine(turn, indices=range(4)):
        for copy in own_copies(turn, indices):
            copy.wait()
        for copy in lane_copies(turn, indices):
            copy.wait_recv()
        if turn < layers - 1:
            for index, copy in zip(indices, layer_copies(turn, indices)):
                owns[index][turn] = lane_total(turn, index).astype(jnp.bfloat16)
                copy.start()

    units = (units_0, units_1, units_2, units_3, units_4, units_5)
    grads = (grad_0, grad_1, grad_2, grad_3, grad_4, grad_5)
    sources = (rows_ref, rows_ref, cotangent_ref, rows_ref, rows_ref, cotangent_ref)

    def units_copy(index):
        return pltpu.make_async_copy(units[index], units_buf.at[index % 2], units_sem.at[index % 2])

    def rows_copy(index, block, slot):
        if index < 3:
            start = pl.multiple_of(block * column_block, column_block)
            part = pl.ds(start, column_block)
            target = rows_buf.at[slot]
        else:
            part = pl.ds(pl.multiple_of(place.me * columns, columns), columns)
            target = rows_buf.at[slot, :, pl.ds(0, columns)]
        return pltpu.make_async_copy(sources[index].at[:, part], target, rows_sem.at[slot])

    def grad_copy(index, block, slot):
        if index < 3:
            start = pl.multiple_of(block * column_block, column_block)
            return pltpu.make_async_copy(
                grad_buf.at[slot], grads[index].at[:, pl.ds(start, column_block)], grad_sem.at[slot]
            )
        return pltpu.make_async_copy(
            grad_buf.at[slot, :, pl.ds(0, columns)], grads[index], grad_sem.at[slot]
        )

    turn_rows = min(512, tokens)

    def turn_units(index):
        units_copy(index).wait()

        def body(block, inner):
            rows = pl.ds(pl.multiple_of(block * turn_rows, turn_rows), turn_rows)
            turned_buf[:, rows] = units_buf[index % 2, rows, :].T
            return inner

        lax.fori_loop(0, tokens // turn_rows, body, 0)
        if index + 2 < 6:
            units_copy(index + 2).start()

    blocks = width // column_block

    def routed(index):
        rows_copy(index, 0, 0).start()
        turn_units(index)

        def body(block, inner):
            slot = block % 2

            @pl.when(block + 1 < blocks)
            def _():
                rows_copy(index, block + 1, 1 - slot).start()

            rows_copy(index, block, slot).wait()

            @pl.when(block >= 2)
            def _():
                grad_copy(index, block - 2, slot).wait()

            grad_buf[slot] = dot_plain(turned_buf[...], rows_buf[slot])
            grad_copy(index, block, slot).start()
            return inner

        lax.fori_loop(0, blocks, body, 0)
        for block in range(max(blocks - 2, 0), blocks):
            grad_copy(index, block, block % 2).wait()

    def shared(index):
        slot = index % 2
        rows_copy(index, 0, slot).start()
        turn_units(index)
        rows_copy(index, 0, slot).wait()
        part = pl.ds(0, columns)
        grad_buf[slot, :, part] = dot_plain(turned_buf[...], rows_buf[slot, :, part])
        grad_copy(index, 0, slot).start()
        grad_copy(index, 0, slot).wait()

    tensor_sums = (
        (first_ref, first_core_land, first_send, first_land),
        (rest_ref, sum_core_land, sum_send, sum_land),
    )

    def core_exchange(which):
        source, land, _, _ = tensor_sums[which]
        return remote(
            source.at[:, 1 - place.core],
            land,
            tensor_core_sem.at[which],
            tensor_core_land_sem.at[which],
            "tensor",
            place.sibling,
        )

    def side_exchange(which, shift):
        _, _, send, land = tensor_sums[which]
        return remote(
            send.at[shift - 1],
            land.at[shift - 1],
            tensor_side_sem.at[which, shift - 1],
            tensor_side_land_sem.at[which, shift - 1],
            "tensor",
            place.tensor_of(shift),
        )

    def core_sum(which, other):
        source, land, _, _ = tensor_sums[which]
        return source[other, place.core].astype(jnp.float32) + land[other].astype(jnp.float32)

    def send_sides(which):
        core_exchange(which).wait_recv()
        for shift in range(1, sides):
            tensor_sums[which][2][shift - 1] = core_sum(which, place.side_of(shift)).astype(
                jnp.bfloat16
            )
            side_exchange(which, shift).start()

    def tensor_total(which):
        total = core_sum(which, place.side)
        for shift in range(1, sides):
            side_exchange(which, shift).wait_recv()
            total = total + tensor_sums[which][3][shift - 1].astype(jnp.float32)
        return total

    first_own = pltpu.make_async_copy(first_part, first_spread.at[place.mine], first_own_sem)

    def first_piece(tensor):
        return first_spread.at[tensor]

    def first_copy(view, sem, tensor, target):
        return remote(
            view, first_piece(tensor), sem, first_arrive_sem.at[tensor], "tensor", target
        )

    first_sends = [
        first_copy(first_part, first_side_sem.at[shift], place.mine, place.tensor_of(shift))
        for shift in range(1, sides)
    ]
    first_sends.append(
        first_copy(first_part, first_core_sem.at[0], place.mine, place.sibling)
    )
    first_forwards = [
        first_copy(
            first_piece(place.tensor_of(shift)),
            first_core_sem.at[shift],
            place.tensor_of(shift),
            place.sibling,
        )
        for shift in range(1, sides)
    ]

    def await_first(tensor):
        view = first_piece(tensor)
        pltpu.make_async_copy(view, view, first_arrive_sem.at[tensor]).wait()

    def finish_first():
        upstream = tensor_total(0)
        rows = inputs_ref[...].astype(jnp.float32)
        factor = lax.rsqrt(jnp.mean(rows * rows, axis=1, keepdims=True) + EPS)
        unit_rows = rows * factor
        scaled = upstream * gain_ref[...]
        inner_mean = jnp.mean(scaled * unit_rows, axis=1, keepdims=True)
        first_part[...] = (
            residual_ref[...] + factor * (scaled - unit_rows * inner_mean)
        ).astype(jnp.bfloat16)
        first_own.start()
        for copy in first_sends:
            copy.start()
        gain_grad = jnp.sum(upstream * unit_rows, axis=0, keepdims=True)
        summed_rows = rest_block.shape[0] - 16
        rest_block[pl.ds(0, summed_rows), :] = tensor_total(1).astype(jnp.bfloat16)
        row = lax.broadcasted_iota(jnp.int32, (16, width), 0)
        rest_block[pl.ds(summed_rows, 16), :] = jnp.where(row == 0, gain_grad, 0.0).astype(
            jnp.bfloat16
        )
        for turn in range(layers):
            for copy in lane_copies(turn, (3,)) + own_copies(turn, (3,)):
                copy.start()

    def forward_first():
        for shift in range(1, sides):
            await_first(place.tensor_of(shift))
            first_forwards[shift - 1].start()

    units_copy(0).start()
    units_copy(1).start()
    pl.semaphore_wait(barrier, count)
    for which in range(2):
        core_exchange(which).start()
    for turn in range(layers):
        for copy in lane_copies(turn, range(3)) + own_copies(turn, range(3)):
            copy.start()
    for which in range(2):
        send_sides(which)
    routed(0)
    combine(0, range(3))
    finish_first()
    routed(1)
    if layers > 2:
        combine(1, range(3))
    forward_first()
    routed(2)
    for turn in range(2, layers - 1):
        combine(turn, range(3))
    for turn in range(layers - 1):
        combine(turn, (3,))
    for index in range(3, 6):
        shared(index)
    combine(layers - 1)

    last = layers - 1
    for turn in range(last):
        for copy in layer_copies(turn):
            copy.wait_recv()
    for index in range(4):
        total = lane_total(last, index)
        for turn in range(last):
            total = total + layer_lands[index][turn].astype(jnp.float32)
        if index < 3:
            sums[index][...] = total
        else:
            rest_part[...] = total.astype(jnp.bfloat16)
    spread_over_tensor(
        place,
        rest_part,
        rest_spread,
        (spread_own_sem, spread_side_sem, spread_core_sem, arrive_sem),
    )
    for shift in range(sides):
        await_first(place.side_of(shift) * 2 + (1 - place.core))
    first_own.wait()
    for copy in first_sends + first_forwards:
        copy.wait_send()
    for which in range(2):
        core_exchange(which).wait_send()
        for shift in range(1, sides):
            side_exchange(which, shift).wait_send()
    for turn in range(layers):
        for copy in lane_copies(turn):
            copy.wait_send()
        if turn < last:
            for copy in layer_copies(turn):
                copy.wait_send()


def run_weights(
    query, latent, out, rest, first, residual, inputs_part, gain, units, rows, cotangent
):
    groups = lax.axis_size("expert")
    tensors = lax.axis_size("tensor")
    layers = min(LAYERS, groups)
    lanes = groups // layers
    sides = tensors // 2
    part_rows = residual.shape[0]
    rest_rows = rest.shape[0] // tensors
    tokens, width = rows.shape
    hidden = units[0].shape[1]
    columns = width // groups
    column_block = min(256, width)
    bf16 = jnp.bfloat16
    f32 = jnp.float32
    dma = pltpu.SemaphoreType.DMA
    query = query.reshape(groups, query.shape[0] // groups, query.shape[1])
    latent = latent.reshape(groups, latent.shape[0] // groups, latent.shape[1])
    shapes = (
        query.shape[1:],
        latent.shape[1:],
        (out.shape[0], columns),
        (rest_rows + 16, columns),
    )
    routed = jax.ShapeDtypeStruct((hidden, width), f32)
    shared = jax.ShapeDtypeStruct((hidden, columns), f32)
    return pl.pallas_call(
        functools.partial(weight_kernel, groups=groups, tensors=tensors),
        out_shape=tuple(jax.ShapeDtypeStruct(shape, f32) for shape in shapes[:3])
        + (jax.ShapeDtypeStruct((tensors,) + shapes[3], bf16),)
        + (jax.ShapeDtypeStruct((tensors, part_rows, width), bf16),)
        + (routed,) * 3
        + (shared,) * 3,
        in_specs=[ANYWHERE] * 3 + [IN_VMEM] * 5 + [ANYWHERE] * 8,
        out_specs=(IN_VMEM,) * 3 + (ANYWHERE,) * 8,
        scratch_shapes=[pltpu.VMEM((layers,) + shape, bf16) for shape in shapes]
        + [pltpu.VMEM((layers, lanes - 1) + shape, bf16) for shape in shapes]
        + [pltpu.VMEM((layers - 1,) + shape, bf16) for shape in shapes]
        + [
            pltpu.VMEM(shapes[3], bf16),
            pltpu.VMEM((rest_rows + 16, width), bf16),
            pltpu.VMEM((sides, part_rows, width), bf16),
            pltpu.VMEM((sides - 1, part_rows, width), bf16),
            pltpu.VMEM((sides - 1, part_rows, width), bf16),
            pltpu.VMEM((part_rows, width), bf16),
            pltpu.VMEM((sides, rest_rows, width), bf16),
            pltpu.VMEM((sides - 1, rest_rows, width), bf16),
            pltpu.VMEM((sides - 1, rest_rows, width), bf16),
            pltpu.VMEM((2, tokens, hidden), bf16),
            pltpu.VMEM((hidden, tokens), bf16),
            pltpu.VMEM((2, tokens, column_block), bf16),
            pltpu.VMEM((2, hidden, column_block), f32),
            dma((layers, 4)),
            dma((layers, lanes - 1, 4)),
            dma((layers, lanes - 1, 4)),
            dma((layers - 1, 4)),
            dma((layers - 1, 4)),
            dma((2,)),
            dma((2,)),
            dma((2,)),
            dma(()),
            dma((sides,)),
            dma((sides,)),
            dma((tensors,)),
            dma((2,)),
            dma((2,)),
            dma((2, sides - 1)),
            dma((2, sides - 1)),
            dma(()),
            dma((sides,)),
            dma((sides,)),
            dma((tensors,)),
        ],
        compiler_params=pltpu.CompilerParams(
            collective_id=4, has_side_effects=True, vmem_limit_bytes=60 * 1024 * 1024
        ),
        cost_estimate=pl.CostEstimate(
            flops=7 * tokens * width * hidden, bytes_accessed=100_000_000, transcendentals=0
        ),
        name="weights",
    )(
        query,
        latent,
        out,
        rest.reshape(sides, 2, rest_rows, width),
        first.reshape(sides, 2, part_rows, width),
        residual,
        inputs_part,
        gain.reshape(1, width),
        *units,
        rows,
        cotangent,
    )


def on_device(
    inputs,
    cotangent,
    positions,
    routes,
    slot_index,
    attention_gain,
    feedforward_gain,
    latent_gain,
    query_weight,
    latent_down,
    latent_up,
    out_weight,
    router_weight,
    shared_gate,
    shared_up,
    shared_down,
    expert_gate,
    expert_up,
    expert_down,
):
    length, model_width = inputs.shape
    tensor_count = lax.axis_size("tensor")
    group_count = lax.axis_size("expert")
    tensor_index = lax.axis_index("tensor")
    group_index = lax.axis_index("expert")
    head_width = NOPE + ROPE
    local_heads = query_weight.shape[1] // head_width
    local_experts, _, expert_hidden_width = expert_gate.shape
    shared_width = shared_gate.shape[1]
    experts_all = local_experts * group_count
    capacity = max(
        tensor_count, length * TOP * 4 // (3 * experts_all) // tensor_count * tensor_count
    )
    score_scale = 1.0 / math.sqrt(head_width)
    part_rows = length // tensor_count
    part_start = tensor_index * part_rows
    shard_columns = model_width // group_count

    def own_part(rows):
        return lax.dynamic_slice_in_dim(rows, part_start, part_rows, 0)

    def own_sequence(rows):
        return lax.dynamic_slice_in_dim(rows, group_index * length, length, 0)

    def own_columns(rows):
        return lax.dynamic_slice_in_dim(rows, group_index * shard_columns, shard_columns, 1)

    marks = expert_table(routes, jnp.where(slot_index < capacity, 2.0, 1.0), LANES)
    cotangent_all = gather_rows(
        jnp.concatenate([own_part(cotangent), own_part(marks).astype(jnp.bfloat16)], axis=1)
    )

    rows_in = inputs.astype(jnp.float32)
    normed_one, unit_one, factor_one = normalize(rows_in, attention_gain)
    first_norm = normed_one.astype(jnp.bfloat16)
    cosine, sine_table = rope_tables(positions)
    query_raw = plain_dot(first_norm, query_weight).reshape(length, local_heads, head_width)
    queries = jnp.concatenate(
        [
            query_raw[..., :NOPE],
            rotate(query_raw[..., NOPE:], cosine[:, None], sine_table[:, None]),
        ],
        axis=-1,
    ).astype(jnp.bfloat16)
    latent_raw = plain_dot(first_norm, latent_down)
    latent_normed, unit_latent, factor_latent = normalize(latent_raw[:, :KVR], latent_gain)
    latent = latent_normed.astype(jnp.bfloat16)
    key_rope = rotate(latent_raw[:, KVR:], cosine, sine_table).astype(jnp.bfloat16)
    key_value = (
        plain_dot(latent, latent_up).astype(jnp.bfloat16).reshape(length, local_heads, NOPE + VD)
    )
    key_rows = jnp.concatenate(
        [
            key_value[..., :NOPE],
            jnp.broadcast_to(key_rope[:, None, :], (length, local_heads, ROPE)),
        ],
        axis=-1,
    )
    values = key_value[..., NOPE:]
    visible = visible_mask(positions, length)
    scores = jnp.where(
        visible[None],
        jnp.einsum("qhd,khd->hqk", queries, key_rows, preferred_element_type=jnp.float32)
        * score_scale,
        -jnp.inf,
    )
    weights = jax.nn.softmax(scores, axis=-1)
    weights_low = weights.astype(jnp.bfloat16)
    head_out = (
        jnp.einsum("hqk,khd->qhd", weights_low, values, preferred_element_type=jnp.float32)
        .astype(jnp.bfloat16)
        .reshape(length, local_heads * VD)
    )
    gate_stored = expert_gate.swapaxes(1, 2).reshape(shared_width, model_width)
    up_stored = expert_up.swapaxes(1, 2).reshape(shared_width, model_width)
    down_stored = expert_down.reshape(shared_width, model_width)
    router_padded = jnp.pad(router_weight, ((0, 0), (0, LANES - experts_all)))
    second_all, acts, logits_all, residual = run_forward(
        plain_dot(head_out, out_weight).astype(jnp.bfloat16),
        inputs,
        feedforward_gain,
        (gate_stored, up_stored, shared_gate.T, shared_up.T),
        router_padded,
    )
    (
        expert_hidden,
        expert_dpre,
        expert_dlin,
        shared_hidden,
        shared_dpre,
        shared_dlin,
        attention_grad,
        result_part,
        grad_residual,
        logit_low,
        grad_feedforward_gain,
    ) = run_backward(
        cotangent_all,
        acts,
        logits_all,
        (gate_stored, up_stored, down_stored, shared_gate.T, shared_up.T, shared_down),
        router_padded,
        residual,
        feedforward_gain,
        local_experts,
    )
    result = lax.all_gather(result_part, "tensor", axis=0, tiled=True)
    tokens = group_count * length
    second_all = second_all.reshape(tokens, model_width)

    attention_grad = attention_grad.reshape(length, model_width)
    second_part = lax.dynamic_slice_in_dim(
        second_all, group_index * length + part_start, part_rows, 0
    )
    grad_out_weight = lead_dot(head_out, attention_grad)
    head_grad = (
        tail_dot(attention_grad, out_weight).astype(jnp.bfloat16).reshape(length, local_heads, VD)
    )
    weight_grad = jnp.einsum("qhd,khd->hqk", head_grad, values, preferred_element_type=jnp.float32)
    score_grad = (
        weights * (weight_grad - jnp.sum(weights * weight_grad, axis=-1, keepdims=True))
    ).astype(jnp.bfloat16)
    query_grad = (
        jnp.einsum("hqk,khd->qhd", score_grad, key_rows, preferred_element_type=jnp.float32)
        * score_scale
    )
    key_grad = (
        jnp.einsum("hqk,qhd->khd", score_grad, queries, preferred_element_type=jnp.float32)
        * score_scale
    )
    value_grad = jnp.einsum(
        "hqk,qhd->khd", weights_low, head_grad, preferred_element_type=jnp.float32
    )
    query_low = (
        jnp.concatenate(
            [
                query_grad[..., :NOPE],
                rotate_back(query_grad[..., NOPE:], cosine[:, None], sine_table[:, None]),
            ],
            axis=-1,
        )
        .astype(jnp.bfloat16)
        .reshape(length, local_heads * head_width)
    )
    grad_query = lead_dot(first_norm, query_low)
    keyvalue_low = (
        jnp.concatenate([key_grad[..., :NOPE], value_grad], axis=-1)
        .astype(jnp.bfloat16)
        .reshape(length, local_heads * (NOPE + VD))
    )
    grad_latent_up = lead_dot(latent, keyvalue_low)
    latent_grad = tail_dot(keyvalue_low, latent_up)
    latent_back, grad_latent_gain = norm_back(latent_grad, unit_latent, factor_latent, latent_gain)
    rope_back = rotate_back(jnp.sum(key_grad[..., NOPE:], axis=1), cosine, sine_table)
    down_low = jnp.concatenate([latent_back, rope_back], axis=1).astype(jnp.bfloat16)
    first_terms = (tail_dot(query_low, query_weight) + tail_dot(down_low, latent_down)).astype(
        jnp.bfloat16
    )
    latent_width = latent_down.shape[1]
    latent_gain_rows = jnp.pad(
        grad_latent_gain.reshape(group_count, -1),
        ((0, 0), (0, shard_columns - KVR // group_count)),
    ).reshape(1, model_width)
    gain_start = latent_width + -(-experts_all // 16) * 16
    rest_count = gain_start + 16
    rest_rows = -(-rest_count // (16 * tensor_count)) * 16 * tensor_count

    def at_row(start, rows):
        return jnp.pad(rows, ((start, rest_rows - start - rows.shape[0]), (0, 0)))

    rest = (
        lead_dot(jnp.pad(down_low, ((0, 0), (0, rest_rows - latent_width))), first_norm)
        + at_row(latent_width, lead_dot(logit_low[:, :experts_all], second_part))
        + at_row(gain_start, grad_feedforward_gain)
        + at_row(gain_start + 1, latent_gain_rows)
    ).astype(jnp.bfloat16)
    (
        grad_query,
        grad_latent_up,
        grad_out_weight,
        rest,
        grad_input,
        grad_expert_gate,
        grad_expert_up,
        grad_expert_down,
        grad_shared_gate,
        grad_shared_up,
        grad_shared_down,
    ) = run_weights(
        grad_query.astype(jnp.bfloat16),
        grad_latent_up.astype(jnp.bfloat16),
        grad_out_weight.astype(jnp.bfloat16),
        rest,
        first_terms,
        grad_residual,
        own_part(inputs),
        attention_gain,
        [
            units.reshape(tokens, shared_width)
            for units in (
                expert_dpre,
                expert_dlin,
                expert_hidden,
                shared_dpre,
                shared_dlin,
                shared_hidden,
            )
        ],
        second_all,
        cotangent_all,
    )
    grad_input = grad_input.reshape(length, model_width).astype(jnp.float32)
    rest = rest.astype(jnp.float32)
    grad_attention_gain = jnp.sum(rest[:, -16], axis=0)
    rest = rest[:, :-16].reshape(-1, shard_columns)
    gain_rows = rest[gain_start:rest_count]

    def stored_experts(rows):
        return rows.reshape(local_experts, expert_hidden_width, model_width)

    return (
        result,
        grad_input,
        grad_attention_gain,
        gain_rows[0],
        gain_rows[1, : KVR // group_count],
        grad_query,
        rest[:latent_width].T,
        grad_latent_up,
        grad_out_weight,
        rest[latent_width : latent_width + experts_all].T,
        grad_shared_gate.T,
        grad_shared_up.T,
        grad_shared_down,
        stored_experts(grad_expert_gate).swapaxes(1, 2),
        stored_experts(grad_expert_up).swapaxes(1, 2),
        stored_experts(grad_expert_down),
    )


def solution(mesh):
    placed = (
        P("expert", None),
        P("expert", None),
        P("expert"),
        P("expert", None),
        P("expert", None),
        P(),
        P(),
        P(),
        P(None, "tensor"),
        P(),
        P(None, "tensor"),
        P("tensor", None),
        P(),
        P(None, "tensor"),
        P(None, "tensor"),
        P("tensor", None),
        P("expert", None, "tensor"),
        P("expert", None, "tensor"),
        P("expert", "tensor", None),
    )
    return jax.shard_map(
        on_device,
        mesh=mesh,
        in_specs=placed,
        out_specs=(
            P("expert", None),
            P("expert", None),
            P("expert"),
            P("expert"),
            P("expert"),
            P("expert", "tensor"),
            P("expert", None),
            P("expert", "tensor"),
            P("tensor", "expert"),
            P("expert", None),
            P("expert", "tensor"),
            P("expert", "tensor"),
            P("tensor", "expert"),
            P("expert", None, "tensor"),
            P("expert", None, "tensor"),
            P("expert", "tensor", None),
        ),
        check_vma=False,
    )
```
